256 devices in a mesh: tm: 64 (over z, y, x_hi), chan: 4 (over x_lo, core).
Axes of the slice: x: 4 (x_hi: 2, x_lo: 2; x = x_hi * 2 + x_lo), y: 4, z: 8, core: 2. Of those that a mesh axis runs over, the one named last changes fastest.
Arguments:
- signal: bfloat16 [384, 8192], P('chan', 'tm'), may hold values from -6 to 6
- codes_init: float32 [128, 8192], P(None, 'tm'), may hold values from -2 to 2
- dictionary_init: float32 [128, 36864], P(None, 'chan'), may hold values from -6 to 6
- threshold: float32 [128], replicated, may hold values from 0.05 to 0.5
- plan: int32 [8], replicated, may hold values from 0 to 7, each once
Outputs:
- sparse_codes: float32 [128, 8192], P(None, 'tm')
- dictionary: float32 [128, 36864], P(None, 'chan')
- residual: float32 [384, 8192], P('chan', 'tm')
The draws below stay inside these ranges and needn't reach their ends.
Inputs may be any that keep to these rules, and one draw needn't show every extreme that they name: `plan`: every atom block from 0 to 7 appears exactly once.
All inputs are finite; a program needn't handle non-finite values.
Results may differ from the reference program's by a relative error of at most 0.013.
Values may be sent and summed in bfloat16 or wider, within the bound.
A program may use at most 64 MiB of HBM per device.

```python
import math
import jax
import jax.numpy as jnp
from jax import lax

C = 384
K = 128
L = 96
BLOCKS = 8
BLOCK_ATOMS = 16
INNER = 2
OUTER = 2
TIME = 8192


def steps_of(key, extent, cuts, low, high):
    def one(dim, blocks):
        draws = jax.random.uniform(jax.random.fold_in(jax.random.fold_in(key, 6), dim), (blocks,), jnp.float32, low / len(cuts), high / len(cuts))
        return jnp.repeat(jnp.exp(draws), extent[dim] // blocks).reshape((-1,) + (1,) * (len(extent) - dim - 1))

    gain = one(*cuts[0])
    for cut in cuts[1:]:
        gain = gain * one(*cut)
    return gain


def centred(stream_key, extent, deviation, bound, pieces=(), kind=jnp.bfloat16):
    drawn = deviation * jax.random.normal(stream_key, extent, jnp.float32)
    if pieces:
        drawn = drawn * steps_of(stream_key, extent, pieces, -0.22, 0.18)
    return jnp.clip(drawn, -bound, bound).astype(kind)


def setup_inputs(seed: int = 0) -> dict:
    arg_keys = jax.random.split(jax.random.key(seed), 6)
    signal = centred(arg_keys[0], (C, TIME), 1.0, 6.0, ((0, 4), (1, 64)))
    codes_init = centred(arg_keys[1], (K, TIME), 0.3, 2.0, ((1, 64),), jnp.float32)
    dictionary_init = centred(arg_keys[2], (K, C * L), 1.0, 6.0, ((1, 4),), jnp.float32)
    threshold = jnp.clip(jnp.exp(jax.random.uniform(arg_keys[3], (K,), jnp.float32, math.log(0.05), math.log(0.5))), 0.05, 0.5)
    plan = jax.random.permutation(arg_keys[4], BLOCKS).astype(jnp.int32)
    return {"signal": signal, "codes_init": codes_init, "dictionary_init": dictionary_init, "threshold": threshold, "plan": plan}


code_rate = 0.3
move_rate = 0.5
tiny_eps = 1e-06

def convolve(dict_low, code_low):
    samples = code_low.shape[1]
    atom_cube = dict_low.astype(jnp.float32).reshape(K, C, L)
    padded = jnp.concatenate([jnp.zeros((K, L - 1), jnp.float32), code_low.astype(jnp.float32)], axis=1)

    def accumulate(offset, running):
        column = lax.dynamic_index_in_dim(atom_cube, offset, 2, keepdims=False)
        shifted = lax.dynamic_slice_in_dim(padded, L - 1 - offset, samples, 1)
        return running + jnp.dot(column.T, shifted, precision=lax.Precision.HIGHEST)
    total_sum = lax.fori_loop(0, L, accumulate, jnp.zeros((C, samples), jnp.float32))
    return total_sum * (C * L) ** (-0.5)

def pad_right(resid_low):
    return jnp.concatenate([resid_low.astype(jnp.float32), jnp.zeros((C, L - 1), jnp.float32)], axis=1)

def correlate(dict_low, resid_low):
    samples = resid_low.shape[1]
    atom_cube = dict_low.astype(jnp.float32).reshape(K, C, L)
    padded = pad_right(resid_low)

    def accumulate(offset, running):
        column = lax.dynamic_index_in_dim(atom_cube, offset, 2, keepdims=False)
        shifted = lax.dynamic_slice_in_dim(padded, offset, samples, 1)
        return running + jnp.dot(column, shifted, precision=lax.Precision.HIGHEST)
    total_sum = lax.fori_loop(0, L, accumulate, jnp.zeros((K, samples), jnp.float32))
    return total_sum * (C * L) ** (-0.5)

def block_gradient(code_block, resid_low):
    samples = resid_low.shape[1]
    padded = pad_right(resid_low)
    block_f = code_block.astype(jnp.float32)

    def per_offset(offset):
        shifted = lax.dynamic_slice_in_dim(padded, offset, samples, 1)
        return jnp.dot(block_f, shifted.T, precision=lax.Precision.HIGHEST)
    stacked = lax.map(per_offset, jnp.arange(L))
    return jnp.transpose(stacked, (1, 2, 0)).reshape(BLOCK_ATOMS, C * L)

def reference(signal, codes_init, dictionary_init, threshold, plan):
    code_state = codes_init
    dictionary = dictionary_init
    limit = threshold[:, None]
    entries = C * L
    residual = signal.astype(jnp.float32)
    for outer_step in range(OUTER):
        dict_low = dictionary.astype(jnp.bfloat16)
        for inner_step in range(INNER):
            code_low = code_state.astype(jnp.bfloat16)
            residual = signal.astype(jnp.float32) - convolve(dict_low, code_low)
            scores = correlate(dict_low, residual.astype(jnp.bfloat16))
            stepped = code_state + code_rate * scores
            code_state = stepped - jnp.clip(stepped, -limit, limit)
        code_low = code_state.astype(jnp.bfloat16)
        residual = signal.astype(jnp.float32) - convolve(dict_low, code_low)
        resid_low = residual.astype(jnp.bfloat16)
        first_row = (plan[outer_step] * BLOCK_ATOMS).astype(jnp.int32)
        code_block = lax.dynamic_slice_in_dim(code_low, first_row, BLOCK_ATOMS, 0)
        gradient = block_gradient(code_block, resid_low)
        old_atoms = lax.dynamic_slice_in_dim(dictionary, first_row, BLOCK_ATOMS, 0)
        mean_sq = lax.optimization_barrier(jnp.sum(old_atoms * old_atoms, axis=1)) / entries + tiny_eps
        along_coef = lax.optimization_barrier(jnp.sum(gradient * old_atoms, axis=1)) / entries / mean_sq
        across = gradient - along_coef[:, None] * old_atoms
        spread = lax.optimization_barrier(jnp.sum(across * across, axis=1)) / entries + tiny_eps
        renewed = (old_atoms + move_rate * across / jnp.sqrt(spread)[:, None]) / jnp.sqrt(mean_sq + 0.25)[:, None]
        dictionary = lax.dynamic_update_slice_in_dim(dictionary, renewed, first_row, 0)
    return (code_state, dictionary, residual)
```

```python
import functools

import jax
import jax.numpy as jnp
from jax import lax
from jax.experimental import pallas as pl
from jax.experimental.pallas import tpu as pltpu
from jax.sharding import PartitionSpec as P

C = 384
K = 128
L = 96
BLOCK_ATOMS = 16
INNER = 2
OUTER = 2
CHANS = 96
SEG = 128
ENTRIES = C * L

code_rate = 0.3
move_rate = 0.5
tiny_eps = 1e-06

MESH = pl.DeviceIdType.MESH
F32 = jnp.float32
BF16 = jnp.bfloat16

OWN = 288
ROWS = 608
PLANE = 8
HALO = (
    (1, 0, 128, 160),
    (2, 0, 128, 32),
    (3, 96, 32, 0),
    (-1, 0, 128, 416),
    (-2, 0, 64, 544),
)
SIGNAL_HALO = (
    (1, 0, 128, 160),
    (2, 64, 64, 96),
    (-1, 0, 128, 416),
    (-2, 0, 64, 544),
)


def dot(a, b):
    return lax.dot_general(a, b, (((1,), (0,)), ((), ())), preferred_element_type=F32)


def dot_t(a, b):
    return lax.dot_general(a, b, (((1,), (1,)), ((), ())), preferred_element_type=F32)


def kernel(
    segments,
    plan_ref,
    dt_ref,
    codes_ref,
    signal_ref,
    thr_ref,
    pick_ref,
    old_ref,
    codes_out,
    resid_out,
    renewed_out,
    zst,
    zsend,
    sgx,
    sgown,
    rst,
    zp,
    rp,
    wb,
    wat,
    acc,
    sx,
    sx2,
    rx1,
    rx2,
    a16,
    gfull,
    gsend,
    grecv,
    zbuf,
    agbuf,
    new_low,
    stats,
    strecv,
    h_send,
    h_recv,
    s_send,
    s_recv,
    c_send,
    c_recv,
    p_send,
    p_recv,
    z_send,
    z_recv,
    a_send,
    a_recv,
    t_send,
    t_recv,
):
    unit = ENTRIES ** (-0.5)
    tm = lax.axis_index("tm")
    chan = lax.axis_index("chan")
    depth = segments // PLANE
    place = tm % PLANE
    level = tm // PLANE

    def seg(d):
        return (tm + d + segments) % segments

    def in_plane(d):
        return level * PLANE + (place + d) % PLANE

    def in_depth(d):
        return ((level + d) % depth) * PLANE + place

    partner = chan + 1 - 2 * (chan % 2)
    opposite = (chan + 2) % 4

    zsend[0] = codes_ref[...].T
    zst[0, OWN : OWN + SEG] = zsend[0]
    low = jnp.concatenate(
        [signal_ref[...].astype(F32), jnp.zeros((SEG - CHANS, SEG), F32)], axis=0
    ).T.astype(BF16)
    sgown[...] = low
    sgx[OWN : OWN + SEG] = low

    barrier = pltpu.get_barrier_semaphore()
    peers = [{"tm": seg(d)} for d in (-3, -2, -1, 1, 2, 3)]
    peers += [{"chan": (chan + d) % 4} for d in range(1, 4)]
    peers += [{"tm": in_plane(d)} for d in range(1, PLANE)]
    peers += [{"tm": in_depth(d)} for d in range(1, depth)]
    for peer in peers:
        pl.semaphore_signal(barrier, inc=1, device_id=peer, device_id_type=MESH)
    pl.semaphore_wait(barrier, len(peers))

    def remote(src, dst, send, recv, peer):
        return pltpu.make_async_remote_copy(
            src_ref=src,
            dst_ref=dst,
            send_sem=send,
            recv_sem=recv,
            device_id=peer,
            device_id_type=MESH,
        )

    def halo_copies(o):
        return [
            remote(
                zsend.at[o, pl.ds(first, rows)],
                zst.at[o, pl.ds(land, rows)],
                h_send.at[o, i],
                h_recv.at[o, i],
                {"tm": seg(d)},
            )
            for i, (d, first, rows, land) in enumerate(HALO)
        ]

    signal_copies = [
        remote(
            sgown.at[pl.ds(first, rows)],
            sgx.at[pl.ds(land, rows)],
            s_send.at[i],
            s_recv.at[i],
            {"tm": seg(d)},
        )
        for i, (d, first, rows, land) in enumerate(SIGNAL_HALO)
    ]
    halo = halo_copies(0)
    for copy in halo + signal_copies:
        copy.start()

    for q in range(3):
        for s in range(16):
            wb[q, s * 128 + CHANS : (s + 1) * 128] = jnp.zeros((128 - CHANS, 256), BF16)
        for j in range(2):
            wat[q, j * 128 + CHANS : (j + 1) * 128] = jnp.zeros((128 - CHANS, 2048), BF16)
    for lag in range(L):
        j, q, s = lag // 48, lag % 48 // 16, lag % 16
        block = dt_ref[pl.ds(lag, CHANS, stride=L), :].astype(BF16)
        wb[q, s * 128 : s * 128 + CHANS, j * 128 : (j + 1) * 128] = block
        wat[q, j * 128 : j * 128 + CHANS, s * 128 : (s + 1) * 128] = block

    for copy in halo + signal_copies:
        copy.wait()

    def in_window(a, b):
        when = tm * SEG - OWN + a + lax.broadcasted_iota(jnp.int32, (b - a, 1), 0)
        return when

    def clear_early(o):
        zst[o, 0:OWN] = jnp.where(in_window(0, OWN) >= 0, zst[o, 0:OWN], 0.0)

    def residual_rows(o, a, b):
        top = a - 80
        for s in range(16):
            zp[top:b, s * 128 : (s + 1) * 128] = zst[o, pl.ds(top - s, b - top), :].astype(BF16)
        n = b - a + 48
        acc[0:n] = dot_t(zp[a - 48 : b, :], wat[0])
        acc[0:n] += dot_t(zp[a - 64 : b - 16, :], wat[1])
        acc[0:n] += dot_t(zp[a - 80 : b - 32, :], wat[2])
        made = unit * (acc[48:n, 0:128] + acc[0 : n - 48, 128:256])
        value = sgx[a:b].astype(F32) - made
        rst[a:b] = jnp.where(in_window(a, b) < segments * SEG, value, 0.0)

    def score_rows(a, b):
        end = b + 80
        for s in range(16):
            rp[a:end, s * 128 : (s + 1) * 128] = rst[pl.ds(a + s, end - a), :].astype(BF16)
        n = b - a + 48
        acc[0:n] = dot(rp[a : b + 48, :], wb[0])
        acc[0:n] += dot(rp[a + 16 : b + 64, :], wb[1])
        acc[0:n] += dot(rp[a + 32 : b + 80, :], wb[2])
        return unit * (acc[0 : n - 48, 0:128] + acc[48:n, 128:256])

    def update_rows(o, step, a, b):
        n = b - a
        i = o * INNER + step
        sx[0:n] = score_rows(a, b).astype(BF16)
        near = remote(
            sx.at[pl.ds(0, n)],
            rx1.at[i, pl.ds(0, n)],
            c_send.at[i, 0],
            c_recv.at[i, 0],
            {"chan": partner},
        )
        near.start()
        near.wait()
        sx2[0:n] = (sx[0:n].astype(F32) + rx1[i, 0:n].astype(F32)).astype(BF16)
        far = remote(
            sx2.at[pl.ds(0, n)],
            rx2.at[i, pl.ds(0, n)],
            c_send.at[i, 1],
            c_recv.at[i, 1],
            {"chan": opposite},
        )
        far.start()
        far.wait()
        scores = sx2[0:n].astype(F32) + rx2[i, 0:n].astype(F32)
        stepped = zst[o, a:b] + code_rate * scores
        limit = thr_ref[...]
        value = stepped - jnp.clip(stepped, -limit, limit)
        zst[o, a:b] = jnp.where(in_window(a, b) >= 0, value, 0.0)

    def lanes_sum(row):
        total = row[:, 0:128] + row[:, 128:256] + row[:, 256:384]
        total = jnp.broadcast_to(total, (8, 128))
        for shift in (64, 32, 16):
            total = total + pltpu.roll(total, shift, 1)
        return total

    def three(row):
        return jnp.concatenate([row[0:1]] * 3, axis=1)

    def renew(o):
        turned = rst[OWN : OWN + SEG].T
        if o == OUTER - 1:
            resid_out[...] = turned[0:CHANS]
        pick = pick_ref[o]
        for half in range(2):
            lanes = slice(half * 128, half * 128 + 128)
            a16[:, lanes] = dot(
                zp[OWN - 80 : OWN + SEG, half * 1024 : half * 1024 + 1024], pick
            ).astype(BF16)
        across_time = turned[0:CHANS].astype(BF16)
        for q in range(6):
            gfull[:, q * 256 : (q + 1) * 256] = dot(
                across_time, a16[80 - 16 * q : 208 - 16 * q, :]
            ).astype(BF16)
        for piece in range(PLANE):
            top, left = piece // 4 * 48, piece % 4 * 384
            gsend[piece] = gfull[top : top + 48, left : left + 384]
        copies = [
            remote(
                gsend.at[(place + d) % PLANE],
                grecv.at[o, d],
                p_send.at[o, d],
                p_recv.at[o, d],
                {"tm": in_plane(d)},
            )
            for d in range(1, PLANE)
        ]
        for copy in copies:
            copy.start()
        total = gsend[place].astype(F32)
        for d, copy in enumerate(copies, 1):
            copy.wait_recv()
            total = total + grecv[o, d].astype(F32)
        zbuf[o, level] = total.astype(BF16)
        sent = copies
        copies = [
            remote(
                zbuf.at[o, level],
                zbuf.at[o, level],
                z_send.at[o, d],
                z_recv.at[o, d],
                {"tm": in_depth(d)},
            )
            for d in range(1, depth)
        ]
        for copy in copies:
            copy.start()
        for copy in copies:
            copy.wait_recv()
        sent = sent + copies
        total = zbuf[o, 0].astype(F32)
        for i in range(1, depth):
            total = total + zbuf[o, i].astype(F32)
        agbuf[o, place] = total.astype(BF16)
        copies = [
            remote(
                agbuf.at[o, place],
                agbuf.at[o, place],
                a_send.at[o, d],
                a_recv.at[o, d],
                {"tm": in_plane(d)},
            )
            for d in range(1, PLANE)
        ]
        for copy in copies:
            copy.start()
        for copy in copies:
            copy.wait_recv()
        sent = sent + copies

        with_old = jnp.zeros((1, 384), F32)
        old_old = jnp.zeros((1, 384), F32)
        for piece in range(PLANE):
            grad, old = agbuf[o, piece].astype(F32), old_ref[o, piece]
            with_old = with_old + jnp.sum(grad * old, axis=0, keepdims=True)
            old_old = old_old + jnp.sum(old * old, axis=0, keepdims=True)
        with_old, old_old = lanes_sum(with_old), lanes_sum(old_old)
        own_coef = jnp.where(old_old > 0.0, with_old / jnp.maximum(old_old, 1e-30), 0.0)
        left_over = jnp.zeros((1, 384), F32)
        coef = three(own_coef)
        for piece in range(PLANE):
            part = agbuf[o, piece].astype(F32) - coef * old_ref[o, piece]
            left_over = left_over + jnp.sum(part * part, axis=0, keepdims=True)
        left_over = lanes_sum(left_over)
        row = lax.broadcasted_iota(jnp.int32, (8, 128), 0)
        packed = jnp.where(row == 0, with_old, jnp.where(row == 1, old_old, left_over))
        strecv[o, chan] = packed
        copies = [
            remote(
                strecv.at[o, chan],
                strecv.at[o, chan],
                t_send.at[o, d],
                t_recv.at[o, d],
                {"chan": (chan + d) % 4},
            )
            for d in range(1, 4)
        ]
        for copy in copies:
            copy.start()
        for copy in copies:
            copy.wait_recv()
        sent = sent + copies
        parts = [strecv[o, i] for i in range(4)]
        gd = [part[0:1] for part in parts]
        dd = [part[1:2] for part in parts]
        rr = [part[2:3] for part in parts]
        mean_sq = (dd[0] + dd[1] + dd[2] + dd[3]) / ENTRIES + tiny_eps
        along = (gd[0] + gd[1] + gd[2] + gd[3]) / ENTRIES / mean_sq
        spread = jnp.zeros((1, 128), F32)
        for i in range(4):
            mine = jnp.where(dd[i] > 0.0, gd[i] / jnp.maximum(dd[i], 1e-30), 0.0)
            off = mine - along
            spread = spread + rr[i] + off * (off * dd[i] + 2.0 * (gd[i] - mine * dd[i]))
        spread = jnp.maximum(spread, 0.0) / ENTRIES + tiny_eps
        along_row = three(along)
        gain = three(move_rate / jnp.sqrt(spread))
        shrink = three(1.0 / jnp.sqrt(mean_sq + 0.25))
        for piece in range(PLANE):
            old = old_ref[o, piece]
            across = agbuf[o, piece].astype(F32) - along_row * old
            value = (old + gain * across) * shrink
            renewed_out[o, piece] = value
            if o < OUTER - 1:
                top, left = piece // 4 * 48, piece % 4 * 384
                new_low[top : top + 48, left : left + 384] = value.astype(BF16)
        for copy in sent:
            copy.wait_send()

    def place_block(o):
        lane = lax.broadcasted_iota(jnp.int32, (1, 128), 1)
        keep = jnp.where(lane // BLOCK_ATOMS == plan_ref[o], 0.0, 1.0).astype(BF16)
        pick = pick_ref[o]
        for group in range(12):
            spread_out = dot_t(new_low[:, group * 128 : (group + 1) * 128], pick).astype(BF16)
            for i in range(8):
                lag = group * 8 + i
                j, q, s = lag // 48, lag % 48 // 16, lag % 16
                rows = slice(s * 128, s * 128 + CHANS)
                lanes = slice(j * 128, (j + 1) * 128)
                block = wb[q, rows, lanes] * keep + spread_out[:, i * 128 : (i + 1) * 128]
                wb[q, rows, lanes] = block
                wat[q, j * 128 : j * 128 + CHANS, s * 128 : (s + 1) * 128] = block

    for o in range(OUTER):
        clear_early(o)
        residual_rows(o, 96, 608)
        update_rows(o, 0, 96, 512)
        residual_rows(o, 192, 512)
        update_rows(o, 1, 192, 416)
        if o < OUTER - 1:
            zsend[o + 1] = zst[o, OWN : OWN + SEG]
            zst[o + 1, OWN : OWN + SEG] = zsend[o + 1]
            halo = halo_copies(o + 1)
            for copy in halo:
                copy.start()
        else:
            codes_out[...] = zst[o, OWN : OWN + SEG].T
        residual_rows(o, 288, 416)
        renew(o)
        if o < OUTER - 1:
            place_block(o)
            for copy in halo:
                copy.wait()


def shards(segments, signal, codes_init, dictionary_init, threshold, plan):
    turned = dictionary_init.T
    first = plan[:OUTER] * BLOCK_ATOMS
    row = jnp.arange(1024)[None, :, None]
    lane = jnp.arange(128)[None, None, :]
    pick = (row // 128 == lane // 16) & (row % 128 == lane % 16 + first[:, None, None])
    pick = pick.astype(BF16)
    old = jnp.stack(
        [lax.dynamic_slice_in_dim(dictionary_init, first[o], BLOCK_ATOMS, 0) for o in range(OUTER)]
    )
    old = old.reshape(OUTER, BLOCK_ATOMS, 2, 48, 4, 24).transpose(0, 2, 4, 3, 5, 1)
    old = old.reshape(OUTER, PLANE, 48, 384)
    depth = segments // PLANE
    vmem = pl.BlockSpec(memory_space=pltpu.VMEM)
    dma = pltpu.SemaphoreType.DMA
    codes, resid, renewed = pl.pallas_call(
        functools.partial(kernel, segments),
        out_shape=(
            jax.ShapeDtypeStruct((K, SEG), F32),
            jax.ShapeDtypeStruct((CHANS, SEG), F32),
            jax.ShapeDtypeStruct((OUTER, PLANE, 48, 384), F32),
        ),
        in_specs=[pl.BlockSpec(memory_space=pltpu.SMEM)] + [vmem] * 6,
        out_specs=(vmem, vmem, vmem),
        scratch_shapes=[
            pltpu.VMEM((OUTER, ROWS, 128), F32),
            pltpu.VMEM((OUTER, SEG, 128), F32),
            pltpu.VMEM((ROWS, 128), BF16),
            pltpu.VMEM((SEG, 128), BF16),
            pltpu.VMEM((ROWS, 128), F32),
            pltpu.VMEM((ROWS, 2048), BF16),
            pltpu.VMEM((ROWS, 2048), BF16),
            pltpu.VMEM((3, 2048, 256), BF16),
            pltpu.VMEM((3, 256, 2048), BF16),
            pltpu.VMEM((560, 256), F32),
            pltpu.VMEM((416, 128), BF16),
            pltpu.VMEM((416, 128), BF16),
            pltpu.VMEM((4, 416, 128), BF16),
            pltpu.VMEM((4, 416, 128), BF16),
            pltpu.VMEM((208, 256), BF16),
            pltpu.VMEM((CHANS, 1536), BF16),
            pltpu.VMEM((PLANE, 48, 384), BF16),
            pltpu.VMEM((OUTER, PLANE, 48, 384), BF16),
            pltpu.VMEM((OUTER, depth, 48, 384), BF16),
            pltpu.VMEM((OUTER, PLANE, 48, 384), BF16),
            pltpu.VMEM((CHANS, 1536), BF16),
            pltpu.VMEM((8, 128), F32),
            pltpu.VMEM((OUTER, 4, 8, 128), F32),
            dma((OUTER, 5)),
            dma((OUTER, 5)),
            dma((4,)),
            dma((4,)),
            dma((4, 2)),
            dma((4, 2)),
            dma((OUTER, PLANE)),
            dma((OUTER, PLANE)),
            dma((OUTER, depth)),
            dma((OUTER, depth)),
            dma((OUTER, PLANE)),
            dma((OUTER, PLANE)),
            dma((OUTER, 4)),
            dma((OUTER, 4)),
        ],
        compiler_params=pltpu.CompilerParams(
            collective_id=0, has_side_effects=True, vmem_limit_bytes=60 * 1024 * 1024
        ),
    )(plan, turned, codes_init, signal, threshold[None, :], pick, old)
    renewed = renewed.reshape(OUTER, 2, 4, 48, 24, BLOCK_ATOMS).transpose(0, 5, 1, 3, 2, 4)
    renewed = renewed.reshape(OUTER, BLOCK_ATOMS, CHANS * L)
    dictionary = dictionary_init
    for o in range(OUTER):
        dictionary = lax.dynamic_update_slice_in_dim(dictionary, renewed[o], first[o], 0)
    return codes, dictionary, resid


def solution(mesh):
    placed = (P("chan", "tm"), P(None, "tm"), P(None, "chan"), P(), P())
    return jax.shard_map(
        functools.partial(shards, mesh.shape["tm"]),
        mesh=mesh,
        in_specs=placed,
        out_specs=(P(None, "tm"), P(None, "chan"), P("chan", "tm")),
        check_vma=False,
    )
```

```python
import functools

import jax
import jax.numpy as jnp
from jax import lax
from jax.experimental import pallas as pl
from jax.experimental.pallas import tpu as pltpu
from jax.sharding import PartitionSpec as P

C = 384
K = 128
L = 96
BLOCK_ATOMS = 16
INNER = 2
OUTER = 2
CHANS = 96
SEG = 128
ENTRIES = C * L

code_rate = 0.3
move_rate = 0.5
tiny_eps = 1e-06

MESH = pl.DeviceIdType.MESH
F32 = jnp.float32
BF16 = jnp.bfloat16

OWN = 288
ROWS = 608
PLANE = 8
HALO = (
    (1, 0, 128, 160),
    (2, 0, 128, 32),
    (3, 96, 32, 0),
    (-1, 0, 128, 416),
    (-2, 0, 64, 544),
)
SIGNAL_HALO = (
    (1, 0, 128, 160),
    (2, 64, 64, 96),
    (-1, 0, 128, 416),
    (-2, 0, 64, 544),
)


def dot(a, b):
    return lax.dot_general(a, b, (((1,), (0,)), ((), ())), preferred_element_type=F32)


def dot_t(a, b):
    return lax.dot_general(a, b, (((1,), (1,)), ((), ())), preferred_element_type=F32)


def split(value):
    high = value.astype(BF16)
    left = value - high.astype(F32)
    middle = left.astype(BF16)
    return high, middle, (left - middle.astype(F32)).astype(BF16)


def kernel(
    segments,
    plan_ref,
    dt_ref,
    codes_ref,
    signal_ref,
    thr_ref,
    codes_out,
    resid_out,
    dt_out,
    zst,
    zsend,
    sgx,
    sgown,
    rst,
    zp,
    rp,
    wb,
    wat,
    acc,
    sx,
    sx2,
    rx1,
    rx2,
    a16,
    gfull,
    gsend,
    grecv,
    zbuf,
    agbuf,
    old,
    new,
    rest,
    pick,
    spot,
    strecv,
    h_send,
    h_recv,
    s_send,
    s_recv,
    c_send,
    c_recv,
    p_send,
    p_recv,
    z_send,
    z_recv,
    a_send,
    a_recv,
    t_send,
    t_recv,
):
    unit = ENTRIES ** (-0.5)
    tm = lax.axis_index("tm")
    chan = lax.axis_index("chan")
    depth = segments // PLANE
    place = tm % PLANE
    level = tm // PLANE

    def seg(d):
        return (tm + d + segments) % segments

    def in_plane(d):
        return level * PLANE + (place + d) % PLANE

    def in_depth(d):
        return ((level + d) % depth) * PLANE + place

    partner = chan + 1 - 2 * (chan % 2)
    opposite = (chan + 2) % 4

    zsend[0] = codes_ref[...].T
    zst[0, OWN : OWN + SEG] = zsend[0]
    low = jnp.concatenate(
        [signal_ref[...].astype(F32), jnp.zeros((SEG - CHANS, SEG), F32)], axis=0
    ).T.astype(BF16)
    sgown[...] = low
    sgx[OWN : OWN + SEG] = low

    tall = lax.broadcasted_iota(jnp.int32, (1024, 128), 0)
    wide = lax.broadcasted_iota(jnp.int32, (1024, 128), 1)
    for o in range(OUTER):
        first = plan_ref[o] * BLOCK_ATOMS
        atom = tall % 128 - first
        hit = (atom >= 0) & (atom < BLOCK_ATOMS) & (tall // 128 * BLOCK_ATOMS + atom == wide)
        pick[:, o * 128 : (o + 1) * 128] = jnp.where(hit, 1.0, 0.0).astype(BF16)
    tall = lax.broadcasted_iota(jnp.int32, (128, 1024), 0)
    wide = lax.broadcasted_iota(jnp.int32, (128, 1024), 1)
    for o in range(OUTER):
        atom = wide % 128 - plan_ref[o] * BLOCK_ATOMS
        hit = (atom >= 0) & (atom < BLOCK_ATOMS) & (wide // 128 * BLOCK_ATOMS + atom == tall)
        spot[o] = jnp.where(hit, 1.0, 0.0).astype(BF16)

    barrier = pltpu.get_barrier_semaphore()
    peers = [{"tm": seg(d)} for d in (-3, -2, -1, 1, 2, 3)]
    peers += [{"chan": (chan + d) % 4} for d in range(1, 4)]
    peers += [{"tm": in_plane(d)} for d in range(1, PLANE)]
    peers += [{"tm": in_depth(d)} for d in range(1, depth)]
    for peer in peers:
        pl.semaphore_signal(barrier, inc=1, device_id=peer, device_id_type=MESH)
    pl.semaphore_wait(barrier, len(peers))

    def remote(src, dst, send, recv, peer):
        return pltpu.make_async_remote_copy(
            src_ref=src,
            dst_ref=dst,
            send_sem=send,
            recv_sem=recv,
            device_id=peer,
            device_id_type=MESH,
        )

    def halo_copies(o):
        return [
            remote(
                zsend.at[o, pl.ds(first, rows)],
                zst.at[o, pl.ds(land, rows)],
                h_send.at[o, i],
                h_recv.at[o, i],
                {"tm": seg(d)},
            )
            for i, (d, first, rows, land) in enumerate(HALO)
        ]

    signal_copies = [
        remote(
            sgown.at[pl.ds(first, rows)],
            sgx.at[pl.ds(land, rows)],
            s_send.at[i],
            s_recv.at[i],
            {"tm": seg(d)},
        )
        for i, (d, first, rows, land) in enumerate(SIGNAL_HALO)
    ]
    halo = halo_copies(0)
    for copy in halo + signal_copies:
        copy.start()

    for q in range(3):
        for s in range(16):
            wb[q, s * 128 + CHANS : (s + 1) * 128] = jnp.zeros((128 - CHANS, 256), BF16)
        for j in range(2):
            wat[q, j * 128 + CHANS : (j + 1) * 128] = jnp.zeros((128 - CHANS, 2048), BF16)
    for j in range(2):
        for q in range(3):
            for s in range(16):
                taps = pl.ds(48 * j + 16 * q + s, CHANS, stride=L)
                rows, lanes = slice(j * 128, j * 128 + CHANS), slice(s * 128, (s + 1) * 128)
                value = dt_ref[taps, :]
                dt_out[taps, :] = value
                parts = split(value)
                wb[q, s * 128 : s * 128 + CHANS, j * 128 : (j + 1) * 128] = parts[0]
                wat[q, rows, lanes] = parts[0]
                rest[0, :, lanes] = parts[1]
                rest[1, :, lanes] = parts[2]
            for half in range(2):
                lanes = slice(half * 1024, (half + 1) * 1024)
                group = 6 * j + 2 * q + half
                both = dot(wat[q, rows, lanes], pick[...])
                both += dot(rest[0, :, lanes], pick[...])
                both += dot(rest[1, :, lanes], pick[...])
                for o in range(OUTER):
                    old[o, :, group * 128 : (group + 1) * 128] = both[:, o * 128 : (o + 1) * 128]

    for copy in halo + signal_copies:
        copy.wait()

    def in_window(a, b):
        when = tm * SEG - OWN + a + lax.broadcasted_iota(jnp.int32, (b - a, 1), 0)
        return when

    def clear_early(o):
        zst[o, 0:OWN] = jnp.where(in_window(0, OWN) >= 0, zst[o, 0:OWN], 0.0)

    def residual_rows(o, a, b):
        top = a - 80
        for s in range(16):
            zp[top:b, s * 128 : (s + 1) * 128] = zst[o, pl.ds(top - s, b - top), :].astype(BF16)
        n = b - a + 48
        acc[0:n] = dot_t(zp[a - 48 : b, :], wat[0])
        acc[0:n] += dot_t(zp[a - 64 : b - 16, :], wat[1])
        acc[0:n] += dot_t(zp[a - 80 : b - 32, :], wat[2])
        made = unit * (acc[48:n, 0:128] + acc[0 : n - 48, 128:256])
        value = sgx[a:b].astype(F32) - made
        rst[a:b] = jnp.where(in_window(a, b) < segments * SEG, value, 0.0)

    def score_rows(a, b):
        end = b + 80
        for s in range(16):
            rp[a:end, s * 128 : (s + 1) * 128] = rst[pl.ds(a + s, end - a), :].astype(BF16)
        n = b - a + 48
        acc[0:n] = dot(rp[a : b + 48, :], wb[0])
        acc[0:n] += dot(rp[a + 16 : b + 64, :], wb[1])
        acc[0:n] += dot(rp[a + 32 : b + 80, :], wb[2])
        return unit * (acc[0 : n - 48, 0:128] + acc[48:n, 128:256])

    def update_rows(o, step, a, b):
        n = b - a
        i = o * INNER + step
        sx[0:n] = score_rows(a, b).astype(BF16)
        near = remote(
            sx.at[pl.ds(0, n)],
            rx1.at[i, pl.ds(0, n)],
            c_send.at[i, 0],
            c_recv.at[i, 0],
            {"chan": partner},
        )
        near.start()
        near.wait()
        sx2[0:n] = (sx[0:n].astype(F32) + rx1[i, 0:n].astype(F32)).astype(BF16)
        far = remote(
            sx2.at[pl.ds(0, n)],
            rx2.at[i, pl.ds(0, n)],
            c_send.at[i, 1],
            c_recv.at[i, 1],
            {"chan": opposite},
        )
        far.start()
        far.wait()
        scores = sx2[0:n].astype(F32) + rx2[i, 0:n].astype(F32)
        stepped = zst[o, a:b] + code_rate * scores
        limit = thr_ref[...]
        value = stepped - jnp.clip(stepped, -limit, limit)
        zst[o, a:b] = jnp.where(in_window(a, b) >= 0, value, 0.0)

    def lanes_sum(row):
        total = row[:, 0:128] + row[:, 128:256] + row[:, 256:384]
        total = jnp.broadcast_to(total, (8, 128))
        for shift in (64, 32, 16):
            total = total + pltpu.roll(total, shift, 1)
        return total

    def old_piece(o, piece):
        top, left = piece // 4 * 48, piece % 4 * 384
        return old[o, top : top + 48, left : left + 384]

    def three(row):
        return jnp.concatenate([row[0:1]] * 3, axis=1)

    def renew(o):
        turned = rst[OWN : OWN + SEG].T
        if o == OUTER - 1:
            resid_out[...] = turned[0:CHANS]
        for half in range(2):
            lanes = slice(half * 128, half * 128 + 128)
            a16[:, lanes] = dot(
                zp[OWN - 80 : OWN + SEG, half * 1024 : half * 1024 + 1024],
                pick[:, o * 128 : (o + 1) * 128],
            ).astype(BF16)
        across_time = turned[0:CHANS].astype(BF16)
        for q in range(6):
            gfull[:, q * 256 : (q + 1) * 256] = dot(
                across_time, a16[80 - 16 * q : 208 - 16 * q, :]
            ).astype(BF16)
        for piece in range(PLANE):
            top, left = piece // 4 * 48, piece % 4 * 384
            gsend[piece] = gfull[top : top + 48, left : left + 384]
        copies = [
            remote(
                gsend.at[(place + d) % PLANE],
                grecv.at[o, d],
                p_send.at[o, d],
                p_recv.at[o, d],
                {"tm": in_plane(d)},
            )
            for d in range(1, PLANE)
        ]
        for copy in copies:
            copy.start()
        total = gsend[place].astype(F32)
        for d, copy in enumerate(copies, 1):
            copy.wait_recv()
            total = total + grecv[o, d].astype(F32)
        zbuf[o, level] = total.astype(BF16)
        sent = copies
        copies = [
            remote(
                zbuf.at[o, level],
                zbuf.at[o, level],
                z_send.at[o, d],
                z_recv.at[o, d],
                {"tm": in_depth(d)},
            )
            for d in range(1, depth)
        ]
        for copy in copies:
            copy.start()
        for copy in copies:
            copy.wait_recv()
        sent = sent + copies
        total = zbuf[o, 0].astype(F32)
        for i in range(1, depth):
            total = total + zbuf[o, i].astype(F32)
        agbuf[o, place] = total.astype(BF16)
        copies = [
            remote(
                agbuf.at[o, place],
                agbuf.at[o, place],
                a_send.at[o, d],
                a_recv.at[o, d],
                {"tm": in_plane(d)},
            )
            for d in range(1, PLANE)
        ]
        for copy in copies:
            copy.start()
        for copy in copies:
            copy.wait_recv()
        sent = sent + copies

        with_old = jnp.zeros((1, 384), F32)
        old_old = jnp.zeros((1, 384), F32)
        for piece in range(PLANE):
            grad, was = agbuf[o, piece].astype(F32), old_piece(o, piece)
            with_old = with_old + jnp.sum(grad * was, axis=0, keepdims=True)
            old_old = old_old + jnp.sum(was * was, axis=0, keepdims=True)
        with_old, old_old = lanes_sum(with_old), lanes_sum(old_old)
        own_coef = jnp.where(old_old > 0.0, with_old / jnp.maximum(old_old, 1e-30), 0.0)
        left_over = jnp.zeros((1, 384), F32)
        coef = three(own_coef)
        for piece in range(PLANE):
            part = agbuf[o, piece].astype(F32) - coef * old_piece(o, piece)
            left_over = left_over + jnp.sum(part * part, axis=0, keepdims=True)
        left_over = lanes_sum(left_over)
        row = lax.broadcasted_iota(jnp.int32, (8, 128), 0)
        packed = jnp.where(row == 0, with_old, jnp.where(row == 1, old_old, left_over))
        strecv[o, chan] = packed
        copies = [
            remote(
                strecv.at[o, chan],
                strecv.at[o, chan],
                t_send.at[o, d],
                t_recv.at[o, d],
                {"chan": (chan + d) % 4},
            )
            for d in range(1, 4)
        ]
        for copy in copies:
            copy.start()
        for copy in copies:
            copy.wait_recv()
        sent = sent + copies
        parts = [strecv[o, i] for i in range(4)]
        gd = [part[0:1] for part in parts]
        dd = [part[1:2] for part in parts]
        rr = [part[2:3] for part in parts]
        mean_sq = (dd[0] + dd[1] + dd[2] + dd[3]) / ENTRIES + tiny_eps
        along = (gd[0] + gd[1] + gd[2] + gd[3]) / ENTRIES / mean_sq
        spread = jnp.zeros((1, 128), F32)
        for i in range(4):
            mine = jnp.where(dd[i] > 0.0, gd[i] / jnp.maximum(dd[i], 1e-30), 0.0)
            off = mine - along
            spread = spread + rr[i] + off * (off * dd[i] + 2.0 * (gd[i] - mine * dd[i]))
        spread = jnp.maximum(spread, 0.0) / ENTRIES + tiny_eps
        along_row = three(along)
        gain = three(move_rate / jnp.sqrt(spread))
        shrink = three(1.0 / jnp.sqrt(mean_sq + 0.25))
        for piece in range(PLANE):
            was = old_piece(o, piece)
            across = agbuf[o, piece].astype(F32) - along_row * was
            top, left = piece // 4 * 48, piece % 4 * 384
            new[top : top + 48, left : left + 384] = (was + gain * across) * shrink
        for copy in sent:
            copy.wait_send()

    def place_block(o):
        lane = lax.broadcasted_iota(jnp.int32, (1, 128), 1)
        keep = jnp.where(lane // BLOCK_ATOMS == plan_ref[o], 0.0, 1.0)
        keep_low = keep.astype(BF16)
        for group in range(12):
            parts = split(new[:, group * 128 : (group + 1) * 128])
            first = dot(parts[0], spot[o])
            whole = first + dot(parts[1], spot[o]) + dot(parts[2], spot[o])
            for i in range(8):
                lag = group * 8 + i
                j, q, s = lag // 48, lag % 48 // 16, lag % 16
                rows = slice(s * 128, s * 128 + CHANS)
                lanes = slice(j * 128, (j + 1) * 128)
                mine = slice(i * 128, (i + 1) * 128)
                taps = pl.ds(lag, CHANS, stride=L)
                dt_out[taps, :] = dt_out[taps, :] * keep + whole[:, mine]
                if o < OUTER - 1:
                    block = wb[q, rows, lanes] * keep_low + first[:, mine].astype(BF16)
                    wb[q, rows, lanes] = block
                    wat[q, j * 128 : j * 128 + CHANS, s * 128 : (s + 1) * 128] = block

    for o in range(OUTER):
        clear_early(o)
        residual_rows(o, 96, 608)
        update_rows(o, 0, 96, 512)
        residual_rows(o, 192, 512)
        update_rows(o, 1, 192, 416)
        if o < OUTER - 1:
            zsend[o + 1] = zst[o, OWN : OWN + SEG]
            zst[o + 1, OWN : OWN + SEG] = zsend[o + 1]
            halo = halo_copies(o + 1)
            for copy in halo:
                copy.start()
        else:
            codes_out[...] = zst[o, OWN : OWN + SEG].T
        residual_rows(o, 288, 416)
        renew(o)
        place_block(o)
        if o < OUTER - 1:
            for copy in halo:
                copy.wait()


def shards(segments, signal, codes_init, dictionary_init, threshold, plan):
    turned = dictionary_init.T
    depth = segments // PLANE
    vmem = pl.BlockSpec(memory_space=pltpu.VMEM)
    dma = pltpu.SemaphoreType.DMA
    codes, resid, dt = pl.pallas_call(
        functools.partial(kernel, segments),
        out_shape=(
            jax.ShapeDtypeStruct((K, SEG), F32),
            jax.ShapeDtypeStruct((CHANS, SEG), F32),
            jax.ShapeDtypeStruct((CHANS * L, K), F32),
        ),
        in_specs=[pl.BlockSpec(memory_space=pltpu.SMEM)] + [vmem] * 4,
        out_specs=(vmem, vmem, vmem),
        scratch_shapes=[
            pltpu.VMEM((OUTER, ROWS, 128), F32),
            pltpu.VMEM((OUTER, SEG, 128), F32),
            pltpu.VMEM((ROWS, 128), BF16),
            pltpu.VMEM((SEG, 128), BF16),
            pltpu.VMEM((ROWS, 128), F32),
            pltpu.VMEM((ROWS, 2048), BF16),
            pltpu.VMEM((ROWS, 2048), BF16),
            pltpu.VMEM((3, 2048, 256), BF16),
            pltpu.VMEM((3, 256, 2048), BF16),
            pltpu.VMEM((560, 256), F32),
            pltpu.VMEM((416, 128), BF16),
            pltpu.VMEM((416, 128), BF16),
            pltpu.VMEM((4, 416, 128), BF16),
            pltpu.VMEM((4, 416, 128), BF16),
            pltpu.VMEM((208, 256), BF16),
            pltpu.VMEM((CHANS, 1536), BF16),
            pltpu.VMEM((PLANE, 48, 384), BF16),
            pltpu.VMEM((OUTER, PLANE, 48, 384), BF16),
            pltpu.VMEM((OUTER, depth, 48, 384), BF16),
            pltpu.VMEM((OUTER, PLANE, 48, 384), BF16),
            pltpu.VMEM((OUTER, CHANS, 1536), F32),
            pltpu.VMEM((CHANS, 1536), F32),
            pltpu.VMEM((2, CHANS, 2048), BF16),
            pltpu.VMEM((1024, 256), BF16),
            pltpu.VMEM((OUTER, 128, 1024), BF16),
            pltpu.VMEM((OUTER, 4, 8, 128), F32),
            dma((OUTER, 5)),
            dma((OUTER, 5)),
            dma((4,)),
            dma((4,)),
            dma((4, 2)),
            dma((4, 2)),
            dma((OUTER, PLANE)),
            dma((OUTER, PLANE)),
            dma((OUTER, depth)),
            dma((OUTER, depth)),
            dma((OUTER, PLANE)),
            dma((OUTER, PLANE)),
            dma((OUTER, 4)),
            dma((OUTER, 4)),
        ],
        compiler_params=pltpu.CompilerParams(
            collective_id=0, has_side_effects=True, vmem_limit_bytes=60 * 1024 * 1024
        ),
    )(plan, turned, codes_init, signal, threshold[None, :])
    return codes, dt.T, resid


def solution(mesh):
    placed = (P("chan", "tm"), P(None, "tm"), P(None, "chan"), P(), P())
    return jax.shard_map(
        functools.partial(shards, mesh.shape["tm"]),
        mesh=mesh,
        in_specs=placed,
        out_specs=(P(None, "tm"), P(None, "chan"), P("chan", "tm")),
        check_vma=False,
    )
```

```python
import functools

import jax
import jax.numpy as jnp
from jax import lax
from jax.experimental import pallas as pl
from jax.experimental.pallas import tpu as pltpu
from jax.sharding import PartitionSpec as P

C = 384
K = 128
L = 96
BLOCK_ATOMS = 16
INNER = 2
OUTER = 2
CHANS = 96
SEG = 128
ENTRIES = C * L

code_rate = 0.3
move_rate = 0.5
tiny_eps = 1e-06

MESH = pl.DeviceIdType.MESH
F32 = jnp.float32
BF16 = jnp.bfloat16

OWN = 288
ROWS = 608
PLANE = 8
HALO = (
    (1, 0, 128, 160),
    (2, 0, 128, 32),
    (3, 96, 32, 0),
    (-1, 0, 128, 416),
    (-2, 0, 64, 544),
)
SIGNAL_HALO = (
    (1, 0, 128, 160),
    (2, 64, 64, 96),
    (-1, 0, 128, 416),
    (-2, 0, 64, 544),
)


def dot(a, b):
    return lax.dot_general(a, b, (((1,), (0,)), ((), ())), preferred_element_type=F32)


def dot_t(a, b):
    return lax.dot_general(a, b, (((1,), (1,)), ((), ())), preferred_element_type=F32)


def kernel(
    segments,
    plan_ref,
    dt_ref,
    codes_ref,
    signal_ref,
    thr_ref,
    codes_out,
    resid_out,
    dt_out,
    zst,
    zsend,
    sgx,
    sgown,
    rst,
    zp,
    rp,
    wb,
    wat,
    acc,
    sx,
    sx2,
    rx1,
    rx2,
    a16,
    gfull,
    gsend,
    grecv,
    zbuf,
    agbuf,
    old,
    new,
    pick,
    strecv,
    h_send,
    h_recv,
    s_send,
    s_recv,
    c_send,
    c_recv,
    p_send,
    p_recv,
    z_send,
    z_recv,
    a_send,
    a_recv,
    t_send,
    t_recv,
    keep_sem,
):
    unit = ENTRIES ** (-0.5)
    tm = lax.axis_index("tm")
    chan = lax.axis_index("chan")
    depth = segments // PLANE
    place = tm % PLANE
    level = tm // PLANE

    def seg(d):
        return (tm + d + segments) % segments

    def in_plane(d):
        return level * PLANE + (place + d) % PLANE

    def in_depth(d):
        return ((level + d) % depth) * PLANE + place

    partner = chan + 1 - 2 * (chan % 2)
    opposite = (chan + 2) % 4

    zsend[0] = codes_ref[...].T
    zst[0, OWN : OWN + SEG] = zsend[0]
    low = jnp.concatenate(
        [signal_ref[...].astype(F32), jnp.zeros((SEG - CHANS, SEG), F32)], axis=0
    ).T.astype(BF16)
    sgown[...] = low
    sgx[OWN : OWN + SEG] = low

    keep = pltpu.make_async_copy(dt_ref, dt_out, keep_sem)
    keep.start()

    def pick_body(o, carry):
        tall = lax.broadcasted_iota(jnp.int32, (1024, 128), 0)
        wide = lax.broadcasted_iota(jnp.int32, (1024, 128), 1)
        block = plan_ref[o]
        hit = ((tall // 128 + block) % 8 == wide // 16) & (
            tall % 128 == wide % 16 + block * BLOCK_ATOMS
        )
        pick[o] = jnp.where(hit, 1.0, 0.0).astype(BF16)
        return carry

    lax.fori_loop(0, OUTER, pick_body, 0)

    barrier = pltpu.get_barrier_semaphore()
    peers = [{"tm": seg(d)} for d in (-3, -2, -1, 1, 2, 3)]
    peers += [{"chan": (chan + d) % 4} for d in range(1, 4)]
    peers += [{"tm": in_plane(d)} for d in range(1, PLANE)]
    peers += [{"tm": in_depth(d)} for d in range(1, depth)]
    for peer in peers:
        pl.semaphore_signal(barrier, inc=1, device_id=peer, device_id_type=MESH)
    pl.semaphore_wait(barrier, len(peers))

    def remote(src, dst, send, recv, peer):
        return pltpu.make_async_remote_copy(
            src_ref=src,
            dst_ref=dst,
            send_sem=send,
            recv_sem=recv,
            device_id=peer,
            device_id_type=MESH,
        )

    def halo_copies(o):
        return [
            remote(
                zsend.at[o, pl.ds(first, rows)],
                zst.at[o, pl.ds(land, rows)],
                h_send.at[o, i],
                h_recv.at[o, i],
                {"tm": seg(d)},
            )
            for i, (d, first, rows, land) in enumerate(HALO)
        ]

    signal_copies = [
        remote(
            sgown.at[pl.ds(first, rows)],
            sgx.at[pl.ds(land, rows)],
            s_send.at[i],
            s_recv.at[i],
            {"tm": seg(d)},
        )
        for i, (d, first, rows, land) in enumerate(SIGNAL_HALO)
    ]
    halo = halo_copies(0)
    for copy in halo + signal_copies:
        copy.start()

    for q in range(3):
        for s in range(16):
            wb[q, s * 128 + CHANS : (s + 1) * 128] = jnp.zeros((128 - CHANS, 256), BF16)
        for j in range(2):
            wat[q, j * 128 + CHANS : (j + 1) * 128] = jnp.zeros((128 - CHANS, 2048), BF16)
    lane_block = lax.broadcasted_iota(jnp.int32, (CHANS, 128), 1) // BLOCK_ATOMS

    def arrange(i, carry):
        j, q = i // 3, i % 3
        here = pl.multiple_of(j * 128, 128)
        for half in range(2):
            found = [jnp.zeros((CHANS, 128), F32)] * OUTER
            for k in range(8):
                s = half * 8 + k
                value = dt_ref[pl.ds(16 * i + s, CHANS, stride=L), :]
                low = value.astype(BF16)
                wb[q, s * 128 : s * 128 + CHANS, pl.ds(here, 128)] = low
                wat[q, pl.ds(here, CHANS), s * 128 : (s + 1) * 128] = low
                turned = pltpu.roll(value, 16 * k, 1) if k else value
                found = [
                    jnp.where(lane_block == (plan_ref[o] + k) % 8, turned, found[o])
                    for o in range(OUTER)
                ]
            group = pl.ds(pl.multiple_of(i * 256 + half * 128, 128), 128)
            for o in range(OUTER):
                old[o, :, group] = found[o]
        return carry

    lax.fori_loop(0, 6, arrange, 0)

    for copy in halo + signal_copies:
        copy.wait()

    def in_window(a, b):
        when = tm * SEG - OWN + a + lax.broadcasted_iota(jnp.int32, (b - a, 1), 0)
        return when

    def clear_early(o):
        zst[o, 0:OWN] = jnp.where(in_window(0, OWN) >= 0, zst[o, 0:OWN], 0.0)

    def residual_rows(o, a, b):
        top = a - 80
        for s in range(16):
            zp[top:b, s * 128 : (s + 1) * 128] = zst[o, pl.ds(top - s, b - top), :].astype(BF16)
        n = b - a + 48
        acc[0:n] = jnp.zeros((n, 256), F32)

        def body(q, carry):
            acc[0:n] += dot_t(zp[pl.ds(pl.multiple_of(a - 48 - 16 * q, 16), n), :], wat[q])
            return carry

        lax.fori_loop(0, 3, body, 0)
        made = unit * (acc[48:n, 0:128] + acc[0 : n - 48, 128:256])
        value = sgx[a:b].astype(F32) - made
        rst[a:b] = jnp.where(in_window(a, b) < segments * SEG, value, 0.0)

    def score_rows(a, b):
        end = b + 80
        for s in range(16):
            rp[a:end, s * 128 : (s + 1) * 128] = rst[pl.ds(a + s, end - a), :].astype(BF16)
        n = b - a + 48
        acc[0:n] = jnp.zeros((n, 256), F32)

        def body(q, carry):
            acc[0:n] += dot(rp[pl.ds(pl.multiple_of(a + 16 * q, 16), n), :], wb[q])
            return carry

        lax.fori_loop(0, 3, body, 0)
        return unit * (acc[0 : n - 48, 0:128] + acc[48:n, 128:256])

    def update_rows(o, step, a, b):
        n = b - a
        i = o * INNER + step
        sx[0:n] = score_rows(a, b).astype(BF16)
        near = remote(
            sx.at[pl.ds(0, n)],
            rx1.at[i, pl.ds(0, n)],
            c_send.at[i, 0],
            c_recv.at[i, 0],
            {"chan": partner},
        )
        near.start()
        near.wait()
        sx2[0:n] = (sx[0:n].astype(F32) + rx1[i, 0:n].astype(F32)).astype(BF16)
        far = remote(
            sx2.at[pl.ds(0, n)],
            rx2.at[i, pl.ds(0, n)],
            c_send.at[i, 1],
            c_recv.at[i, 1],
            {"chan": opposite},
        )
        far.start()
        far.wait()
        scores = sx2[0:n].astype(F32) + rx2[i, 0:n].astype(F32)
        stepped = zst[o, a:b] + code_rate * scores
        limit = thr_ref[...]
        value = stepped - jnp.clip(stepped, -limit, limit)
        zst[o, a:b] = jnp.where(in_window(a, b) >= 0, value, 0.0)

    def lanes_sum(row):
        total = row[:, 0:128] + row[:, 128:256] + row[:, 256:384]
        total = jnp.broadcast_to(total, (8, 128))
        for shift in (64, 32, 16):
            total = total + pltpu.roll(total, shift, 1)
        return total

    def old_piece(o, piece):
        top, left = piece // 4 * 48, piece % 4 * 384
        return old[o, top : top + 48, left : left + 384]

    def three(row):
        return jnp.concatenate([row[0:1]] * 3, axis=1)

    def renew(o):
        turned = rst[OWN : OWN + SEG].T
        resid_out[...] = turned[0:CHANS]
        for half in range(2):
            lanes = slice(half * 128, half * 128 + 128)
            a16[:, lanes] = dot(
                zp[OWN - 80 : OWN + SEG, half * 1024 : half * 1024 + 1024],
                pick[o],
            ).astype(BF16)
        across_time = turned[0:CHANS].astype(BF16)
        for q in range(6):
            gfull[:, q * 256 : (q + 1) * 256] = dot(
                across_time, a16[80 - 16 * q : 208 - 16 * q, :]
            ).astype(BF16)
        for piece in range(PLANE):
            top, left = piece // 4 * 48, piece % 4 * 384
            gsend[piece] = gfull[top : top + 48, left : left + 384]
        copies = [
            remote(
                gsend.at[(place + d) % PLANE],
                grecv.at[o, d],
                p_send.at[o, d],
                p_recv.at[o, d],
                {"tm": in_plane(d)},
            )
            for d in range(1, PLANE)
        ]
        for copy in copies:
            copy.start()
        total = gsend[place].astype(F32)
        for d, copy in enumerate(copies, 1):
            copy.wait_recv()
            total = total + grecv[o, d].astype(F32)
        zbuf[o, level] = total.astype(BF16)
        sent = copies
        copies = [
            remote(
                zbuf.at[o, level],
                zbuf.at[o, level],
                z_send.at[o, d],
                z_recv.at[o, d],
                {"tm": in_depth(d)},
            )
            for d in range(1, depth)
        ]
        for copy in copies:
            copy.start()
        for copy in copies:
            copy.wait_recv()
        sent = sent + copies
        total = zbuf[o, 0].astype(F32)
        for i in range(1, depth):
            total = total + zbuf[o, i].astype(F32)
        agbuf[o, place] = total.astype(BF16)
        copies = [
            remote(
                agbuf.at[o, place],
                agbuf.at[o, place],
                a_send.at[o, d],
                a_recv.at[o, d],
                {"tm": in_plane(d)},
            )
            for d in range(1, PLANE)
        ]
        for copy in copies:
            copy.start()
        for copy in copies:
            copy.wait_recv()
        sent = sent + copies

        with_old = jnp.zeros((1, 384), F32)
        old_old = jnp.zeros((1, 384), F32)
        for piece in range(PLANE):
            grad, was = agbuf[o, piece].astype(F32), old_piece(o, piece)
            with_old = with_old + jnp.sum(grad * was, axis=0, keepdims=True)
            old_old = old_old + jnp.sum(was * was, axis=0, keepdims=True)
        with_old, old_old = lanes_sum(with_old), lanes_sum(old_old)
        own_coef = jnp.where(old_old > 0.0, with_old / jnp.maximum(old_old, 1e-30), 0.0)
        left_over = jnp.zeros((1, 384), F32)
        coef = three(own_coef)
        for piece in range(PLANE):
            part = agbuf[o, piece].astype(F32) - coef * old_piece(o, piece)
            left_over = left_over + jnp.sum(part * part, axis=0, keepdims=True)
        left_over = lanes_sum(left_over)
        row = lax.broadcasted_iota(jnp.int32, (8, 128), 0)
        packed = jnp.where(row == 0, with_old, jnp.where(row == 1, old_old, left_over))
        strecv[o, chan] = packed
        copies = [
            remote(
                strecv.at[o, chan],
                strecv.at[o, chan],
                t_send.at[o, d],
                t_recv.at[o, d],
                {"chan": (chan + d) % 4},
            )
            for d in range(1, 4)
        ]
        for copy in copies:
            copy.start()
        for copy in copies:
            copy.wait_recv()
        sent = sent + copies
        parts = [strecv[o, i] for i in range(4)]
        gd = [part[0:1] for part in parts]
        dd = [part[1:2] for part in parts]
        rr = [part[2:3] for part in parts]
        mean_sq = (dd[0] + dd[1] + dd[2] + dd[3]) / ENTRIES + tiny_eps
        along = (gd[0] + gd[1] + gd[2] + gd[3]) / ENTRIES / mean_sq
        spread = jnp.zeros((1, 128), F32)
        for i in range(4):
            mine = jnp.where(dd[i] > 0.0, gd[i] / jnp.maximum(dd[i], 1e-30), 0.0)
            off = mine - along
            spread = spread + rr[i] + off * (off * dd[i] + 2.0 * (gd[i] - mine * dd[i]))
        spread = jnp.maximum(spread, 0.0) / ENTRIES + tiny_eps
        along_row = three(along)
        gain = three(move_rate / jnp.sqrt(spread))
        shrink = three(1.0 / jnp.sqrt(mean_sq + 0.25))
        for piece in range(PLANE):
            was = old_piece(o, piece)
            across = agbuf[o, piece].astype(F32) - along_row * was
            top, left = piece // 4 * 48, piece % 4 * 384
            new[top : top + 48, left : left + 384] = (was + gain * across) * shrink
        for copy in sent:
            copy.wait_send()

    def place_block(o, arranged):
        mine = lane_block == plan_ref[o]

        def body(i, carry):
            j, q = i // 3, i % 3
            here = pl.multiple_of(j * 128, 128)
            for half in range(2):
                value = new[:, pl.ds(pl.multiple_of(i * 256 + half * 128, 128), 128)]
                for k in range(8):
                    s = half * 8 + k
                    taps = pl.ds(16 * i + s, CHANS, stride=L)
                    turned = pltpu.roll(value, 128 - 16 * k, 1) if k else value
                    merged = jnp.where(mine, turned, dt_out[taps, :])
                    dt_out[taps, :] = merged
                    if arranged:
                        low = merged.astype(BF16)
                        wb[q, s * 128 : s * 128 + CHANS, pl.ds(here, 128)] = low
                        wat[q, pl.ds(here, CHANS), s * 128 : (s + 1) * 128] = low
            return carry

        lax.fori_loop(0, 6, body, 0)

    keep.wait()

    def outer(o, carry):
        clear_early(o)
        residual_rows(o, 96, 608)
        update_rows(o, 0, 96, 512)
        residual_rows(o, 192, 512)
        update_rows(o, 1, 192, 416)

        @pl.when(o < OUTER - 1)
        def _():
            zsend[1] = zst[0, OWN : OWN + SEG]
            zst[1, OWN : OWN + SEG] = zst[0, OWN : OWN + SEG]
            for copy in halo_copies(1):
                copy.start()

        residual_rows(o, 288, 416)
        renew(o)

        @pl.when(o < OUTER - 1)
        def _():
            place_block(0, True)
            for copy in halo_copies(1):
                copy.wait()

        return carry

    lax.fori_loop(0, OUTER, outer, 0)
    codes_out[...] = zst[OUTER - 1, OWN : OWN + SEG].T
    place_block(OUTER - 1, False)


def shards(segments, signal, codes_init, dictionary_init, threshold, plan):
    turned = dictionary_init.T
    depth = segments // PLANE
    vmem = pl.BlockSpec(memory_space=pltpu.VMEM)
    dma = pltpu.SemaphoreType.DMA
    codes, resid, dt = pl.pallas_call(
        functools.partial(kernel, segments),
        out_shape=(
            jax.ShapeDtypeStruct((K, SEG), F32),
            jax.ShapeDtypeStruct((CHANS, SEG), F32),
            jax.ShapeDtypeStruct((CHANS * L, K), F32),
        ),
        in_specs=[pl.BlockSpec(memory_space=pltpu.SMEM)] + [vmem] * 4,
        out_specs=(vmem, vmem, vmem),
        scratch_shapes=[
            pltpu.VMEM((OUTER, ROWS, 128), F32),
            pltpu.VMEM((OUTER, SEG, 128), F32),
            pltpu.VMEM((ROWS, 128), BF16),
            pltpu.VMEM((SEG, 128), BF16),
            pltpu.VMEM((ROWS, 128), F32),
            pltpu.VMEM((ROWS, 2048), BF16),
            pltpu.VMEM((ROWS, 2048), BF16),
            pltpu.VMEM((3, 2048, 256), BF16),
            pltpu.VMEM((3, 256, 2048), BF16),
            pltpu.VMEM((560, 256), F32),
            pltpu.VMEM((416, 128), BF16),
            pltpu.VMEM((416, 128), BF16),
            pltpu.VMEM((4, 416, 128), BF16),
            pltpu.VMEM((4, 416, 128), BF16),
            pltpu.VMEM((208, 256), BF16),
            pltpu.VMEM((CHANS, 1536), BF16),
            pltpu.VMEM((PLANE, 48, 384), BF16),
            pltpu.VMEM((OUTER, PLANE, 48, 384), BF16),
            pltpu.VMEM((OUTER, depth, 48, 384), BF16),
            pltpu.VMEM((OUTER, PLANE, 48, 384), BF16),
            pltpu.VMEM((OUTER, CHANS, 1536), F32),
            pltpu.VMEM((CHANS, 1536), F32),
            pltpu.VMEM((OUTER, 1024, 128), BF16),
            pltpu.VMEM((OUTER, 4, 8, 128), F32),
            dma((OUTER, 5)),
            dma((OUTER, 5)),
            dma((4,)),
            dma((4,)),
            dma((4, 2)),
            dma((4, 2)),
            dma((OUTER, PLANE)),
            dma((OUTER, PLANE)),
            dma((OUTER, depth)),
            dma((OUTER, depth)),
            dma((OUTER, PLANE)),
            dma((OUTER, PLANE)),
            dma((OUTER, 4)),
            dma((OUTER, 4)),
            dma,
        ],
        compiler_params=pltpu.CompilerParams(
            collective_id=0, has_side_effects=True, vmem_limit_bytes=60 * 1024 * 1024
        ),
    )(plan, turned, codes_init, signal, threshold[None, :])
    return codes, dt.T, resid


def solution(mesh):
    placed = (P("chan", "tm"), P(None, "tm"), P(None, "chan"), P(), P())
    return jax.shard_map(
        functools.partial(shards, mesh.shape["tm"]),
        mesh=mesh,
        in_specs=placed,
        out_specs=(P(None, "tm"), P(None, "chan"), P("chan", "tm")),
        check_vma=False,
    )
```

```python
import functools

import jax
import jax.numpy as jnp
from jax import lax
from jax.experimental import pallas as pl
from jax.experimental.pallas import tpu as pltpu
from jax.sharding import PartitionSpec as P

C = 384
K = 128
L = 96
BLOCK_ATOMS = 16
INNER = 2
OUTER = 2
CHANS = 96
SEG = 128
ENTRIES = C * L

code_rate = 0.3
move_rate = 0.5
tiny_eps = 1e-06

MESH = pl.DeviceIdType.MESH
F32 = jnp.float32
BF16 = jnp.bfloat16

OWN = 288
ROWS = 608
PLANE = 8
HALO = (
    (1, 0, 128, 160),
    (2, 0, 128, 32),
    (3, 96, 32, 0),
    (-1, 0, 128, 416),
    (-2, 0, 64, 544),
)
SIGNAL_HALO = (
    (1, 0, 128, 160),
    (2, 64, 64, 96),
    (-1, 0, 128, 416),
    (-2, 0, 64, 544),
)


def dot(a, b):
    return lax.dot_general(a, b, (((1,), (0,)), ((), ())), preferred_element_type=F32)


def dot_t(a, b):
    return lax.dot_general(a, b, (((1,), (1,)), ((), ())), preferred_element_type=F32)


def kernel(
    segments,
    plan_ref,
    dt_hbm,
    codes_ref,
    signal_ref,
    thr_ref,
    codes_out,
    resid_out,
    dt_out,
    zst,
    zsend,
    sgx,
    sgown,
    rst,
    zp,
    rp,
    wb,
    wat,
    acc,
    sx,
    sx2,
    rx1,
    rx2,
    a16,
    gfull,
    gsend,
    grecv,
    zbuf,
    agbuf,
    old,
    new,
    pick,
    dt_ref,
    by_lag,
    strecv,
    h_send,
    h_recv,
    s_send,
    s_recv,
    c_send,
    c_recv,
    p_send,
    p_recv,
    z_send,
    z_recv,
    a_send,
    a_recv,
    t_send,
    t_recv,
    load_sem,
):
    unit = ENTRIES ** (-0.5)
    tm = lax.axis_index("tm")
    chan = lax.axis_index("chan")
    depth = segments // PLANE
    place = tm % PLANE
    level = tm // PLANE

    def seg(d):
        return (tm + d + segments) % segments

    def in_plane(d):
        return level * PLANE + (place + d) % PLANE

    def in_depth(d):
        return ((level + d) % depth) * PLANE + place

    partner = chan + 1 - 2 * (chan % 2)
    opposite = (chan + 2) % 4

    load = pltpu.make_async_copy(dt_hbm, dt_ref, load_sem)
    load.start()
    zsend[0] = codes_ref[...].T
    zst[0, OWN : OWN + SEG] = zsend[0]
    low = jnp.concatenate(
        [signal_ref[...].astype(F32), jnp.zeros((SEG - CHANS, SEG), F32)], axis=0
    ).T.astype(BF16)
    sgown[...] = low
    sgx[OWN : OWN + SEG] = low


    def pick_body(o, carry):
        tall = lax.broadcasted_iota(jnp.int32, (1024, 128), 0)
        wide = lax.broadcasted_iota(jnp.int32, (1024, 128), 1)
        block = plan_ref[o]
        hit = ((tall // 128 + block) % 8 == wide // 16) & (
            tall % 128 == wide % 16 + block * BLOCK_ATOMS
        )
        pick[o] = jnp.where(hit, 1.0, 0.0).astype(BF16)
        return carry

    lax.fori_loop(0, OUTER, pick_body, 0)

    barrier = pltpu.get_barrier_semaphore()
    peers = [{"tm": seg(d)} for d in (-3, -2, -1, 1, 2, 3)]
    peers += [{"chan": (chan + d) % 4} for d in range(1, 4)]
    peers += [{"tm": in_plane(d)} for d in range(1, PLANE)]
    peers += [{"tm": in_depth(d)} for d in range(1, depth)]
    for peer in peers:
        pl.semaphore_signal(barrier, inc=1, device_id=peer, device_id_type=MESH)
    pl.semaphore_wait(barrier, len(peers))

    def remote(src, dst, send, recv, peer):
        return pltpu.make_async_remote_copy(
            src_ref=src,
            dst_ref=dst,
            send_sem=send,
            recv_sem=recv,
            device_id=peer,
            device_id_type=MESH,
        )

    def halo_copies(o):
        return [
            remote(
                zsend.at[o, pl.ds(first, rows)],
                zst.at[o, pl.ds(land, rows)],
                h_send.at[o, i],
                h_recv.at[o, i],
                {"tm": seg(d)},
            )
            for i, (d, first, rows, land) in enumerate(HALO)
        ]

    signal_copies = [
        remote(
            sgown.at[pl.ds(first, rows)],
            sgx.at[pl.ds(land, rows)],
            s_send.at[i],
            s_recv.at[i],
            {"tm": seg(d)},
        )
        for i, (d, first, rows, land) in enumerate(SIGNAL_HALO)
    ]
    halo = halo_copies(0)
    for copy in halo + signal_copies:
        copy.start()

    for q in range(3):
        for s in range(16):
            wb[q, s * 128 + CHANS : (s + 1) * 128] = jnp.zeros((128 - CHANS, 256), BF16)
        for j in range(2):
            wat[q, j * 128 + CHANS : (j + 1) * 128] = jnp.zeros((128 - CHANS, 2048), BF16)
    load.wait()
    lane_block = lax.broadcasted_iota(jnp.int32, (CHANS, 128), 1) // BLOCK_ATOMS

    def arrange(i, carry):
        j, q = i // 3, i % 3
        here = pl.multiple_of(j * 128, 128)
        for half in range(2):
            found = [jnp.zeros((CHANS, 128), F32)] * OUTER
            for k in range(8):
                s = half * 8 + k
                value = dt_ref[pl.ds(16 * i + s, CHANS, stride=L), :]
                by_lag[16 * i + s] = value
                low = value.astype(BF16)
                wb[q, s * 128 : s * 128 + CHANS, pl.ds(here, 128)] = low
                wat[q, pl.ds(here, CHANS), s * 128 : (s + 1) * 128] = low
                turned = pltpu.roll(value, 16 * k, 1) if k else value
                found = [
                    jnp.where(lane_block == (plan_ref[o] + k) % 8, turned, found[o])
                    for o in range(OUTER)
                ]
            group = pl.ds(pl.multiple_of(i * 256 + half * 128, 128), 128)
            for o in range(OUTER):
                old[o, :, group] = found[o]
        return carry

    lax.fori_loop(0, 6, arrange, 0)

    for copy in halo + signal_copies:
        copy.wait()

    def in_window(a, b):
        when = tm * SEG - OWN + a + lax.broadcasted_iota(jnp.int32, (b - a, 1), 0)
        return when

    def clear_early(o):
        zst[o, 0:OWN] = jnp.where(in_window(0, OWN) >= 0, zst[o, 0:OWN], 0.0)

    def residual_rows(o, a, b):
        top = a - 80
        for s in range(16):
            zp[top:b, s * 128 : (s + 1) * 128] = zst[o, pl.ds(top - s, b - top), :].astype(BF16)
        n = b - a + 48
        acc[0:n] = jnp.zeros((n, 256), F32)

        def body(q, carry):
            acc[0:n] += dot_t(zp[pl.ds(pl.multiple_of(a - 48 - 16 * q, 16), n), :], wat[q])
            return carry

        lax.fori_loop(0, 3, body, 0)
        made = unit * (acc[48:n, 0:128] + acc[0 : n - 48, 128:256])
        value = sgx[a:b].astype(F32) - made
        rst[a:b] = jnp.where(in_window(a, b) < segments * SEG, value, 0.0)

    def update_rows(o, step, a, b):
        n, i = b - a, o * INNER + step
        half = n // 2
        end = b + 80
        for s in range(16):
            rp[a:end, s * 128 : (s + 1) * 128] = rst[pl.ds(a + s, end - a), :].astype(BF16)
        near, far = [], []
        for part, (first, last) in enumerate(((0, half + 48), (half + 48, n + 48))):
            rows = last - first
            acc[first:last] = jnp.zeros((rows, 256), F32)

            def body(q, carry):
                start = pl.multiple_of(a + first + 16 * q, 16)
                acc[first:last] += dot(rp[pl.ds(start, rows), :], wb[q])
                return carry

            lax.fori_loop(0, 3, body, 0)
            low, high = part * half, (part + 1) * half
            scores = unit * (acc[low:high, 0:128] + acc[low + 48 : high + 48, 128:256])
            sx[low:high] = scores.astype(BF16)
            copy = remote(
                sx.at[pl.ds(low, half)],
                rx1.at[i, pl.ds(low, half)],
                c_send.at[i, 0, part],
                c_recv.at[i, 0, part],
                {"chan": partner},
            )
            copy.start()
            near.append(copy)
        for part in range(2):
            low, high = part * half, (part + 1) * half
            near[part].wait()
            sx2[low:high] = (
                sx[low:high].astype(F32) + rx1[i, pl.ds(low, half)].astype(F32)
            ).astype(BF16)
            copy = remote(
                sx2.at[pl.ds(low, half)],
                rx2.at[i, pl.ds(low, half)],
                c_send.at[i, 1, part],
                c_recv.at[i, 1, part],
                {"chan": opposite},
            )
            copy.start()
            far.append(copy)
        limit = thr_ref[...]
        for part in range(2):
            low, high = part * half, (part + 1) * half
            far[part].wait()
            scores = sx2[low:high].astype(F32) + rx2[i, pl.ds(low, half)].astype(F32)
            stepped = zst[o, a + low : a + high] + code_rate * scores
            value = stepped - jnp.clip(stepped, -limit, limit)
            zst[o, a + low : a + high] = jnp.where(in_window(a + low, a + high) >= 0, value, 0.0)

    def lanes_sum(row):
        total = row[:, 0:128] + row[:, 128:256] + row[:, 256:384]
        total = jnp.broadcast_to(total, (8, 128))
        for shift in (64, 32, 16):
            total = total + pltpu.roll(total, shift, 1)
        return total

    def old_piece(o, piece):
        top, left = piece // 4 * 48, piece % 4 * 384
        return old[o, top : top + 48, left : left + 384]

    def three(row):
        return jnp.concatenate([row[0:1]] * 3, axis=1)

    def renew(o):
        turned = rst[OWN : OWN + SEG].T
        resid_out[...] = turned[0:CHANS]
        for half in range(2):
            lanes = slice(half * 128, half * 128 + 128)
            a16[:, lanes] = dot(
                zp[OWN - 80 : OWN + SEG, half * 1024 : half * 1024 + 1024],
                pick[o],
            ).astype(BF16)
        across_time = turned[0:CHANS].astype(BF16)
        for q in range(6):
            gfull[:, q * 256 : (q + 1) * 256] = dot(
                across_time, a16[80 - 16 * q : 208 - 16 * q, :]
            ).astype(BF16)
        for piece in range(PLANE):
            top, left = piece // 4 * 48, piece % 4 * 384
            gsend[piece] = gfull[top : top + 48, left : left + 384]
        sent = []

        def spread_rows(part, peers, source, target, send, recv):
            rows = pl.ds(part * 16, 16)
            copies = [
                remote(
                    source(d).at[rows],
                    target(d).at[rows],
                    send.at[o, d, part],
                    recv.at[o, d, part],
                    {"tm": peer},
                )
                for d, peer in peers
            ]
            for copy in copies:
                copy.start()
            sent.extend(copies)
            return copies

        plane = [(d, in_plane(d)) for d in range(1, PLANE)]
        levels = [(d, in_depth(d)) for d in range(1, depth)]
        scatter = [
            spread_rows(
                part,
                plane,
                lambda d: gsend.at[(place + d) % PLANE],
                lambda d: grecv.at[o, d],
                p_send,
                p_recv,
            )
            for part in range(3)
        ]
        across_levels = []
        for part in range(3):
            rows = pl.ds(part * 16, 16)
            total = gsend[place, rows].astype(F32)
            for d, copy in enumerate(scatter[part], 1):
                copy.wait_recv()
                total = total + grecv[o, d, rows].astype(F32)
            zbuf[o, level, rows] = total.astype(BF16)
            slot = lambda d: zbuf.at[o, level]
            across_levels.append(spread_rows(part, levels, slot, slot, z_send, z_recv))
        gather = []
        for part in range(3):
            rows = pl.ds(part * 16, 16)
            for copy in across_levels[part]:
                copy.wait_recv()
            total = zbuf[o, 0, rows].astype(F32)
            for i in range(1, depth):
                total = total + zbuf[o, i, rows].astype(F32)
            agbuf[o, place, rows] = total.astype(BF16)
            slot = lambda d: agbuf.at[o, place]
            gather.append(spread_rows(part, plane, slot, slot, a_send, a_recv))
        for copies in gather:
            for copy in copies:
                copy.wait_recv()

        with_old = jnp.zeros((1, 384), F32)
        old_old = jnp.zeros((1, 384), F32)
        for piece in range(PLANE):
            grad, was = agbuf[o, piece].astype(F32), old_piece(o, piece)
            with_old = with_old + jnp.sum(grad * was, axis=0, keepdims=True)
            old_old = old_old + jnp.sum(was * was, axis=0, keepdims=True)
        with_old, old_old = lanes_sum(with_old), lanes_sum(old_old)
        own_coef = jnp.where(old_old > 0.0, with_old / jnp.maximum(old_old, 1e-30), 0.0)
        left_over = jnp.zeros((1, 384), F32)
        coef = three(own_coef)
        for piece in range(PLANE):
            part = agbuf[o, piece].astype(F32) - coef * old_piece(o, piece)
            left_over = left_over + jnp.sum(part * part, axis=0, keepdims=True)
        left_over = lanes_sum(left_over)
        row = lax.broadcasted_iota(jnp.int32, (8, 128), 0)
        packed = jnp.where(row == 0, with_old, jnp.where(row == 1, old_old, left_over))
        strecv[o, chan] = packed
        copies = [
            remote(
                strecv.at[o, chan],
                strecv.at[o, chan],
                t_send.at[o, d],
                t_recv.at[o, d],
                {"chan": (chan + d) % 4},
            )
            for d in range(1, 4)
        ]
        for copy in copies:
            copy.start()
        for copy in copies:
            copy.wait_recv()
        sent = sent + copies
        parts = [strecv[o, i] for i in range(4)]
        gd = [part[0:1] for part in parts]
        dd = [part[1:2] for part in parts]
        rr = [part[2:3] for part in parts]
        mean_sq = (dd[0] + dd[1] + dd[2] + dd[3]) / ENTRIES + tiny_eps
        along = (gd[0] + gd[1] + gd[2] + gd[3]) / ENTRIES / mean_sq
        spread = jnp.zeros((1, 128), F32)
        for i in range(4):
            mine = jnp.where(dd[i] > 0.0, gd[i] / jnp.maximum(dd[i], 1e-30), 0.0)
            off = mine - along
            spread = spread + rr[i] + off * (off * dd[i] + 2.0 * (gd[i] - mine * dd[i]))
        spread = jnp.maximum(spread, 0.0) / ENTRIES + tiny_eps
        along_row = three(along)
        gain = three(move_rate / jnp.sqrt(spread))
        shrink = three(1.0 / jnp.sqrt(mean_sq + 0.25))
        for piece in range(PLANE):
            was = old_piece(o, piece)
            across = agbuf[o, piece].astype(F32) - along_row * was
            top, left = piece // 4 * 48, piece % 4 * 384
            new[top : top + 48, left : left + 384] = (was + gain * across) * shrink
        for copy in sent:
            copy.wait_send()

    def place_block(o, arranged):
        mine = lane_block == plan_ref[o]

        def body(i, carry):
            j, q = i // 3, i % 3
            here = pl.multiple_of(j * 128, 128)
            for half in range(2):
                value = new[:, pl.ds(pl.multiple_of(i * 256 + half * 128, 128), 128)]
                for k in range(8):
                    s = half * 8 + k
                    turned = pltpu.roll(value, 128 - 16 * k, 1) if k else value
                    merged = jnp.where(mine, turned, by_lag[16 * i + s])
                    if not arranged:
                        dt_out[pl.ds(16 * i + s, CHANS, stride=L), :] = merged
                    else:
                        by_lag[16 * i + s] = merged
                        low = merged.astype(BF16)
                        wb[q, s * 128 : s * 128 + CHANS, pl.ds(here, 128)] = low
                        wat[q, pl.ds(here, CHANS), s * 128 : (s + 1) * 128] = low
            return carry

        lax.fori_loop(0, 6, body, 0)

    def outer(o, carry):
        clear_early(o)
        residual_rows(o, 96, 608)
        update_rows(o, 0, 96, 512)
        residual_rows(o, 192, 512)
        update_rows(o, 1, 192, 416)

        @pl.when(o < OUTER - 1)
        def _():
            zsend[1] = zst[0, OWN : OWN + SEG]
            zst[1, OWN : OWN + SEG] = zst[0, OWN : OWN + SEG]
            for copy in halo_copies(1):
                copy.start()

        residual_rows(o, 288, 416)
        renew(o)

        @pl.when(o < OUTER - 1)
        def _():
            place_block(0, True)
            for copy in halo_copies(1):
                copy.wait()

        return carry

    lax.fori_loop(0, OUTER, outer, 0)
    codes_out[...] = zst[OUTER - 1, OWN : OWN + SEG].T
    place_block(OUTER - 1, False)


def shards(segments, signal, codes_init, dictionary_init, threshold, plan):
    turned = dictionary_init.T
    depth = segments // PLANE
    vmem = pl.BlockSpec(memory_space=pltpu.VMEM)
    dma = pltpu.SemaphoreType.DMA
    codes, resid, dt = pl.pallas_call(
        functools.partial(kernel, segments),
        out_shape=(
            jax.ShapeDtypeStruct((K, SEG), F32),
            jax.ShapeDtypeStruct((CHANS, SEG), F32),
            jax.ShapeDtypeStruct((CHANS * L, K), F32),
        ),
        in_specs=[pl.BlockSpec(memory_space=pltpu.SMEM), pl.BlockSpec(memory_space=pl.ANY)]
        + [vmem] * 3,
        out_specs=(vmem, vmem, vmem),
        scratch_shapes=[
            pltpu.VMEM((OUTER, ROWS, 128), F32),
            pltpu.VMEM((OUTER, SEG, 128), F32),
            pltpu.VMEM((ROWS, 128), BF16),
            pltpu.VMEM((SEG, 128), BF16),
            pltpu.VMEM((ROWS, 128), F32),
            pltpu.VMEM((ROWS, 2048), BF16),
            pltpu.VMEM((ROWS, 2048), BF16),
            pltpu.VMEM((3, 2048, 256), BF16),
            pltpu.VMEM((3, 256, 2048), BF16),
            pltpu.VMEM((560, 256), F32),
            pltpu.VMEM((416, 128), BF16),
            pltpu.VMEM((416, 128), BF16),
            pltpu.VMEM((4, 416, 128), BF16),
            pltpu.VMEM((4, 416, 128), BF16),
            pltpu.VMEM((208, 256), BF16),
            pltpu.VMEM((CHANS, 1536), BF16),
            pltpu.VMEM((PLANE, 48, 384), BF16),
            pltpu.VMEM((OUTER, PLANE, 48, 384), BF16),
            pltpu.VMEM((OUTER, depth, 48, 384), BF16),
            pltpu.VMEM((OUTER, PLANE, 48, 384), BF16),
            pltpu.VMEM((OUTER, CHANS, 1536), F32),
            pltpu.VMEM((CHANS, 1536), F32),
            pltpu.VMEM((OUTER, 1024, 128), BF16),
            pltpu.VMEM((CHANS * L, K), F32),
            pltpu.VMEM((L, CHANS, K), F32),
            pltpu.VMEM((OUTER, 4, 8, 128), F32),
            dma((OUTER, 5)),
            dma((OUTER, 5)),
            dma((4,)),
            dma((4,)),
            dma((4, 2, 2)),
            dma((4, 2, 2)),
            dma((OUTER, PLANE, 3)),
            dma((OUTER, PLANE, 3)),
            dma((OUTER, depth, 3)),
            dma((OUTER, depth, 3)),
            dma((OUTER, PLANE, 3)),
            dma((OUTER, PLANE, 3)),
            dma((OUTER, 4)),
            dma((OUTER, 4)),
            dma,
        ],
        compiler_params=pltpu.CompilerParams(
            collective_id=0, has_side_effects=True, vmem_limit_bytes=60 * 1024 * 1024
        ),
    )(plan, turned, codes_init, signal, threshold[None, :])
    return codes, dt.T, resid


def solution(mesh):
    placed = (P("chan", "tm"), P(None, "tm"), P(None, "chan"), P(), P())
    return jax.shard_map(
        functools.partial(shards, mesh.shape["tm"]),
        mesh=mesh,
        in_specs=placed,
        out_specs=(P(None, "tm"), P(None, "chan"), P("chan", "tm")),
        check_vma=False,
    )
```

```python
import functools

import jax
import jax.numpy as jnp
from jax import lax
from jax.experimental import pallas as pl
from jax.experimental.pallas import tpu as pltpu
from jax.sharding import PartitionSpec as P

C = 384
K = 128
L = 96
BLOCK_ATOMS = 16
INNER = 2
OUTER = 2
CHANS = 96
SEG = 128
ENTRIES = C * L

code_rate = 0.3
move_rate = 0.5
tiny_eps = 1e-06

MESH = pl.DeviceIdType.MESH
F32 = jnp.float32
BF16 = jnp.bfloat16

OWN = 288
ROWS = 608
PLANE = 8
HALO = (
    (1, 0, 128, 160),
    (2, 0, 128, 32),
    (3, 96, 32, 0),
    (-1, 0, 128, 416),
    (-2, 0, 64, 544),
)
SIGNAL_HALO = (
    (1, 0, 128, 160),
    (2, 64, 64, 96),
    (-1, 0, 128, 416),
    (-2, 0, 64, 544),
)


def dot(a, b):
    return lax.dot_general(a, b, (((1,), (0,)), ((), ())), preferred_element_type=F32)


def dot_t(a, b):
    return lax.dot_general(a, b, (((1,), (1,)), ((), ())), preferred_element_type=F32)


def kernel(
    segments,
    plan_ref,
    dt_hbm,
    codes_ref,
    signal_ref,
    thr_ref,
    codes_out,
    resid_out,
    rows_first,
    rows_last,
    zst,
    zsend,
    sgx,
    sgown,
    rst,
    zp,
    rp,
    wb,
    wat,
    acc,
    sx,
    sx2,
    rx1,
    rx2,
    a16,
    gfull,
    gsend,
    grecv,
    zbuf,
    agbuf,
    old,
    new,
    pick,
    dt_ref,
    block_codes,
    block_low,
    by_tap,
    in_order,
    by_atom,
    strecv,
    h_send,
    h_recv,
    s_send,
    s_recv,
    c_send,
    c_recv,
    p_send,
    p_recv,
    z_send,
    z_recv,
    a_send,
    a_recv,
    t_send,
    t_recv,
    load_sem,
):
    unit = ENTRIES ** (-0.5)
    tm = lax.axis_index("tm")
    chan = lax.axis_index("chan")
    depth = segments // PLANE
    place = tm % PLANE
    level = tm // PLANE

    def seg(d):
        return (tm + d + segments) % segments

    def in_plane(d):
        return level * PLANE + (place + d) % PLANE

    def in_depth(d):
        return ((level + d) % depth) * PLANE + place

    partner = chan + 1 - 2 * (chan % 2)
    opposite = (chan + 2) % 4

    load = pltpu.make_async_copy(dt_hbm, dt_ref, load_sem)
    load.start()
    zsend[0] = codes_ref[...].T
    zst[0, OWN : OWN + SEG] = zsend[0]
    low = jnp.concatenate(
        [signal_ref[...].astype(F32), jnp.zeros((SEG - CHANS, SEG), F32)], axis=0
    ).T.astype(BF16)
    sgown[...] = low
    sgx[OWN : OWN + SEG] = low


    def pick_body(o, carry):
        tall = lax.broadcasted_iota(jnp.int32, (1024, 128), 0)
        wide = lax.broadcasted_iota(jnp.int32, (1024, 128), 1)
        block = plan_ref[o]
        hit = ((tall // 128 + block) % 8 == wide // 16) & (
            tall % 128 == wide % 16 + block * BLOCK_ATOMS
        )
        pick[o] = jnp.where(hit, 1.0, 0.0).astype(BF16)
        return carry

    lax.fori_loop(0, OUTER, pick_body, 0)

    barrier = pltpu.get_barrier_semaphore()
    peers = [{"tm": seg(d)} for d in (-3, -2, -1, 1, 2, 3)]
    peers += [{"chan": (chan + d) % 4} for d in range(1, 4)]
    peers += [{"tm": in_plane(d)} for d in range(1, PLANE)]
    peers += [{"tm": in_depth(d)} for d in range(1, depth)]
    for peer in peers:
        pl.semaphore_signal(barrier, inc=1, device_id=peer, device_id_type=MESH)
    pl.semaphore_wait(barrier, len(peers))

    def remote(src, dst, send, recv, peer):
        return pltpu.make_async_remote_copy(
            src_ref=src,
            dst_ref=dst,
            send_sem=send,
            recv_sem=recv,
            device_id=peer,
            device_id_type=MESH,
        )

    def halo_copies(o):
        return [
            remote(
                zsend.at[o, pl.ds(first, rows)],
                zst.at[o, pl.ds(land, rows)],
                h_send.at[o, i],
                h_recv.at[o, i],
                {"tm": seg(d)},
            )
            for i, (d, first, rows, land) in enumerate(HALO)
        ]

    signal_copies = [
        remote(
            sgown.at[pl.ds(first, rows)],
            sgx.at[pl.ds(land, rows)],
            s_send.at[i],
            s_recv.at[i],
            {"tm": seg(d)},
        )
        for i, (d, first, rows, land) in enumerate(SIGNAL_HALO)
    ]
    halo = halo_copies(0)
    for copy in halo + signal_copies:
        copy.start()

    for q in range(3):
        for s in range(16):
            wb[q, s * 128 + CHANS : (s + 1) * 128] = jnp.zeros((128 - CHANS, 256), BF16)
        for j in range(2):
            wat[q, j * 128 + CHANS : (j + 1) * 128] = jnp.zeros((128 - CHANS, 2048), BF16)
    load.wait()
    lane_block = lax.broadcasted_iota(jnp.int32, (CHANS, 128), 1) // BLOCK_ATOMS

    def arrange(i, carry):
        j, q = i // 3, i % 3
        here = pl.multiple_of(j * 128, 128)
        for half in range(2):
            found = [jnp.zeros((CHANS, 128), F32)] * OUTER
            for k in range(8):
                s = half * 8 + k
                value = dt_ref[pl.ds(16 * i + s, CHANS, stride=L), :]
                low = value.astype(BF16)
                wb[q, s * 128 : s * 128 + CHANS, pl.ds(here, 128)] = low
                wat[q, pl.ds(here, CHANS), s * 128 : (s + 1) * 128] = low
                turned = pltpu.roll(value, 16 * k, 1) if k else value
                found = [
                    jnp.where(lane_block == (plan_ref[o] + k) % 8, turned, found[o])
                    for o in range(OUTER)
                ]
            group = pl.ds(pl.multiple_of(i * 256 + half * 128, 128), 128)
            for o in range(OUTER):
                old[o, :, group] = found[o]
        return carry

    lax.fori_loop(0, 6, arrange, 0)

    for copy in halo + signal_copies:
        copy.wait()

    def in_window(a, b):
        when = tm * SEG - OWN + a + lax.broadcasted_iota(jnp.int32, (b - a, 1), 0)
        return when

    def clear_early(o):
        zst[o, 0:OWN] = jnp.where(in_window(0, OWN) >= 0, zst[o, 0:OWN], 0.0)

    def convolve_rows(o, a, b):
        top = a - 80
        for s in range(16):
            zp[top:b, s * 128 : (s + 1) * 128] = zst[o, pl.ds(top - s, b - top), :].astype(BF16)
        total = dot_t(zp[a - 48 : b, :], wat[0])
        total = total + dot_t(zp[a - 64 : b - 16, :], wat[1])
        acc[0 : b - a + 48] = total + dot_t(zp[a - 80 : b - 32, :], wat[2])

    def residual_rows(a, b):
        n = b - a + 48
        made = unit * (acc[48:n, 0:128] + acc[0 : n - 48, 128:256])
        value = sgx[a:b].astype(F32) - made
        rst[a:b] = jnp.where(in_window(a, b) < segments * SEG, value, 0.0)

    def update_rows(o, step, a, b):
        n, i = b - a, o * INNER + step
        half = n // 2
        end = b + 80
        for s in range(16):
            rp[a:end, s * 128 : (s + 1) * 128] = rst[pl.ds(a + s, end - a), :].astype(BF16)
        near, far = [], []
        for part, (first, last) in enumerate(((0, half + 48), (half + 48, n + 48))):
            start, stop = a + first, a + last
            total = dot(rp[start:stop, :], wb[0])
            total = total + dot(rp[start + 16 : stop + 16, :], wb[1])
            acc[first:last] = total + dot(rp[start + 32 : stop + 32, :], wb[2])
            low, high = part * half, (part + 1) * half
            scores = unit * (acc[low:high, 0:128] + acc[low + 48 : high + 48, 128:256])
            sx[low:high] = scores.astype(BF16)
            copy = remote(
                sx.at[pl.ds(low, half)],
                rx1.at[i, pl.ds(low, half)],
                c_send.at[i, 0, part],
                c_recv.at[i, 0, part],
                {"chan": partner},
            )
            copy.start()
            near.append(copy)
        for part in range(2):
            low, high = part * half, (part + 1) * half
            near[part].wait()
            sx2[low:high] = (
                sx[low:high].astype(F32) + rx1[i, pl.ds(low, half)].astype(F32)
            ).astype(BF16)
            copy = remote(
                sx2.at[pl.ds(low, half)],
                rx2.at[i, pl.ds(low, half)],
                c_send.at[i, 1, part],
                c_recv.at[i, 1, part],
                {"chan": opposite},
            )
            copy.start()
            far.append(copy)
        limit = thr_ref[...]
        for part in range(2):
            low, high = part * half, (part + 1) * half
            far[part].wait()
            scores = sx2[low:high].astype(F32) + rx2[i, pl.ds(low, half)].astype(F32)
            stepped = zst[o, a + low : a + high] + code_rate * scores
            value = stepped - jnp.clip(stepped, -limit, limit)
            zst[o, a + low : a + high] = jnp.where(in_window(a + low, a + high) >= 0, value, 0.0)

    def lanes_sum(row):
        total = row[:, 0:128] + row[:, 128:256] + row[:, 256:384]
        total = jnp.broadcast_to(total, (8, 128))
        for shift in (64, 32, 16):
            total = total + pltpu.roll(total, shift, 1)
        return total

    def old_piece(o, piece):
        top, left = piece // 4 * 48, piece % 4 * 384
        return old[o, top : top + 48, left : left + 384]

    def three(row):
        return jnp.concatenate([row[0:1]] * 3, axis=1)

    def renew(o):
        turned = rst[OWN : OWN + SEG].T
        resid_out[...] = turned[0:CHANS]
        for half in range(2):
            lanes = slice(half * 128, half * 128 + 128)
            a16[:, lanes] = dot(
                zp[OWN - 80 : OWN + SEG, half * 1024 : half * 1024 + 1024],
                pick[o],
            ).astype(BF16)
        across_time = turned[0:CHANS].astype(BF16)
        for q in range(6):
            gfull[:, q * 256 : (q + 1) * 256] = dot(
                across_time, a16[80 - 16 * q : 208 - 16 * q, :]
            ).astype(BF16)
        for piece in range(PLANE):
            top, left = piece // 4 * 48, piece % 4 * 384
            gsend[piece] = gfull[top : top + 48, left : left + 384]
        sent = []

        def spread_rows(part, peers, source, target, send, recv):
            rows = pl.ds(part * 16, 16)
            copies = [
                remote(
                    source(d).at[rows],
                    target(d).at[rows],
                    send.at[o, d, part],
                    recv.at[o, d, part],
                    {"tm": peer},
                )
                for d, peer in peers
            ]
            for copy in copies:
                copy.start()
            sent.extend(copies)
            return copies

        plane = [(d, in_plane(d)) for d in range(1, PLANE)]
        levels = [(d, in_depth(d)) for d in range(1, depth)]
        scatter = [
            spread_rows(
                part,
                plane,
                lambda d: gsend.at[(place + d) % PLANE],
                lambda d: grecv.at[o, d],
                p_send,
                p_recv,
            )
            for part in range(3)
        ]
        cover(o)
        across_levels = []
        for part in range(3):
            rows = pl.ds(part * 16, 16)
            total = gsend[place, rows].astype(F32)
            for d, copy in enumerate(scatter[part], 1):
                copy.wait_recv()
                total = total + grecv[o, d, rows].astype(F32)
            zbuf[o, level, rows] = total.astype(BF16)
            slot = lambda d: zbuf.at[o, level]
            across_levels.append(spread_rows(part, levels, slot, slot, z_send, z_recv))
        gather = []
        for part in range(3):
            rows = pl.ds(part * 16, 16)
            for copy in across_levels[part]:
                copy.wait_recv()
            total = zbuf[o, 0, rows].astype(F32)
            for i in range(1, depth):
                total = total + zbuf[o, i, rows].astype(F32)
            agbuf[o, place, rows] = total.astype(BF16)
            slot = lambda d: agbuf.at[o, place]
            gather.append(spread_rows(part, plane, slot, slot, a_send, a_recv))
        for copies in gather:
            for copy in copies:
                copy.wait_recv()

        with_old = jnp.zeros((1, 384), F32)
        old_old = jnp.zeros((1, 384), F32)
        for piece in range(PLANE):
            grad, was = agbuf[o, piece].astype(F32), old_piece(o, piece)
            with_old = with_old + jnp.sum(grad * was, axis=0, keepdims=True)
            old_old = old_old + jnp.sum(was * was, axis=0, keepdims=True)
        with_old, old_old = lanes_sum(with_old), lanes_sum(old_old)
        own_coef = jnp.where(old_old > 0.0, with_old / jnp.maximum(old_old, 1e-30), 0.0)
        left_over = jnp.zeros((1, 384), F32)
        coef = three(own_coef)
        for piece in range(PLANE):
            part = agbuf[o, piece].astype(F32) - coef * old_piece(o, piece)
            left_over = left_over + jnp.sum(part * part, axis=0, keepdims=True)
        left_over = lanes_sum(left_over)
        row = lax.broadcasted_iota(jnp.int32, (8, 128), 0)
        packed = jnp.where(row == 0, with_old, jnp.where(row == 1, old_old, left_over))
        strecv[o, chan] = packed
        copies = [
            remote(
                strecv.at[o, chan],
                strecv.at[o, chan],
                t_send.at[o, d],
                t_recv.at[o, d],
                {"chan": (chan + d) % 4},
            )
            for d in range(1, 4)
        ]
        for copy in copies:
            copy.start()
        for copy in copies:
            copy.wait_recv()
        sent = sent + copies
        parts = [strecv[o, i] for i in range(4)]
        gd = [part[0:1] for part in parts]
        dd = [part[1:2] for part in parts]
        rr = [part[2:3] for part in parts]
        mean_sq = (dd[0] + dd[1] + dd[2] + dd[3]) / ENTRIES + tiny_eps
        along = (gd[0] + gd[1] + gd[2] + gd[3]) / ENTRIES / mean_sq
        spread = jnp.zeros((1, 128), F32)
        for i in range(4):
            mine = jnp.where(dd[i] > 0.0, gd[i] / jnp.maximum(dd[i], 1e-30), 0.0)
            off = mine - along
            spread = spread + rr[i] + off * (off * dd[i] + 2.0 * (gd[i] - mine * dd[i]))
        spread = jnp.maximum(spread, 0.0) / ENTRIES + tiny_eps
        along_row = three(along)
        gain = three(move_rate / jnp.sqrt(spread))
        shrink = three(1.0 / jnp.sqrt(mean_sq + 0.25))
        for piece in range(PLANE):
            was = old_piece(o, piece)
            across = agbuf[o, piece].astype(F32) - along_row * was
            top, left = piece // 4 * 48, piece % 4 * 384
            value = (was + gain * across) * shrink
            new[o, top : top + 48, left : left + 384] = value
            block_low[0, top : top + 48, left : left + 384] = value.astype(BF16)
        for copy in sent:
            copy.wait_send()

    def place_block(o):
        mine = jnp.where(lane_block == plan_ref[o], 1.0, 0.0)
        others = (1.0 - mine).astype(BF16)

        def body(i, carry):
            j, q = i // 3, i % 3
            here = pl.multiple_of(j * 128, 128)
            for half in range(2):
                value = new[o, :, pl.ds(pl.multiple_of(i * 256 + half * 128, 128), 128)]
                for k in range(8):
                    s = half * 8 + k
                    rows = slice(s * 128, s * 128 + CHANS)
                    turned = pltpu.roll(value, 128 - 16 * k, 1) if k else value
                    low = wb[q, rows, pl.ds(here, 128)] * others + (turned * mine).astype(BF16)
                    wb[q, rows, pl.ds(here, 128)] = low
                    wat[q, pl.ds(here, CHANS), s * 128 : (s + 1) * 128] = low
            return carry

        lax.fori_loop(0, 6, body, 0)

    def correct(which, sign):
        total = None
        for q in range(6):
            part = dot_t(
                block_codes[96 - 16 * q : ROWS - 16 * q, :],
                block_low[which, :, q * 256 : (q + 1) * 256],
            )
            total = part if total is None else total + part
        acc[48:560, 0:128] += sign * total

    def write_rows(o):
        rows_out = (rows_first, rows_last)[o]
        block = jnp.zeros((BLOCK_ATOMS, 128), jnp.int32) + plan_ref[o]
        bits = [block // step % 2 == 1 for step in (4, 2, 1)]
        pad = jnp.zeros((128 - CHANS, 128), F32)
        for g in range(12):
            value = new[o, :, g * 128 : (g + 1) * 128]
            by_tap[g * 128 : (g + 1) * 128] = jnp.concatenate([value, pad], axis=0).T
        for g in range(12):
            group = [by_tap[g * 128 + i * 16 : g * 128 + (i + 1) * 16] for i in range(8)]
            for step, moved in zip((4, 2, 1), bits):
                group = [jnp.where(moved, group[(i + step) % 8], group[i]) for i in range(8)]
            for i in range(8):
                in_order[g * 128 + i * 16 : g * 128 + (i + 1) * 16] = group[i]
        for atom in range(BLOCK_ATOMS):
            taps = in_order[pl.ds(atom, L, stride=BLOCK_ATOMS), :]
            turned = jnp.concatenate([taps, pad], axis=0).T
            by_atom[atom * 97 : atom * 97 + CHANS] = turned[0:CHANS]
        lane = lax.broadcasted_iota(jnp.int32, (BLOCK_ATOMS, 128), 1)

        def body(m, carry):
            one = [by_atom[pl.ds(4 * m + r, BLOCK_ATOMS, stride=97), :] for r in range(4)]
            one = [pltpu.roll(part, 96 * r % 128, 1) if r else part for r, part in enumerate(one)]
            for t in range(3):
                lanes = pl.ds(pl.multiple_of(m * 384 + t * 128, 128), 128)
                rows_out[:, lanes] = jnp.where(lane < 96 - 32 * t, one[t], one[t + 1])
            return carry

        lax.fori_loop(0, 24, body, 0)

    def cover(o):
        @pl.when(o < OUTER - 1)
        def _():
            for copy in halo_copies(1):
                copy.wait()
            clear_early(1)
            convolve_rows(1, 96, 608)
            for half in range(2):
                block_codes[16:ROWS, half * 128 : half * 128 + 128] = dot(
                    zp[16:ROWS, half * 1024 : half * 1024 + 1024], pick[0]
                ).astype(BF16)
            block_low[1, 0:CHANS] = old[0].astype(BF16)
            correct(1, -1.0)

        @pl.when(o > 0)
        def _():
            write_rows(0)

    block_low[:, CHANS:128] = jnp.zeros((2, 128 - CHANS, 1536), BF16)
    clear_early(0)
    convolve_rows(0, 96, 608)

    def outer(o, carry):
        residual_rows(96, 608)
        update_rows(o, 0, 96, 512)
        convolve_rows(o, 192, 512)
        residual_rows(192, 512)
        update_rows(o, 1, 192, 416)

        @pl.when(o < OUTER - 1)
        def _():
            zsend[1] = zst[0, OWN : OWN + SEG]
            zst[1, OWN : OWN + SEG] = zst[0, OWN : OWN + SEG]
            for copy in halo_copies(1):
                copy.start()

        convolve_rows(o, 288, 416)
        residual_rows(288, 416)
        renew(o)

        @pl.when(o < OUTER - 1)
        def _():
            correct(0, 1.0)
            place_block(0)

        return carry

    lax.fori_loop(0, OUTER, outer, 0)
    codes_out[...] = zst[OUTER - 1, OWN : OWN + SEG].T
    write_rows(OUTER - 1)


def shards(segments, signal, codes_init, dictionary_init, threshold, plan):
    turned = dictionary_init.T
    depth = segments // PLANE
    vmem = pl.BlockSpec(memory_space=pltpu.VMEM)
    dma = pltpu.SemaphoreType.DMA
    codes, resid, *rows = pl.pallas_call(
        functools.partial(kernel, segments),
        out_shape=(
            jax.ShapeDtypeStruct((K, SEG), F32),
            jax.ShapeDtypeStruct((CHANS, SEG), F32),
        )
        + (jax.ShapeDtypeStruct((BLOCK_ATOMS, CHANS * L), F32),) * OUTER,
        in_specs=[pl.BlockSpec(memory_space=pltpu.SMEM), pl.BlockSpec(memory_space=pl.ANY)]
        + [vmem] * 3,
        out_specs=(vmem,) * 4,
        scratch_shapes=[
            pltpu.VMEM((OUTER, ROWS, 128), F32),
            pltpu.VMEM((OUTER, SEG, 128), F32),
            pltpu.VMEM((ROWS, 128), BF16),
            pltpu.VMEM((SEG, 128), BF16),
            pltpu.VMEM((ROWS, 128), F32),
            pltpu.VMEM((ROWS, 2048), BF16),
            pltpu.VMEM((ROWS, 2048), BF16),
            pltpu.VMEM((3, 2048, 256), BF16),
            pltpu.VMEM((3, 256, 2048), BF16),
            pltpu.VMEM((560, 256), F32),
            pltpu.VMEM((416, 128), BF16),
            pltpu.VMEM((416, 128), BF16),
            pltpu.VMEM((4, 416, 128), BF16),
            pltpu.VMEM((4, 416, 128), BF16),
            pltpu.VMEM((208, 256), BF16),
            pltpu.VMEM((CHANS, 1536), BF16),
            pltpu.VMEM((PLANE, 48, 384), BF16),
            pltpu.VMEM((OUTER, PLANE, 48, 384), BF16),
            pltpu.VMEM((OUTER, depth, 48, 384), BF16),
            pltpu.VMEM((OUTER, PLANE, 48, 384), BF16),
            pltpu.VMEM((OUTER, CHANS, 1536), F32),
            pltpu.VMEM((OUTER, CHANS, 1536), F32),
            pltpu.VMEM((OUTER, 1024, 128), BF16),
            pltpu.VMEM((CHANS * L, K), F32),
            pltpu.VMEM((ROWS, 256), BF16),
            pltpu.VMEM((2, 128, 1536), BF16),
            pltpu.VMEM((1536, 128), F32),
            pltpu.VMEM((1536, 128), F32),
            pltpu.VMEM((16 * 97, 128), F32),
            pltpu.VMEM((OUTER, 4, 8, 128), F32),
            dma((OUTER, 5)),
            dma((OUTER, 5)),
            dma((4,)),
            dma((4,)),
            dma((4, 2, 2)),
            dma((4, 2, 2)),
            dma((OUTER, PLANE, 3)),
            dma((OUTER, PLANE, 3)),
            dma((OUTER, depth, 3)),
            dma((OUTER, depth, 3)),
            dma((OUTER, PLANE, 3)),
            dma((OUTER, PLANE, 3)),
            dma((OUTER, 4)),
            dma((OUTER, 4)),
            dma,
        ],
        compiler_params=pltpu.CompilerParams(
            collective_id=0, has_side_effects=True, vmem_limit_bytes=60 * 1024 * 1024
        ),
    )(plan, turned, codes_init, signal, threshold[None, :])
    dictionary = dictionary_init.reshape(K // BLOCK_ATOMS, BLOCK_ATOMS, CHANS * L)
    block = jnp.arange(K // BLOCK_ATOMS)[:, None, None]
    for o in range(OUTER):
        dictionary = jnp.where(block == plan[o], rows[o], dictionary)
    return codes, dictionary.reshape(K, CHANS * L), resid


def solution(mesh):
    placed = (P("chan", "tm"), P(None, "tm"), P(None, "chan"), P(), P())
    return jax.shard_map(
        functools.partial(shards, mesh.shape["tm"]),
        mesh=mesh,
        in_specs=placed,
        out_specs=(P(None, "tm"), P(None, "chan"), P("chan", "tm")),
        check_vma=False,
    )
```

```python
import functools

import jax
import jax.numpy as jnp
from jax import lax
from jax.experimental import pallas as pl
from jax.experimental.pallas import tpu as pltpu
from jax.sharding import PartitionSpec as P

C = 384
K = 128
L = 96
BLOCK_ATOMS = 16
INNER = 2
OUTER = 2
CHANS = 96
SEG = 128
ENTRIES = C * L

code_rate = 0.3
move_rate = 0.5
tiny_eps = 1e-06

VMEM_LIMIT = 32 * 1024 * 1024
MESH = pl.DeviceIdType.MESH
F32 = jnp.float32
BF16 = jnp.bfloat16

OWN = 288
ROWS = 608
PLANE = 8
HALO = (
    (1, 0, 128, 160),
    (2, 0, 128, 32),
    (3, 96, 32, 0),
    (-1, 0, 128, 416),
    (-2, 0, 64, 544),
)
SIGNAL_HALO = (
    (1, 0, 128, 160),
    (2, 64, 64, 96),
    (-1, 0, 128, 416),
    (-2, 0, 64, 544),
)


def dot(a, b):
    return lax.dot_general(a, b, (((1,), (0,)), ((), ())), preferred_element_type=F32)


def dot_t(a, b):
    return lax.dot_general(a, b, (((1,), (1,)), ((), ())), preferred_element_type=F32)


def kernel(
    segments,
    plan_ref,
    dt_hbm,
    codes_ref,
    signal_ref,
    thr_ref,
    codes_out,
    resid_out,
    rows_first,
    rows_last,
    owner_out,
    zst,
    zsend,
    sgx,
    sgown,
    rst,
    zp,
    rp,
    wb,
    wat,
    acc,
    sx,
    sx2,
    rx1,
    rx2,
    a16,
    gfull,
    gsend,
    grecv,
    zbuf,
    agbuf,
    old,
    new,
    pick,
    dt_ref,
    block_codes,
    block_low,
    by_tap,
    in_order,
    by_atom,
    strecv,
    h_send,
    h_recv,
    s_send,
    s_recv,
    c_send,
    c_recv,
    p_send,
    p_recv,
    z_send,
    z_recv,
    a_send,
    a_recv,
    t_send,
    t_recv,
    load_sem,
):
    unit = ENTRIES ** (-0.5)
    tm = lax.axis_index("tm")
    chan = lax.axis_index("chan")
    depth = segments // PLANE
    place = tm % PLANE
    level = tm // PLANE

    def seg(d):
        return (tm + d + segments) % segments

    def in_plane(d):
        return level * PLANE + (place + d) % PLANE

    def in_depth(d):
        return ((level + d) % depth) * PLANE + place

    partner = chan + 1 - 2 * (chan % 2)
    opposite = (chan + 2) % 4

    load = pltpu.make_async_copy(dt_hbm, dt_ref, load_sem)
    load.start()
    zsend[0] = codes_ref[...].T
    zst[0, OWN : OWN + SEG] = zsend[0]
    low = jnp.concatenate(
        [signal_ref[...].astype(F32), jnp.zeros((SEG - CHANS, SEG), F32)], axis=0
    ).T.astype(BF16)
    sgown[...] = low
    sgx[OWN : OWN + SEG] = low


    def pick_body(o, carry):
        tall = lax.broadcasted_iota(jnp.int32, (1024, 128), 0)
        wide = lax.broadcasted_iota(jnp.int32, (1024, 128), 1)
        block = plan_ref[o]
        hit = ((tall // 128 + block) % 8 == wide // 16) & (
            tall % 128 == wide % 16 + block * BLOCK_ATOMS
        )
        pick[o] = jnp.where(hit, 1.0, 0.0).astype(BF16)
        return carry

    lax.fori_loop(0, OUTER, pick_body, 0)

    barrier = pltpu.get_barrier_semaphore()
    peers = [{"tm": seg(d)} for d in (-3, -2, -1, 1, 2, 3)]
    peers += [{"chan": (chan + d) % 4} for d in range(1, 4)]
    peers += [{"tm": in_plane(d)} for d in range(1, PLANE)]
    peers += [{"tm": in_depth(d)} for d in range(1, depth)]
    for peer in peers:
        pl.semaphore_signal(barrier, inc=1, device_id=peer, device_id_type=MESH)
    pl.semaphore_wait(barrier, len(peers))

    def remote(src, dst, send, recv, peer):
        return pltpu.make_async_remote_copy(
            src_ref=src,
            dst_ref=dst,
            send_sem=send,
            recv_sem=recv,
            device_id=peer,
            device_id_type=MESH,
        )

    def halo_copies(o):
        return [
            remote(
                zsend.at[o, pl.ds(first, rows)],
                zst.at[o, pl.ds(land, rows)],
                h_send.at[o, i],
                h_recv.at[o, i],
                {"tm": seg(d)},
            )
            for i, (d, first, rows, land) in enumerate(HALO)
        ]

    signal_copies = [
        remote(
            sgown.at[pl.ds(first, rows)],
            sgx.at[pl.ds(land, rows)],
            s_send.at[i],
            s_recv.at[i],
            {"tm": seg(d)},
        )
        for i, (d, first, rows, land) in enumerate(SIGNAL_HALO)
    ]
    halo = halo_copies(0)
    for copy in halo + signal_copies:
        copy.start()

    for q in range(3):
        for s in range(16):
            wb[q, s * 128 + CHANS : (s + 1) * 128] = jnp.zeros((128 - CHANS, 256), BF16)
        for j in range(2):
            wat[q, j * 128 + CHANS : (j + 1) * 128] = jnp.zeros((128 - CHANS, 2048), BF16)
    load.wait()
    lane_block = lax.broadcasted_iota(jnp.int32, (CHANS, 128), 1) // BLOCK_ATOMS

    def arrange(i, carry):
        j, q = i // 3, i % 3
        here = pl.multiple_of(j * 128, 128)
        for half in range(2):
            found = [jnp.zeros((CHANS, 128), F32)] * OUTER
            for k in range(8):
                s = half * 8 + k
                value = dt_ref[pl.ds(16 * i + s, CHANS, stride=L), :]
                low = value.astype(BF16)
                wb[q, s * 128 : s * 128 + CHANS, pl.ds(here, 128)] = low
                wat[q, pl.ds(here, CHANS), s * 128 : (s + 1) * 128] = low
                turned = pltpu.roll(value, 16 * k, 1) if k else value
                found = [
                    jnp.where(lane_block == (plan_ref[o] + k) % 8, turned, found[o])
                    for o in range(OUTER)
                ]
            group = pl.ds(pl.multiple_of(i * 256 + half * 128, 128), 128)
            for o in range(OUTER):
                old[o, :, group] = found[o]
        return carry

    lax.fori_loop(0, 6, arrange, 0)

    for copy in halo + signal_copies:
        copy.wait()

    def in_window(a, b):
        when = tm * SEG - OWN + a + lax.broadcasted_iota(jnp.int32, (b - a, 1), 0)
        return when

    def clear_early(o):
        zst[o, 0:OWN] = jnp.where(in_window(0, OWN) >= 0, zst[o, 0:OWN], 0.0)

    def convolve_rows(o, a, b, first, last, lead=0):
        base = a - 48
        top = lead or first - 32
        for s in range(16):
            lanes = slice(s * 128, (s + 1) * 128)
            zp[top:last, lanes] = zst[o, pl.ds(top - s, last - top), :].astype(BF16)
        total = dot_t(zp[first:last, :], wat[0])
        total = total + dot_t(zp[first - 16 : last - 16, :], wat[1])
        acc[first - base : last - base] = total + dot_t(zp[first - 32 : last - 32, :], wat[2])

    def residual_rows(a, b):
        n = b - a + 48
        made = unit * (acc[48:n, 0:128] + acc[0 : n - 48, 128:256])
        value = sgx[a:b].astype(F32) - made
        rst[a:b] = jnp.where(in_window(a, b) < segments * SEG, value, 0.0)

    def update_rows(o, step, a, b, following):
        n, i = b - a, o * INNER + step
        half = n // 2
        end = b + 80
        for s in range(16):
            rp[a:end, s * 128 : (s + 1) * 128] = rst[pl.ds(a + s, end - a), :].astype(BF16)
        near, far = [], []
        for part, (first, last) in enumerate(((0, half + 48), (half + 48, n + 48))):
            start, stop = a + first, a + last
            total = dot(rp[start:stop, :], wb[0])
            total = total + dot(rp[start + 16 : stop + 16, :], wb[1])
            acc[first:last] = total + dot(rp[start + 32 : stop + 32, :], wb[2])
            low, high = part * half, (part + 1) * half
            scores = unit * (acc[low:high, 0:128] + acc[low + 48 : high + 48, 128:256])
            sx[low:high] = scores.astype(BF16)
            copy = remote(
                sx.at[pl.ds(low, half)],
                rx1.at[i, pl.ds(low, half)],
                c_send.at[i, 0, part],
                c_recv.at[i, 0, part],
                {"chan": partner},
            )
            copy.start()
            near.append(copy)
        for part in range(2):
            low, high = part * half, (part + 1) * half
            near[part].wait()
            sx2[low:high] = (
                sx[low:high].astype(F32) + rx1[i, pl.ds(low, half)].astype(F32)
            ).astype(BF16)
            copy = remote(
                sx2.at[pl.ds(low, half)],
                rx2.at[i, pl.ds(low, half)],
                c_send.at[i, 1, part],
                c_recv.at[i, 1, part],
                {"chan": opposite},
            )
            copy.start()
            far.append(copy)
        limit = thr_ref[...]
        for part in range(2):
            low, high = part * half, (part + 1) * half
            far[part].wait()
            scores = sx2[low:high].astype(F32) + rx2[i, pl.ds(low, half)].astype(F32)
            stepped = zst[o, a + low : a + high] + code_rate * scores
            value = stepped - jnp.clip(stepped, -limit, limit)
            zst[o, a + low : a + high] = jnp.where(in_window(a + low, a + high) >= 0, value, 0.0)
            middle, (c, d) = a + half, following
            if part == 0:
                convolve_rows(o, c, d, c - 48, middle)
            else:
                convolve_rows(o, c, d, middle, d, middle)

    def lanes_sum(row):
        total = row[:, 0:128] + row[:, 128:256] + row[:, 256:384]
        total = jnp.broadcast_to(total, (8, 128))
        for shift in (64, 32, 16):
            total = total + pltpu.roll(total, shift, 1)
        return total

    def old_piece(o, piece):
        top, left = piece // 4 * 48, piece % 4 * 384
        return old[o, top : top + 48, left : left + 384]

    def three(row):
        return jnp.concatenate([row[0:1]] * 3, axis=1)

    def renew(o):
        turned = rst[OWN : OWN + SEG].T
        resid_out[...] = turned[0:CHANS]
        for half in range(2):
            lanes = slice(half * 128, half * 128 + 128)
            a16[:, lanes] = dot(
                zp[OWN - 80 : OWN + SEG, half * 1024 : half * 1024 + 1024],
                pick[o],
            ).astype(BF16)
        across_time = turned[0:CHANS].astype(BF16)
        for q in range(6):
            gfull[:, q * 256 : (q + 1) * 256] = dot(
                across_time, a16[80 - 16 * q : 208 - 16 * q, :]
            ).astype(BF16)
        for piece in range(PLANE):
            top, left = piece // 4 * 48, piece % 4 * 384
            gsend[piece] = gfull[top : top + 48, left : left + 384]
        sent = []

        def spread_rows(part, peers, source, target, send, recv):
            rows = pl.ds(part * 16, 16)
            copies = [
                remote(
                    source(d).at[rows],
                    target(d).at[rows],
                    send.at[o, d, part],
                    recv.at[o, d, part],
                    {"tm": peer},
                )
                for d, peer in peers
            ]
            for copy in copies:
                copy.start()
            sent.extend(copies)
            return copies

        plane = [(d, in_plane(d)) for d in range(1, PLANE)]
        levels = [(d, in_depth(d)) for d in range(1, depth)]
        scatter = [
            spread_rows(
                part,
                plane,
                lambda d: gsend.at[(place + d) % PLANE],
                lambda d: grecv.at[o, d],
                p_send,
                p_recv,
            )
            for part in range(3)
        ]
        cover(o)
        across_levels = []
        for part in range(3):
            rows = pl.ds(part * 16, 16)
            total = gsend[place, rows].astype(F32)
            for d, copy in enumerate(scatter[part], 1):
                copy.wait_recv()
                total = total + grecv[o, d, rows].astype(F32)
            zbuf[o, level, rows] = total.astype(BF16)
            slot = lambda d: zbuf.at[o, level]
            across_levels.append(spread_rows(part, levels, slot, slot, z_send, z_recv))
        gather = []
        for part in range(3):
            rows = pl.ds(part * 16, 16)
            for copy in across_levels[part]:
                copy.wait_recv()
            total = zbuf[o, 0, rows].astype(F32)
            for i in range(1, depth):
                total = total + zbuf[o, i, rows].astype(F32)
            agbuf[o, place, rows] = total.astype(BF16)
            slot = lambda d: agbuf.at[o, place]
            gather.append(spread_rows(part, plane, slot, slot, a_send, a_recv))
        for copies in gather:
            for copy in copies:
                copy.wait_recv()

        with_old = jnp.zeros((1, 384), F32)
        old_old = jnp.zeros((1, 384), F32)
        for piece in range(PLANE):
            grad, was = agbuf[o, piece].astype(F32), old_piece(o, piece)
            with_old = with_old + jnp.sum(grad * was, axis=0, keepdims=True)
            old_old = old_old + jnp.sum(was * was, axis=0, keepdims=True)
        with_old, old_old = lanes_sum(with_old), lanes_sum(old_old)
        own_coef = jnp.where(old_old > 0.0, with_old / jnp.maximum(old_old, 1e-30), 0.0)
        left_over = jnp.zeros((1, 384), F32)
        coef = three(own_coef)
        for piece in range(PLANE):
            part = agbuf[o, piece].astype(F32) - coef * old_piece(o, piece)
            left_over = left_over + jnp.sum(part * part, axis=0, keepdims=True)
        left_over = lanes_sum(left_over)
        row = lax.broadcasted_iota(jnp.int32, (8, 128), 0)
        packed = jnp.where(row == 0, with_old, jnp.where(row == 1, old_old, left_over))
        strecv[o, chan] = packed
        copies = [
            remote(
                strecv.at[o, chan],
                strecv.at[o, chan],
                t_send.at[o, d],
                t_recv.at[o, d],
                {"chan": (chan + d) % 4},
            )
            for d in range(1, 4)
        ]
        for copy in copies:
            copy.start()
        for copy in copies:
            copy.wait_recv()
        sent = sent + copies
        parts = [strecv[o, i] for i in range(4)]
        gd = [part[0:1] for part in parts]
        dd = [part[1:2] for part in parts]
        rr = [part[2:3] for part in parts]
        mean_sq = (dd[0] + dd[1] + dd[2] + dd[3]) / ENTRIES + tiny_eps
        along = (gd[0] + gd[1] + gd[2] + gd[3]) / ENTRIES / mean_sq
        spread = jnp.zeros((1, 128), F32)
        for i in range(4):
            mine = jnp.where(dd[i] > 0.0, gd[i] / jnp.maximum(dd[i], 1e-30), 0.0)
            off = mine - along
            spread = spread + rr[i] + off * (off * dd[i] + 2.0 * (gd[i] - mine * dd[i]))
        spread = jnp.maximum(spread, 0.0) / ENTRIES + tiny_eps
        along_row = three(along)
        gain = three(move_rate / jnp.sqrt(spread))
        shrink = three(1.0 / jnp.sqrt(mean_sq + 0.25))
        for piece in range(PLANE):
            was = old_piece(o, piece)
            across = agbuf[o, piece].astype(F32) - along_row * was
            top, left = piece // 4 * 48, piece % 4 * 384
            value = (was + gain * across) * shrink
            new[o, top : top + 48, left : left + 384] = value
            block_low[0, top : top + 48, left : left + 384] = value.astype(BF16)
        for copy in sent:
            copy.wait_send()

    def place_block(o):
        mine = jnp.where(lane_block == plan_ref[o], 1.0, 0.0)
        others = (1.0 - mine).astype(BF16)

        def body(i, carry):
            j, q = i // 3, i % 3
            here = pl.multiple_of(j * 128, 128)
            for half in range(2):
                value = new[o, :, pl.ds(pl.multiple_of(i * 256 + half * 128, 128), 128)]
                for k in range(8):
                    s = half * 8 + k
                    rows = slice(s * 128, s * 128 + CHANS)
                    turned = pltpu.roll(value, 128 - 16 * k, 1) if k else value
                    low = wb[q, rows, pl.ds(here, 128)] * others + (turned * mine).astype(BF16)
                    wb[q, rows, pl.ds(here, 128)] = low
                    wat[q, pl.ds(here, CHANS), s * 128 : (s + 1) * 128] = low
            return carry

        lax.fori_loop(0, 6, body, 0)

    def correct(which, sign):
        total = None
        for q in range(6):
            part = dot_t(
                block_codes[96 - 16 * q : ROWS - 16 * q, :],
                block_low[which, :, q * 256 : (q + 1) * 256],
            )
            total = part if total is None else total + part
        acc[48:560, 0:128] += sign * total

    def write_rows(o):
        rows_out = (rows_first, rows_last)[o]
        block = jnp.zeros((BLOCK_ATOMS, 128), jnp.int32) + plan_ref[o]
        bits = [block // step % 2 == 1 for step in (4, 2, 1)]
        pad = jnp.zeros((128 - CHANS, 128), F32)
        for g in range(12):
            value = new[o, :, g * 128 : (g + 1) * 128]
            by_tap[g * 128 : (g + 1) * 128] = jnp.concatenate([value, pad], axis=0).T
        for g in range(12):
            group = [by_tap[g * 128 + i * 16 : g * 128 + (i + 1) * 16] for i in range(8)]
            for step, moved in zip((4, 2, 1), bits):
                group = [jnp.where(moved, group[(i + step) % 8], group[i]) for i in range(8)]
            for i in range(8):
                in_order[g * 128 + i * 16 : g * 128 + (i + 1) * 16] = group[i]
        for atom in range(BLOCK_ATOMS):
            taps = in_order[pl.ds(atom, L, stride=BLOCK_ATOMS), :]
            turned = jnp.concatenate([taps, pad], axis=0).T
            by_atom[atom * 97 : atom * 97 + CHANS] = turned[0:CHANS]
        lane = lax.broadcasted_iota(jnp.int32, (BLOCK_ATOMS, 128), 1)

        def body(m, carry):
            one = [by_atom[pl.ds(4 * m + r, BLOCK_ATOMS, stride=97), :] for r in range(4)]
            one = [pltpu.roll(part, 96 * r % 128, 1) if r else part for r, part in enumerate(one)]
            for t in range(3):
                lanes = pl.ds(pl.multiple_of(m * 384 + t * 128, 128), 128)
                rows_out[:, lanes] = jnp.where(lane < 96 - 32 * t, one[t], one[t + 1])
            return carry

        lax.fori_loop(0, 24, body, 0)

    def cover(o):
        @pl.when(o < OUTER - 1)
        def _():
            for copy in halo_copies(1):
                copy.wait()
            clear_early(1)
            convolve_rows(1, 96, 608, 48, 608)
            for half in range(2):
                block_codes[16:ROWS, half * 128 : half * 128 + 128] = dot(
                    zp[16:ROWS, half * 1024 : half * 1024 + 1024], pick[0]
                ).astype(BF16)
            block_low[1, 0:CHANS] = old[0].astype(BF16)
            correct(1, -1.0)

        @pl.when(o > 0)
        def _():
            write_rows(0)

    block_low[:, CHANS:128] = jnp.zeros((2, 128 - CHANS, 1536), BF16)
    clear_early(0)
    convolve_rows(0, 96, 608, 48, 608)

    def outer(o, carry):
        residual_rows(96, 608)
        update_rows(o, 0, 96, 512, (192, 512))
        residual_rows(192, 512)
        update_rows(o, 1, 192, 416, (288, 416))

        @pl.when(o < OUTER - 1)
        def _():
            zsend[1] = zst[0, OWN : OWN + SEG]
            zst[1, OWN : OWN + SEG] = zst[0, OWN : OWN + SEG]
            for copy in halo_copies(1):
                copy.start()

        residual_rows(288, 416)
        renew(o)

        @pl.when(o < OUTER - 1)
        def _():
            correct(0, 1.0)
            place_block(0)

        return carry

    lax.fori_loop(0, OUTER, outer, 0)
    atom_block = lax.broadcasted_iota(jnp.int32, (K, 128), 0) // BLOCK_ATOMS
    owner_out[...] = jnp.where(atom_block == plan_ref[0], 1, 0) + jnp.where(
        atom_block == plan_ref[1], 2, 0
    )
    codes_out[...] = zst[OUTER - 1, OWN : OWN + SEG].T
    write_rows(OUTER - 1)


def shards(segments, signal, codes_init, dictionary_init, threshold, plan):
    turned = dictionary_init.T
    depth = segments // PLANE
    vmem = pl.BlockSpec(memory_space=pltpu.VMEM)
    dma = pltpu.SemaphoreType.DMA
    codes, resid, first, last, owner = pl.pallas_call(
        functools.partial(kernel, segments),
        out_shape=(
            jax.ShapeDtypeStruct((K, SEG), F32),
            jax.ShapeDtypeStruct((CHANS, SEG), F32),
        )
        + (jax.ShapeDtypeStruct((BLOCK_ATOMS, CHANS * L), F32),) * OUTER
        + (jax.ShapeDtypeStruct((K, 128), jnp.int32),),
        in_specs=[pl.BlockSpec(memory_space=pltpu.SMEM), pl.BlockSpec(memory_space=pl.ANY)]
        + [vmem] * 3,
        out_specs=(vmem,) * 5,
        scratch_shapes=[
            pltpu.VMEM((OUTER, ROWS, 128), F32),
            pltpu.VMEM((OUTER, SEG, 128), F32),
            pltpu.VMEM((ROWS, 128), BF16),
            pltpu.VMEM((SEG, 128), BF16),
            pltpu.VMEM((ROWS, 128), F32),
            pltpu.VMEM((ROWS, 2048), BF16),
            pltpu.VMEM((ROWS, 2048), BF16),
            pltpu.VMEM((3, 2048, 256), BF16),
            pltpu.VMEM((3, 256, 2048), BF16),
            pltpu.VMEM((560, 256), F32),
            pltpu.VMEM((416, 128), BF16),
            pltpu.VMEM((416, 128), BF16),
            pltpu.VMEM((4, 416, 128), BF16),
            pltpu.VMEM((4, 416, 128), BF16),
            pltpu.VMEM((208, 256), BF16),
            pltpu.VMEM((CHANS, 1536), BF16),
            pltpu.VMEM((PLANE, 48, 384), BF16),
            pltpu.VMEM((OUTER, PLANE, 48, 384), BF16),
            pltpu.VMEM((OUTER, depth, 48, 384), BF16),
            pltpu.VMEM((OUTER, PLANE, 48, 384), BF16),
            pltpu.VMEM((OUTER, CHANS, 1536), F32),
            pltpu.VMEM((OUTER, CHANS, 1536), F32),
            pltpu.VMEM((OUTER, 1024, 128), BF16),
            pltpu.VMEM((CHANS * L, K), F32),
            pltpu.VMEM((ROWS, 256), BF16),
            pltpu.VMEM((2, 128, 1536), BF16),
            pltpu.VMEM((1536, 128), F32),
            pltpu.VMEM((1536, 128), F32),
            pltpu.VMEM((16 * 97, 128), F32),
            pltpu.VMEM((OUTER, 4, 8, 128), F32),
            dma((OUTER, 5)),
            dma((OUTER, 5)),
            dma((4,)),
            dma((4,)),
            dma((4, 2, 2)),
            dma((4, 2, 2)),
            dma((OUTER, PLANE, 3)),
            dma((OUTER, PLANE, 3)),
            dma((OUTER, depth, 3)),
            dma((OUTER, depth, 3)),
            dma((OUTER, PLANE, 3)),
            dma((OUTER, PLANE, 3)),
            dma((OUTER, 4)),
            dma((OUTER, 4)),
            dma,
        ],
        compiler_params=pltpu.CompilerParams(
            collective_id=0, has_side_effects=True, vmem_limit_bytes=VMEM_LIMIT
        ),
    )(plan, turned, codes_init, signal, threshold[None, :])
    owner = owner[:, :1]
    first, last = (jnp.tile(rows, (K // BLOCK_ATOMS, 1)) for rows in (first, last))
    dictionary = jnp.where(owner == 1, first, jnp.where(owner == 2, last, dictionary_init))
    return codes, dictionary, resid


def solution(mesh):
    placed = (P("chan", "tm"), P(None, "tm"), P(None, "chan"), P(), P())
    return jax.shard_map(
        functools.partial(shards, mesh.shape["tm"]),
        mesh=mesh,
        in_specs=placed,
        out_specs=(P(None, "tm"), P(None, "chan"), P("chan", "tm")),
        check_vma=False,
    )
```

```python
import functools

import jax
import jax.numpy as jnp
from jax import lax
from jax.experimental import pallas as pl
from jax.experimental.pallas import tpu as pltpu
from jax.sharding import PartitionSpec as P

C = 384
K = 128
L = 96
BLOCK_ATOMS = 16
INNER = 2
OUTER = 2
CHANS = 96
SEG = 128
ENTRIES = C * L

code_rate = 0.3
move_rate = 0.5
tiny_eps = 1e-06

VMEM_LIMIT = 32 * 1024 * 1024
MESH = pl.DeviceIdType.MESH
F32 = jnp.float32
BF16 = jnp.bfloat16

OWN = 288
ROWS = 608
PLANE = 8
HALO = (
    (1, 0, 128, 160),
    (2, 0, 128, 32),
    (3, 96, 32, 0),
    (-1, 0, 128, 416),
    (-2, 0, 64, 544),
)
SIGNAL_HALO = (
    (1, 0, 128, 160),
    (2, 64, 64, 96),
    (-1, 0, 128, 416),
    (-2, 0, 64, 544),
)


def dot(a, b):
    return lax.dot_general(a, b, (((1,), (0,)), ((), ())), preferred_element_type=F32)


def dot_t(a, b):
    return lax.dot_general(a, b, (((1,), (1,)), ((), ())), preferred_element_type=F32)


def kernel(
    segments,
    plan_ref,
    dict_ref,
    codes_ref,
    signal_ref,
    thr_ref,
    codes_out,
    resid_out,
    rows_first,
    rows_last,
    owner_out,
    zst,
    zsend,
    sgx,
    sgown,
    rst,
    zp,
    rp,
    wb,
    wat,
    acc,
    sx,
    sx2,
    rx1,
    rx2,
    a16,
    gfull,
    gsend,
    grecv,
    zbuf,
    agbuf,
    old,
    new,
    pick,
    dt_ref,
    block_codes,
    block_low,
    by_tap,
    in_order,
    by_atom,
    strecv,
    h_send,
    h_recv,
    s_send,
    s_recv,
    c_send,
    c_recv,
    p_send,
    p_recv,
    z_send,
    z_recv,
    a_send,
    a_recv,
    t_send,
    t_recv,
):
    unit = ENTRIES ** (-0.5)
    tm = lax.axis_index("tm")
    chan = lax.axis_index("chan")
    depth = segments // PLANE
    place = tm % PLANE
    level = tm // PLANE

    def seg(d):
        return (tm + d + segments) % segments

    def in_plane(d):
        return level * PLANE + (place + d) % PLANE

    def in_depth(d):
        return ((level + d) % depth) * PLANE + place

    partner = chan + 1 - 2 * (chan % 2)
    opposite = (chan + 2) % 4

    zsend[0] = codes_ref[...].T
    zst[0, OWN : OWN + SEG] = zsend[0]
    low = jnp.concatenate(
        [signal_ref[...].astype(F32), jnp.zeros((SEG - CHANS, SEG), F32)], axis=0
    ).T.astype(BF16)
    sgown[...] = low
    sgx[OWN : OWN + SEG] = low


    barrier = pltpu.get_barrier_semaphore()
    peers = [{"tm": seg(d)} for d in (-3, -2, -1, 1, 2, 3)]
    peers += [{"chan": (chan + d) % 4} for d in range(1, 4)]
    peers += [{"tm": in_plane(d)} for d in range(1, PLANE)]
    peers += [{"tm": in_depth(d)} for d in range(1, depth)]
    for peer in peers:
        pl.semaphore_signal(barrier, inc=1, device_id=peer, device_id_type=MESH)
    def pick_body(o, carry):
        tall = lax.broadcasted_iota(jnp.int32, (1024, 128), 0)
        wide = lax.broadcasted_iota(jnp.int32, (1024, 128), 1)
        block = plan_ref[o]
        hit = ((tall // 128 + block) % 8 == wide // 16) & (
            tall % 128 == wide % 16 + block * BLOCK_ATOMS
        )
        pick[o] = jnp.where(hit, 1.0, 0.0).astype(BF16)
        return carry

    lax.fori_loop(0, OUTER, pick_body, 0)

    for m in range(CHANS // 4):
        tiles = [dict_ref[:, m * 384 + t * 128 : m * 384 + t * 128 + 128].T for t in range(3)]
        turned = jnp.concatenate(tiles, axis=0)
        for r in range(4):
            row = (4 * m + r) * 97
            dt_ref[row : row + L] = turned[r * L : (r + 1) * L]

    pl.semaphore_wait(barrier, len(peers))

    def remote(src, dst, send, recv, peer):
        return pltpu.make_async_remote_copy(
            src_ref=src,
            dst_ref=dst,
            send_sem=send,
            recv_sem=recv,
            device_id=peer,
            device_id_type=MESH,
        )

    def halo_copies(o):
        return [
            remote(
                zsend.at[o, pl.ds(first, rows)],
                zst.at[o, pl.ds(land, rows)],
                h_send.at[o, i],
                h_recv.at[o, i],
                {"tm": seg(d)},
            )
            for i, (d, first, rows, land) in enumerate(HALO)
        ]

    signal_copies = [
        remote(
            sgown.at[pl.ds(first, rows)],
            sgx.at[pl.ds(land, rows)],
            s_send.at[i],
            s_recv.at[i],
            {"tm": seg(d)},
        )
        for i, (d, first, rows, land) in enumerate(SIGNAL_HALO)
    ]
    halo = halo_copies(0)
    for copy in halo + signal_copies:
        copy.start()

    for q in range(3):
        for s in range(16):
            wb[q, s * 128 + CHANS : (s + 1) * 128] = jnp.zeros((128 - CHANS, 256), BF16)
        for j in range(2):
            wat[q, j * 128 + CHANS : (j + 1) * 128] = jnp.zeros((128 - CHANS, 2048), BF16)
    lane_block = lax.broadcasted_iota(jnp.int32, (CHANS, 128), 1) // BLOCK_ATOMS

    def arrange(i, carry):
        j, q = i // 3, i % 3
        here = pl.multiple_of(j * 128, 128)
        for half in range(2):
            found = [jnp.zeros((CHANS, 128), F32)] * OUTER
            for k in range(8):
                s = half * 8 + k
                value = dt_ref[pl.ds(16 * i + s, CHANS, stride=97), :]
                low = value.astype(BF16)
                wb[q, s * 128 : s * 128 + CHANS, pl.ds(here, 128)] = low
                wat[q, pl.ds(here, CHANS), s * 128 : (s + 1) * 128] = low
                turned = pltpu.roll(value, 16 * k, 1) if k else value
                found = [
                    jnp.where(lane_block == (plan_ref[o] + k) % 8, turned, found[o])
                    for o in range(OUTER)
                ]
            group = pl.ds(pl.multiple_of(i * 256 + half * 128, 128), 128)
            for o in range(OUTER):
                old[o, :, group] = found[o]
        return carry

    lax.fori_loop(0, 6, arrange, 0)

    for copy in halo + signal_copies:
        copy.wait()

    def in_window(a, b):
        when = tm * SEG - OWN + a + lax.broadcasted_iota(jnp.int32, (b - a, 1), 0)
        return when

    def clear_early(o):
        zst[o, 0:OWN] = jnp.where(in_window(0, OWN) >= 0, zst[o, 0:OWN], 0.0)

    def convolve_rows(o, a, b):
        top = a - 80
        for s in range(16):
            zp[top:b, s * 128 : (s + 1) * 128] = zst[o, pl.ds(top - s, b - top), :].astype(BF16)
        total = dot_t(zp[a - 48 : b, :], wat[0])
        total = total + dot_t(zp[a - 64 : b - 16, :], wat[1])
        acc[0 : b - a + 48] = total + dot_t(zp[a - 80 : b - 32, :], wat[2])

    def residual_rows(a, b):
        n = b - a + 48
        made = unit * (acc[48:n, 0:128] + acc[0 : n - 48, 128:256])
        value = sgx[a:b].astype(F32) - made
        rst[a:b] = jnp.where(in_window(a, b) < segments * SEG, value, 0.0)

    def update_rows(o, step, a, b):
        n, i = b - a, o * INNER + step
        half = n // 2
        end = b + 80
        for s in range(16):
            rp[a:end, s * 128 : (s + 1) * 128] = rst[pl.ds(a + s, end - a), :].astype(BF16)
        near, far = [], []
        for part, (first, last) in enumerate(((0, half + 48), (half + 48, n + 48))):
            start, stop = a + first, a + last
            total = dot(rp[start:stop, :], wb[0])
            total = total + dot(rp[start + 16 : stop + 16, :], wb[1])
            acc[first:last] = total + dot(rp[start + 32 : stop + 32, :], wb[2])
            low, high = part * half, (part + 1) * half
            scores = unit * (acc[low:high, 0:128] + acc[low + 48 : high + 48, 128:256])
            sx[low:high] = scores.astype(BF16)
            copy = remote(
                sx.at[pl.ds(low, half)],
                rx1.at[i, pl.ds(low, half)],
                c_send.at[i, 0, part],
                c_recv.at[i, 0, part],
                {"chan": partner},
            )
            copy.start()
            near.append(copy)
        for part in range(2):
            low, high = part * half, (part + 1) * half
            near[part].wait()
            sx2[low:high] = (
                sx[low:high].astype(F32) + rx1[i, pl.ds(low, half)].astype(F32)
            ).astype(BF16)
            copy = remote(
                sx2.at[pl.ds(low, half)],
                rx2.at[i, pl.ds(low, half)],
                c_send.at[i, 1, part],
                c_recv.at[i, 1, part],
                {"chan": opposite},
            )
            copy.start()
            far.append(copy)
        limit = thr_ref[...]
        for part in range(2):
            low, high = part * half, (part + 1) * half
            far[part].wait()
            scores = sx2[low:high].astype(F32) + rx2[i, pl.ds(low, half)].astype(F32)
            stepped = zst[o, a + low : a + high] + code_rate * scores
            value = stepped - jnp.clip(stepped, -limit, limit)
            zst[o, a + low : a + high] = jnp.where(in_window(a + low, a + high) >= 0, value, 0.0)

    def lanes_sum(row):
        total = row[:, 0:128] + row[:, 128:256] + row[:, 256:384]
        total = jnp.broadcast_to(total, (8, 128))
        for shift in (64, 32, 16):
            total = total + pltpu.roll(total, shift, 1)
        return total

    def old_piece(o, piece):
        top, left = piece // 4 * 48, piece % 4 * 384
        return old[o, top : top + 48, left : left + 384]

    def three(row):
        return jnp.concatenate([row[0:1]] * 3, axis=1)

    def renew(o):
        turned = rst[OWN : OWN + SEG].T
        resid_out[...] = turned[0:CHANS]
        for half in range(2):
            lanes = slice(half * 128, half * 128 + 128)
            a16[:, lanes] = dot(
                zp[OWN - 80 : OWN + SEG, half * 1024 : half * 1024 + 1024],
                pick[o],
            ).astype(BF16)
        across_time = turned[0:CHANS].astype(BF16)
        for q in range(6):
            gfull[:, q * 256 : (q + 1) * 256] = dot(
                across_time, a16[80 - 16 * q : 208 - 16 * q, :]
            ).astype(BF16)
        for piece in range(PLANE):
            top, left = piece // 4 * 48, piece % 4 * 384
            gsend[piece] = gfull[top : top + 48, left : left + 384]
        sent = []

        def spread_rows(part, peers, source, target, send, recv):
            rows = pl.ds(part * 16, 16)
            copies = [
                remote(
                    source(d).at[rows],
                    target(d).at[rows],
                    send.at[o, d, part],
                    recv.at[o, d, part],
                    {"tm": peer},
                )
                for d, peer in peers
            ]
            for copy in copies:
                copy.start()
            sent.extend(copies)
            return copies

        plane = [(d, in_plane(d)) for d in range(1, PLANE)]
        levels = [(d, in_depth(d)) for d in range(1, depth)]
        scatter = [
            spread_rows(
                part,
                plane,
                lambda d: gsend.at[(place + d) % PLANE],
                lambda d: grecv.at[o, d],
                p_send,
                p_recv,
            )
            for part in range(3)
        ]
        cover(o)
        across_levels = []
        for part in range(3):
            rows = pl.ds(part * 16, 16)
            total = gsend[place, rows].astype(F32)
            for d, copy in enumerate(scatter[part], 1):
                copy.wait_recv()
                total = total + grecv[o, d, rows].astype(F32)
            zbuf[o, level, rows] = total.astype(BF16)
            slot = lambda d: zbuf.at[o, level]
            across_levels.append(spread_rows(part, levels, slot, slot, z_send, z_recv))
        gather = []
        for part in range(3):
            rows = pl.ds(part * 16, 16)
            for copy in across_levels[part]:
                copy.wait_recv()
            total = zbuf[o, 0, rows].astype(F32)
            for i in range(1, depth):
                total = total + zbuf[o, i, rows].astype(F32)
            agbuf[o, place, rows] = total.astype(BF16)
            slot = lambda d: agbuf.at[o, place]
            gather.append(spread_rows(part, plane, slot, slot, a_send, a_recv))
        for copies in gather:
            for copy in copies:
                copy.wait_recv()

        with_old = jnp.zeros((1, 384), F32)
        old_old = jnp.zeros((1, 384), F32)
        for piece in range(PLANE):
            grad, was = agbuf[o, piece].astype(F32), old_piece(o, piece)
            with_old = with_old + jnp.sum(grad * was, axis=0, keepdims=True)
            old_old = old_old + jnp.sum(was * was, axis=0, keepdims=True)
        with_old, old_old = lanes_sum(with_old), lanes_sum(old_old)
        own_coef = jnp.where(old_old > 0.0, with_old / jnp.maximum(old_old, 1e-30), 0.0)
        left_over = jnp.zeros((1, 384), F32)
        coef = three(own_coef)
        for piece in range(PLANE):
            part = agbuf[o, piece].astype(F32) - coef * old_piece(o, piece)
            left_over = left_over + jnp.sum(part * part, axis=0, keepdims=True)
        left_over = lanes_sum(left_over)
        row = lax.broadcasted_iota(jnp.int32, (8, 128), 0)
        packed = jnp.where(row == 0, with_old, jnp.where(row == 1, old_old, left_over))
        strecv[o, chan] = packed
        copies = [
            remote(
                strecv.at[o, chan],
                strecv.at[o, chan],
                t_send.at[o, d],
                t_recv.at[o, d],
                {"chan": (chan + d) % 4},
            )
            for d in range(1, 4)
        ]
        for copy in copies:
            copy.start()
        for copy in copies:
            copy.wait_recv()
        sent = sent + copies
        parts = [strecv[o, i] for i in range(4)]
        gd = [part[0:1] for part in parts]
        dd = [part[1:2] for part in parts]
        rr = [part[2:3] for part in parts]
        mean_sq = (dd[0] + dd[1] + dd[2] + dd[3]) / ENTRIES + tiny_eps
        along = (gd[0] + gd[1] + gd[2] + gd[3]) / ENTRIES / mean_sq
        spread = jnp.zeros((1, 128), F32)
        for i in range(4):
            mine = jnp.where(dd[i] > 0.0, gd[i] / jnp.maximum(dd[i], 1e-30), 0.0)
            off = mine - along
            spread = spread + rr[i] + off * (off * dd[i] + 2.0 * (gd[i] - mine * dd[i]))
        spread = jnp.maximum(spread, 0.0) / ENTRIES + tiny_eps
        along_row = three(along)
        gain = three(move_rate / jnp.sqrt(spread))
        shrink = three(1.0 / jnp.sqrt(mean_sq + 0.25))
        for piece in range(PLANE):
            was = old_piece(o, piece)
            across = agbuf[o, piece].astype(F32) - along_row * was
            top, left = piece // 4 * 48, piece % 4 * 384
            value = (was + gain * across) * shrink
            new[o, top : top + 48, left : left + 384] = value
            block_low[0, top : top + 48, left : left + 384] = value.astype(BF16)
        for copy in sent:
            copy.wait_send()

    def place_block(o):
        mine = jnp.where(lane_block == plan_ref[o], 1.0, 0.0)
        others = (1.0 - mine).astype(BF16)

        def body(i, carry):
            j, q = i // 3, i % 3
            here = pl.multiple_of(j * 128, 128)
            for half in range(2):
                value = new[o, :, pl.ds(pl.multiple_of(i * 256 + half * 128, 128), 128)]
                for k in range(8):
                    s = half * 8 + k
                    rows = slice(s * 128, s * 128 + CHANS)
                    turned = pltpu.roll(value, 128 - 16 * k, 1) if k else value
                    low = wb[q, rows, pl.ds(here, 128)] * others + (turned * mine).astype(BF16)
                    wb[q, rows, pl.ds(here, 128)] = low
                    wat[q, pl.ds(here, CHANS), s * 128 : (s + 1) * 128] = low
            return carry

        lax.fori_loop(0, 6, body, 0)

    def correct(which, sign):
        total = None
        for q in range(6):
            part = dot_t(
                block_codes[96 - 16 * q : ROWS - 16 * q, :],
                block_low[which, :, q * 256 : (q + 1) * 256],
            )
            total = part if total is None else total + part
        acc[48:560, 0:128] += sign * total

    def write_rows(o):
        rows_out = (rows_first, rows_last)[o]
        block = jnp.zeros((BLOCK_ATOMS, 128), jnp.int32) + plan_ref[o]
        bits = [block // step % 2 == 1 for step in (4, 2, 1)]
        pad = jnp.zeros((128 - CHANS, 128), F32)
        for g in range(12):
            value = new[o, :, g * 128 : (g + 1) * 128]
            by_tap[g * 128 : (g + 1) * 128] = jnp.concatenate([value, pad], axis=0).T
        for g in range(12):
            group = [by_tap[g * 128 + i * 16 : g * 128 + (i + 1) * 16] for i in range(8)]
            for step, moved in zip((4, 2, 1), bits):
                group = [jnp.where(moved, group[(i + step) % 8], group[i]) for i in range(8)]
            for i in range(8):
                in_order[g * 128 + i * 16 : g * 128 + (i + 1) * 16] = group[i]
        for atom in range(BLOCK_ATOMS):
            taps = in_order[pl.ds(atom, L, stride=BLOCK_ATOMS), :]
            turned = jnp.concatenate([taps, pad], axis=0).T
            by_atom[atom * 97 : atom * 97 + CHANS] = turned[0:CHANS]
        lane = lax.broadcasted_iota(jnp.int32, (BLOCK_ATOMS, 128), 1)

        def body(m, carry):
            one = [by_atom[pl.ds(4 * m + r, BLOCK_ATOMS, stride=97), :] for r in range(4)]
            one = [pltpu.roll(part, 96 * r % 128, 1) if r else part for r, part in enumerate(one)]
            for t in range(3):
                lanes = pl.ds(pl.multiple_of(m * 384 + t * 128, 128), 128)
                rows_out[:, lanes] = jnp.where(lane < 96 - 32 * t, one[t], one[t + 1])
            return carry

        lax.fori_loop(0, 24, body, 0)

    def cover(o):
        @pl.when(o < OUTER - 1)
        def _():
            for copy in halo_copies(1):
                copy.wait()
            clear_early(1)
            convolve_rows(1, 96, 608)
            for half in range(2):
                block_codes[16:ROWS, half * 128 : half * 128 + 128] = dot(
                    zp[16:ROWS, half * 1024 : half * 1024 + 1024], pick[0]
                ).astype(BF16)
            block_low[1, 0:CHANS] = old[0].astype(BF16)
            correct(1, -1.0)

        @pl.when(o > 0)
        def _():
            write_rows(0)

    block_low[:, CHANS:128] = jnp.zeros((2, 128 - CHANS, 1536), BF16)
    clear_early(0)
    convolve_rows(0, 96, 608)

    def outer(o, carry):
        residual_rows(96, 608)
        update_rows(o, 0, 96, 512)
        convolve_rows(o, 192, 512)
        residual_rows(192, 512)
        update_rows(o, 1, 192, 416)

        @pl.when(o < OUTER - 1)
        def _():
            zsend[1] = zst[0, OWN : OWN + SEG]
            zst[1, OWN : OWN + SEG] = zst[0, OWN : OWN + SEG]
            for copy in halo_copies(1):
                copy.start()

        convolve_rows(o, 288, 416)
        residual_rows(288, 416)
        renew(o)

        @pl.when(o < OUTER - 1)
        def _():
            correct(0, 1.0)
            place_block(0)

        return carry

    lax.fori_loop(0, OUTER, outer, 0)
    atom_block = lax.broadcasted_iota(jnp.int32, (K, 128), 0) // BLOCK_ATOMS
    owner_out[...] = jnp.where(atom_block == plan_ref[0], 1, 0) + jnp.where(
        atom_block == plan_ref[1], 2, 0
    )
    codes_out[...] = zst[OUTER - 1, OWN : OWN + SEG].T
    write_rows(OUTER - 1)


def shards(segments, signal, codes_init, dictionary_init, threshold, plan):
    depth = segments // PLANE
    vmem = pl.BlockSpec(memory_space=pltpu.VMEM)
    dma = pltpu.SemaphoreType.DMA
    codes, resid, first, last, owner = pl.pallas_call(
        functools.partial(kernel, segments),
        out_shape=(
            jax.ShapeDtypeStruct((K, SEG), F32),
            jax.ShapeDtypeStruct((CHANS, SEG), F32),
        )
        + (jax.ShapeDtypeStruct((BLOCK_ATOMS, CHANS * L), F32),) * OUTER
        + (jax.ShapeDtypeStruct((K, 128), jnp.int32),),
        in_specs=[pl.BlockSpec(memory_space=pltpu.SMEM)] + [vmem] * 4,
        out_specs=(vmem,) * 5,
        scratch_shapes=[
            pltpu.VMEM((OUTER, ROWS, 128), F32),
            pltpu.VMEM((OUTER, SEG, 128), F32),
            pltpu.VMEM((ROWS, 128), BF16),
            pltpu.VMEM((SEG, 128), BF16),
            pltpu.VMEM((ROWS, 128), F32),
            pltpu.VMEM((ROWS, 2048), BF16),
            pltpu.VMEM((ROWS, 2048), BF16),
            pltpu.VMEM((3, 2048, 256), BF16),
            pltpu.VMEM((3, 256, 2048), BF16),
            pltpu.VMEM((560, 256), F32),
            pltpu.VMEM((416, 128), BF16),
            pltpu.VMEM((416, 128), BF16),
            pltpu.VMEM((4, 416, 128), BF16),
            pltpu.VMEM((4, 416, 128), BF16),
            pltpu.VMEM((208, 256), BF16),
            pltpu.VMEM((CHANS, 1536), BF16),
            pltpu.VMEM((PLANE, 48, 384), BF16),
            pltpu.VMEM((OUTER, PLANE, 48, 384), BF16),
            pltpu.VMEM((OUTER, depth, 48, 384), BF16),
            pltpu.VMEM((OUTER, PLANE, 48, 384), BF16),
            pltpu.VMEM((OUTER, CHANS, 1536), F32),
            pltpu.VMEM((OUTER, CHANS, 1536), F32),
            pltpu.VMEM((OUTER, 1024, 128), BF16),
            pltpu.VMEM((CHANS * 97, K), F32),
            pltpu.VMEM((ROWS, 256), BF16),
            pltpu.VMEM((2, 128, 1536), BF16),
            pltpu.VMEM((1536, 128), F32),
            pltpu.VMEM((1536, 128), F32),
            pltpu.VMEM((16 * 97, 128), F32),
            pltpu.VMEM((OUTER, 4, 8, 128), F32),
            dma((OUTER, 5)),
            dma((OUTER, 5)),
            dma((4,)),
            dma((4,)),
            dma((4, 2, 2)),
            dma((4, 2, 2)),
            dma((OUTER, PLANE, 3)),
            dma((OUTER, PLANE, 3)),
            dma((OUTER, depth, 3)),
            dma((OUTER, depth, 3)),
            dma((OUTER, PLANE, 3)),
            dma((OUTER, PLANE, 3)),
            dma((OUTER, 4)),
            dma((OUTER, 4)),
        ],
        compiler_params=pltpu.CompilerParams(
            collective_id=0, has_side_effects=True, vmem_limit_bytes=VMEM_LIMIT
        ),
    )(plan, dictionary_init, codes_init, signal, threshold[None, :])
    owner = owner[:, :1]
    first, last = (jnp.tile(rows, (K // BLOCK_ATOMS, 1)) for rows in (first, last))
    dictionary = jnp.where(owner == 1, first, jnp.where(owner == 2, last, dictionary_init))
    return codes, dictionary, resid


def solution(mesh):
    placed = (P("chan", "tm"), P(None, "tm"), P(None, "chan"), P(), P())
    return jax.shard_map(
        functools.partial(shards, mesh.shape["tm"]),
        mesh=mesh,
        in_specs=placed,
        out_specs=(P(None, "tm"), P(None, "chan"), P("chan", "tm")),
        check_vma=False,
    )
```

```python
import functools

import jax
import jax.numpy as jnp
from jax import lax
from jax.experimental import pallas as pl
from jax.experimental.pallas import tpu as pltpu
from jax.sharding import PartitionSpec as P

C = 384
K = 128
L = 96
BLOCK_ATOMS = 16
INNER = 2
OUTER = 2
CHANS = 96
SEG = 128
ENTRIES = C * L

code_rate = 0.3
move_rate = 0.5
tiny_eps = 1e-06

VMEM_LIMIT = 32 * 1024 * 1024
MESH = pl.DeviceIdType.MESH
F32 = jnp.float32
BF16 = jnp.bfloat16

OWN = 288
ROWS = 608
PLANE = 8
HALO = (
    (1, 0, 128, 160),
    (2, 0, 128, 32),
    (3, 96, 32, 0),
    (-1, 0, 128, 416),
    (-2, 0, 64, 544),
)
SIGNAL_HALO = (
    (1, 0, 128, 160),
    (2, 64, 64, 96),
    (-1, 0, 128, 416),
    (-2, 0, 64, 544),
)


def dot(a, b):
    return lax.dot_general(a, b, (((1,), (0,)), ((), ())), preferred_element_type=F32)


def dot_t(a, b):
    return lax.dot_general(a, b, (((1,), (1,)), ((), ())), preferred_element_type=F32)


def kernel(
    segments,
    plan_ref,
    dict_ref,
    small_ref,
    codes_out,
    resid_out,
    rows_first,
    rows_last,
    owner_out,
    zst,
    zsend,
    sgx,
    sgown,
    rst,
    zp,
    rp,
    wb,
    wat,
    acc,
    sx,
    sx2,
    rx1,
    rx2,
    a16,
    gfull,
    gsend,
    grecv,
    zbuf,
    agbuf,
    old,
    new,
    pick,
    dt_ref,
    block_codes,
    block_low,
    by_tap,
    in_order,
    by_atom,
    strecv,
    plane_sums,
    h_send,
    h_recv,
    s_send,
    s_recv,
    c_send,
    c_recv,
    p_send,
    p_recv,
    z_send,
    z_recv,
    a_send,
    a_recv,
    t_send,
    t_recv,
    u_send,
    u_recv,
):
    unit = ENTRIES ** (-0.5)
    tm = lax.axis_index("tm")
    chan = lax.axis_index("chan")
    depth = segments // PLANE
    place = tm % PLANE
    level = tm // PLANE

    def seg(d):
        return (tm + d + segments) % segments

    def in_plane(d):
        return level * PLANE + (place + d) % PLANE

    def in_depth(d):
        return ((level + d) % depth) * PLANE + place

    partner = chan + 1 - 2 * (chan % 2)
    opposite = (chan + 2) % 4

    zsend[0] = small_ref[0:K].T
    zst[0, OWN : OWN + SEG] = zsend[0]
    low = jnp.concatenate(
        [small_ref[K : K + CHANS], jnp.zeros((SEG - CHANS, SEG), F32)], axis=0
    ).T.astype(BF16)
    sgown[...] = low
    sgx[OWN : OWN + SEG] = low


    barrier = pltpu.get_barrier_semaphore()
    peers = [{"tm": seg(d)} for d in (-3, -2, -1, 1, 2, 3)]
    peers += [{"chan": (chan + d) % 4} for d in range(1, 4)]
    peers += [{"tm": in_plane(d)} for d in range(1, PLANE)]
    peers += [{"tm": in_depth(d)} for d in range(1, depth)]
    for peer in peers:
        pl.semaphore_signal(barrier, inc=1, device_id=peer, device_id_type=MESH)
    def pick_body(o, carry):
        tall = lax.broadcasted_iota(jnp.int32, (1024, 128), 0)
        wide = lax.broadcasted_iota(jnp.int32, (1024, 128), 1)
        block = plan_ref[o]
        hit = ((tall // 128 + block) % 8 == wide // 16) & (
            tall % 128 == wide % 16 + block * BLOCK_ATOMS
        )
        pick[o] = jnp.where(hit, 1.0, 0.0).astype(BF16)
        return carry

    lax.fori_loop(0, OUTER, pick_body, 0)

    for m in range(CHANS // 4):
        tiles = [dict_ref[:, m * 384 + t * 128 : m * 384 + t * 128 + 128].T for t in range(3)]
        turned = jnp.concatenate(tiles, axis=0)
        for r in range(4):
            row = (4 * m + r) * 97
            dt_ref[row : row + L] = turned[r * L : (r + 1) * L]

    pl.semaphore_wait(barrier, len(peers))

    def remote(src, dst, send, recv, peer):
        return pltpu.make_async_remote_copy(
            src_ref=src,
            dst_ref=dst,
            send_sem=send,
            recv_sem=recv,
            device_id=peer,
            device_id_type=MESH,
        )

    def halo_copies(o):
        return [
            remote(
                zsend.at[o, pl.ds(first, rows)],
                zst.at[o, pl.ds(land, rows)],
                h_send.at[o, i],
                h_recv.at[o, i],
                {"tm": seg(d)},
            )
            for i, (d, first, rows, land) in enumerate(HALO)
        ]

    signal_copies = [
        remote(
            sgown.at[pl.ds(first, rows)],
            sgx.at[pl.ds(land, rows)],
            s_send.at[i],
            s_recv.at[i],
            {"tm": seg(d)},
        )
        for i, (d, first, rows, land) in enumerate(SIGNAL_HALO)
    ]
    halo = halo_copies(0)
    for copy in halo + signal_copies:
        copy.start()

    for q in range(3):
        for s in range(16):
            wb[q, s * 128 + CHANS : (s + 1) * 128] = jnp.zeros((128 - CHANS, 256), BF16)
        for j in range(2):
            wat[q, j * 128 + CHANS : (j + 1) * 128] = jnp.zeros((128 - CHANS, 2048), BF16)
    lane_block = lax.broadcasted_iota(jnp.int32, (CHANS, 128), 1) // BLOCK_ATOMS

    def arrange(i, carry):
        j, q = i // 3, i % 3
        here = pl.multiple_of(j * 128, 128)
        for half in range(2):
            found = [jnp.zeros((CHANS, 128), F32)] * OUTER
            for k in range(8):
                s = half * 8 + k
                value = dt_ref[pl.ds(16 * i + s, CHANS, stride=97), :]
                low = value.astype(BF16)
                wb[q, s * 128 : s * 128 + CHANS, pl.ds(here, 128)] = low
                wat[q, pl.ds(here, CHANS), s * 128 : (s + 1) * 128] = low
                turned = pltpu.roll(value, 16 * k, 1) if k else value
                found = [
                    jnp.where(lane_block == (plan_ref[o] + k) % 8, turned, found[o])
                    for o in range(OUTER)
                ]
            group = pl.ds(pl.multiple_of(i * 256 + half * 128, 128), 128)
            for o in range(OUTER):
                old[o, :, group] = found[o]
        return carry

    lax.fori_loop(0, 6, arrange, 0)

    for copy in halo + signal_copies:
        copy.wait()

    def in_window(a, b):
        when = tm * SEG - OWN + a + lax.broadcasted_iota(jnp.int32, (b - a, 1), 0)
        return when

    def clear_early(o):
        zst[o, 0:OWN] = jnp.where(in_window(0, OWN) >= 0, zst[o, 0:OWN], 0.0)

    def convolve_rows(o, a, b):
        top = a - 80
        for s in range(16):
            zp[top:b, s * 128 : (s + 1) * 128] = zst[o, pl.ds(top - s, b - top), :].astype(BF16)
        total = dot_t(zp[a - 48 : b, :], wat[0])
        total = total + dot_t(zp[a - 64 : b - 16, :], wat[1])
        acc[0 : b - a + 48] = total + dot_t(zp[a - 80 : b - 32, :], wat[2])

    def residual_rows(a, b):
        n = b - a + 48
        made = unit * (acc[48:n, 0:128] + acc[0 : n - 48, 128:256])
        value = sgx[a:b].astype(F32) - made
        rst[a:b] = jnp.where(in_window(a, b) < segments * SEG, value, 0.0)

    def update_rows(o, step, a, b):
        n, i = b - a, o * INNER + step
        half = n // 2
        end = b + 80
        for s in range(16):
            rp[a:end, s * 128 : (s + 1) * 128] = rst[pl.ds(a + s, end - a), :].astype(BF16)
        near, far = [], []
        for part, (first, last) in enumerate(((0, half + 48), (half + 48, n + 48))):
            start, stop = a + first, a + last
            total = dot(rp[start:stop, :], wb[0])
            total = total + dot(rp[start + 16 : stop + 16, :], wb[1])
            acc[first:last] = total + dot(rp[start + 32 : stop + 32, :], wb[2])
            low, high = part * half, (part + 1) * half
            scores = unit * (acc[low:high, 0:128] + acc[low + 48 : high + 48, 128:256])
            sx[low:high] = scores.astype(BF16)
            copy = remote(
                sx.at[pl.ds(low, half)],
                rx1.at[i, pl.ds(low, half)],
                c_send.at[i, 0, part],
                c_recv.at[i, 0, part],
                {"chan": partner},
            )
            copy.start()
            near.append(copy)
        for part in range(2):
            low, high = part * half, (part + 1) * half
            near[part].wait()
            sx2[low:high] = (
                sx[low:high].astype(F32) + rx1[i, pl.ds(low, half)].astype(F32)
            ).astype(BF16)
            copy = remote(
                sx2.at[pl.ds(low, half)],
                rx2.at[i, pl.ds(low, half)],
                c_send.at[i, 1, part],
                c_recv.at[i, 1, part],
                {"chan": opposite},
            )
            copy.start()
            far.append(copy)
        limit = small_ref[K + CHANS : K + CHANS + 1]
        for part in range(2):
            low, high = part * half, (part + 1) * half
            far[part].wait()
            scores = sx2[low:high].astype(F32) + rx2[i, pl.ds(low, half)].astype(F32)
            stepped = zst[o, a + low : a + high] + code_rate * scores
            value = stepped - jnp.clip(stepped, -limit, limit)
            zst[o, a + low : a + high] = jnp.where(in_window(a + low, a + high) >= 0, value, 0.0)

    def lanes_sum(row):
        total = row[:, 0:128] + row[:, 128:256] + row[:, 256:384]
        total = jnp.broadcast_to(total, (8, 128))
        for shift in (64, 32, 16):
            total = total + pltpu.roll(total, shift, 1)
        return total

    def old_piece(o, piece):
        top, left = piece // 4 * 48, piece % 4 * 384
        return old[o, top : top + 48, left : left + 384]

    def coef_of(with_old, old_old):
        return jnp.where(old_old > 0.0, with_old / jnp.maximum(old_old, 1e-30), 0.0)

    def packed(with_old, old_old, left_over):
        row = lax.broadcasted_iota(jnp.int32, (8, 128), 0)
        return jnp.where(row == 0, with_old, jnp.where(row == 1, old_old, left_over))

    def total_of(parts, row):
        total = parts[0][row : row + 1]
        for part in parts[1:]:
            total = total + part[row : row + 1]
        return total

    def pooled(parts, coef):
        total = jnp.zeros((1, 128), F32)
        for part in parts:
            gd, dd, rr = part[0:1], part[1:2], part[2:3]
            mine = coef_of(gd, dd)
            off = mine - coef
            total = total + rr + off * (off * dd + 2.0 * (gd - mine * dd))
        return total

    def three(row):
        return jnp.concatenate([row[0:1]] * 3, axis=1)

    def renew(o):
        turned = rst[OWN : OWN + SEG].T
        resid_out[...] = turned[0:CHANS]
        for half in range(2):
            lanes = slice(half * 128, half * 128 + 128)
            a16[:, lanes] = dot(
                zp[OWN - 80 : OWN + SEG, half * 1024 : half * 1024 + 1024],
                pick[o],
            ).astype(BF16)
        across_time = turned[0:CHANS].astype(BF16)
        for q in range(6):
            gfull[:, q * 256 : (q + 1) * 256] = dot(
                across_time, a16[80 - 16 * q : 208 - 16 * q, :]
            ).astype(BF16)
        for piece in range(PLANE):
            top, left = piece // 4 * 48, piece % 4 * 384
            gsend[piece] = gfull[top : top + 48, left : left + 384]
        sent = []

        def spread_rows(part, peers, source, target, send, recv):
            rows = pl.ds(part * 16, 16)
            copies = [
                remote(
                    source(d).at[rows],
                    target(d).at[rows],
                    send.at[o, d, part],
                    recv.at[o, d, part],
                    {"tm": peer},
                )
                for d, peer in peers
            ]
            for copy in copies:
                copy.start()
            sent.extend(copies)
            return copies

        plane = [(d, in_plane(d)) for d in range(1, PLANE)]
        levels = [(d, in_depth(d)) for d in range(1, depth)]
        scatter = [
            spread_rows(
                part,
                plane,
                lambda d: gsend.at[(place + d) % PLANE],
                lambda d: grecv.at[o, d],
                p_send,
                p_recv,
            )
            for part in range(3)
        ]
        cover(o)
        across_levels = []
        for part in range(3):
            rows = pl.ds(part * 16, 16)
            total = gsend[place, rows].astype(F32)
            for d, copy in enumerate(scatter[part], 1):
                copy.wait_recv()
                total = total + grecv[o, d, rows].astype(F32)
            zbuf[o, level, rows] = total.astype(BF16)
            slot = lambda d: zbuf.at[o, level]
            across_levels.append(spread_rows(part, levels, slot, slot, z_send, z_recv))
        gather = []
        for part in range(3):
            rows = pl.ds(part * 16, 16)
            for copy in across_levels[part]:
                copy.wait_recv()
            total = zbuf[o, 0, rows].astype(F32)
            for i in range(1, depth):
                total = total + zbuf[o, i, rows].astype(F32)
            agbuf[o, place, rows] = total.astype(BF16)
            slot = lambda d: agbuf.at[o, place]
            gather.append(spread_rows(part, plane, slot, slot, a_send, a_recv))
        grad = agbuf[o, place].astype(F32)
        top = pl.multiple_of(place // 4 * 48, 16)
        left = pl.multiple_of(place % 4 * 384, 128)
        was = old[o, pl.ds(top, 48), pl.ds(left, 384)]
        with_old = lanes_sum(jnp.sum(grad * was, axis=0, keepdims=True))
        old_old = lanes_sum(jnp.sum(was * was, axis=0, keepdims=True))
        part = grad - three(coef_of(with_old, old_old)) * was
        strecv[o, chan] = packed(
            with_old, old_old, lanes_sum(jnp.sum(part * part, axis=0, keepdims=True))
        )

        def share(slot, send, recv, peers):
            copies = [
                remote(slot, slot, send.at[o, d], recv.at[o, d], peer) for d, peer in peers
            ]
            for copy in copies:
                copy.start()
            for copy in copies:
                copy.wait_recv()
            sent.extend(copies)

        share(
            strecv.at[o, chan],
            t_send,
            t_recv,
            [(d, {"chan": (chan + d) % 4}) for d in range(1, 4)],
        )
        parts = [strecv[o, i] for i in range(4)]
        with_old, old_old = total_of(parts, 0), total_of(parts, 1)
        plane_sums[o, place] = packed(
            with_old, old_old, pooled(parts, coef_of(with_old, old_old))
        )
        share(plane_sums.at[o, place], u_send, u_recv, [(d, {"tm": peer}) for d, peer in plane])
        parts = [plane_sums[o, i] for i in range(PLANE)]
        mean_sq = total_of(parts, 1)[0:1] / ENTRIES + tiny_eps
        along = total_of(parts, 0)[0:1] / ENTRIES / mean_sq
        spread = jnp.maximum(pooled(parts, along), 0.0) / ENTRIES + tiny_eps
        for copies in gather:
            for copy in copies:
                copy.wait_recv()
        along_row = three(along)
        gain = three(move_rate / jnp.sqrt(spread))
        shrink = three(1.0 / jnp.sqrt(mean_sq + 0.25))
        for piece in range(PLANE):
            was = old_piece(o, piece)
            across = agbuf[o, piece].astype(F32) - along_row * was
            top, left = piece // 4 * 48, piece % 4 * 384
            value = (was + gain * across) * shrink
            new[o, top : top + 48, left : left + 384] = value
            block_low[0, top : top + 48, left : left + 384] = value.astype(BF16)
        for copy in sent:
            copy.wait_send()

    def place_block(o):
        mine = jnp.where(lane_block == plan_ref[o], 1.0, 0.0)
        others = (1.0 - mine).astype(BF16)

        def body(i, carry):
            j, q = i // 3, i % 3
            here = pl.multiple_of(j * 128, 128)
            for half in range(2):
                value = new[o, :, pl.ds(pl.multiple_of(i * 256 + half * 128, 128), 128)]
                for k in range(8):
                    s = half * 8 + k
                    rows = slice(s * 128, s * 128 + CHANS)
                    turned = pltpu.roll(value, 128 - 16 * k, 1) if k else value
                    low = wb[q, rows, pl.ds(here, 128)] * others + (turned * mine).astype(BF16)
                    wb[q, rows, pl.ds(here, 128)] = low
                    wat[q, pl.ds(here, CHANS), s * 128 : (s + 1) * 128] = low
            return carry

        lax.fori_loop(0, 6, body, 0)

    def correct(which, sign):
        total = None
        for q in range(6):
            part = dot_t(
                block_codes[96 - 16 * q : ROWS - 16 * q, :],
                block_low[which, :, q * 256 : (q + 1) * 256],
            )
            total = part if total is None else total + part
        acc[48:560, 0:128] += sign * total

    def write_rows(o):
        rows_out = (rows_first, rows_last)[o]
        block = jnp.zeros((BLOCK_ATOMS, 128), jnp.int32) + plan_ref[o]
        bits = [block // step % 2 == 1 for step in (4, 2, 1)]
        pad = jnp.zeros((128 - CHANS, 128), F32)
        for g in range(12):
            value = new[o, :, g * 128 : (g + 1) * 128]
            by_tap[g * 128 : (g + 1) * 128] = jnp.concatenate([value, pad], axis=0).T
        for g in range(12):
            group = [by_tap[g * 128 + i * 16 : g * 128 + (i + 1) * 16] for i in range(8)]
            for step, moved in zip((4, 2, 1), bits):
                group = [jnp.where(moved, group[(i + step) % 8], group[i]) for i in range(8)]
            for i in range(8):
                in_order[g * 128 + i * 16 : g * 128 + (i + 1) * 16] = group[i]
        for atom in range(BLOCK_ATOMS):
            taps = in_order[pl.ds(atom, L, stride=BLOCK_ATOMS), :]
            turned = jnp.concatenate([taps, pad], axis=0).T
            by_atom[atom * 97 : atom * 97 + CHANS] = turned[0:CHANS]
        lane = lax.broadcasted_iota(jnp.int32, (BLOCK_ATOMS, 128), 1)

        def body(m, carry):
            one = [by_atom[pl.ds(4 * m + r, BLOCK_ATOMS, stride=97), :] for r in range(4)]
            one = [pltpu.roll(part, 96 * r % 128, 1) if r else part for r, part in enumerate(one)]
            for t in range(3):
                lanes = pl.ds(pl.multiple_of(m * 384 + t * 128, 128), 128)
                rows_out[:, lanes] = jnp.where(lane < 96 - 32 * t, one[t], one[t + 1])
            return carry

        lax.fori_loop(0, 24, body, 0)

    def cover(o):
        @pl.when(o < OUTER - 1)
        def _():
            for copy in halo_copies(1):
                copy.wait()
            clear_early(1)
            convolve_rows(1, 96, 608)
            for half in range(2):
                block_codes[16:ROWS, half * 128 : half * 128 + 128] = dot(
                    zp[16:ROWS, half * 1024 : half * 1024 + 1024], pick[0]
                ).astype(BF16)
            block_low[1, 0:CHANS] = old[0].astype(BF16)
            correct(1, -1.0)

        @pl.when(o > 0)
        def _():
            write_rows(0)

    block_low[:, CHANS:128] = jnp.zeros((2, 128 - CHANS, 1536), BF16)
    clear_early(0)
    convolve_rows(0, 96, 608)

    def outer(o, carry):
        residual_rows(96, 608)
        update_rows(o, 0, 96, 512)
        convolve_rows(o, 192, 512)
        residual_rows(192, 512)
        update_rows(o, 1, 192, 416)

        @pl.when(o < OUTER - 1)
        def _():
            zsend[1] = zst[0, OWN : OWN + SEG]
            zst[1, OWN : OWN + SEG] = zst[0, OWN : OWN + SEG]
            for copy in halo_copies(1):
                copy.start()

        convolve_rows(o, 288, 416)
        residual_rows(288, 416)
        renew(o)

        @pl.when(o < OUTER - 1)
        def _():
            correct(0, 1.0)
            place_block(0)

        return carry

    lax.fori_loop(0, OUTER, outer, 0)
    atom_block = lax.broadcasted_iota(jnp.int32, (K, 128), 0) // BLOCK_ATOMS
    owner_out[...] = jnp.where(atom_block == plan_ref[0], 1, 0) + jnp.where(
        atom_block == plan_ref[1], 2, 0
    )
    codes_out[...] = zst[OUTER - 1, OWN : OWN + SEG].T
    write_rows(OUTER - 1)


def shards(segments, signal, codes_init, dictionary_init, threshold, plan):
    limits = jnp.broadcast_to(threshold[None, :], (8, K))
    small = jnp.concatenate([codes_init, signal.astype(F32), limits], axis=0)
    depth = segments // PLANE
    vmem = pl.BlockSpec(memory_space=pltpu.VMEM)
    dma = pltpu.SemaphoreType.DMA
    codes, resid, first, last, owner = pl.pallas_call(
        functools.partial(kernel, segments),
        out_shape=(
            jax.ShapeDtypeStruct((K, SEG), F32),
            jax.ShapeDtypeStruct((CHANS, SEG), F32),
        )
        + (jax.ShapeDtypeStruct((BLOCK_ATOMS, CHANS * L), F32),) * OUTER
        + (jax.ShapeDtypeStruct((K, 128), jnp.int32),),
        in_specs=[pl.BlockSpec(memory_space=pltpu.SMEM)] + [vmem] * 2,
        out_specs=(vmem,) * 5,
        scratch_shapes=[
            pltpu.VMEM((OUTER, ROWS, 128), F32),
            pltpu.VMEM((OUTER, SEG, 128), F32),
            pltpu.VMEM((ROWS, 128), BF16),
            pltpu.VMEM((SEG, 128), BF16),
            pltpu.VMEM((ROWS, 128), F32),
            pltpu.VMEM((ROWS, 2048), BF16),
            pltpu.VMEM((ROWS, 2048), BF16),
            pltpu.VMEM((3, 2048, 256), BF16),
            pltpu.VMEM((3, 256, 2048), BF16),
            pltpu.VMEM((560, 256), F32),
            pltpu.VMEM((416, 128), BF16),
            pltpu.VMEM((416, 128), BF16),
            pltpu.VMEM((4, 416, 128), BF16),
            pltpu.VMEM((4, 416, 128), BF16),
            pltpu.VMEM((208, 256), BF16),
            pltpu.VMEM((CHANS, 1536), BF16),
            pltpu.VMEM((PLANE, 48, 384), BF16),
            pltpu.VMEM((OUTER, PLANE, 48, 384), BF16),
            pltpu.VMEM((OUTER, depth, 48, 384), BF16),
            pltpu.VMEM((OUTER, PLANE, 48, 384), BF16),
            pltpu.VMEM((OUTER, CHANS, 1536), F32),
            pltpu.VMEM((OUTER, CHANS, 1536), F32),
            pltpu.VMEM((OUTER, 1024, 128), BF16),
            pltpu.VMEM((CHANS * 97, K), F32),
            pltpu.VMEM((ROWS, 256), BF16),
            pltpu.VMEM((2, 128, 1536), BF16),
            pltpu.VMEM((1536, 128), F32),
            pltpu.VMEM((1536, 128), F32),
            pltpu.VMEM((16 * 97, 128), F32),
            pltpu.VMEM((OUTER, 4, 8, 128), F32),
            pltpu.VMEM((OUTER, PLANE, 8, 128), F32),
            dma((OUTER, 5)),
            dma((OUTER, 5)),
            dma((4,)),
            dma((4,)),
            dma((4, 2, 2)),
            dma((4, 2, 2)),
            dma((OUTER, PLANE, 3)),
            dma((OUTER, PLANE, 3)),
            dma((OUTER, depth, 3)),
            dma((OUTER, depth, 3)),
            dma((OUTER, PLANE, 3)),
            dma((OUTER, PLANE, 3)),
            dma((OUTER, 4)),
            dma((OUTER, 4)),
            dma((OUTER, PLANE)),
            dma((OUTER, PLANE)),
        ],
        compiler_params=pltpu.CompilerParams(
            collective_id=0, has_side_effects=True, vmem_limit_bytes=VMEM_LIMIT
        ),
    )(plan, dictionary_init, small)
    owner = owner[:, :1]
    first, last = (jnp.tile(rows, (K // BLOCK_ATOMS, 1)) for rows in (first, last))
    dictionary = jnp.where(owner == 1, first, jnp.where(owner == 2, last, dictionary_init))
    return codes, dictionary, resid


def solution(mesh):
    placed = (P("chan", "tm"), P(None, "tm"), P(None, "chan"), P(), P())
    return jax.shard_map(
        functools.partial(shards, mesh.shape["tm"]),
        mesh=mesh,
        in_specs=placed,
        out_specs=(P(None, "tm"), P(None, "chan"), P("chan", "tm")),
        check_vma=False,
    )
```

```python
import functools

import jax
import jax.numpy as jnp
from jax import lax
from jax.experimental import pallas as pl
from jax.experimental.pallas import tpu as pltpu
from jax.sharding import PartitionSpec as P

C = 384
K = 128
L = 96
BLOCK_ATOMS = 16
INNER = 2
OUTER = 2
CHANS = 96
SEG = 128
ENTRIES = C * L

code_rate = 0.3
move_rate = 0.5
tiny_eps = 1e-06

VMEM_LIMIT = 32 * 1024 * 1024
PARTS = 9
MESH = pl.DeviceIdType.MESH
F32 = jnp.float32
BF16 = jnp.bfloat16

OWN = 288
ROWS = 608
PLANE = 8
HALO = (
    (1, 0, 128, 160),
    (2, 0, 128, 32),
    (3, 96, 32, 0),
    (-1, 0, 128, 416),
    (-2, 0, 64, 544),
)
SIGNAL_HALO = (
    (1, 0, 128, 160),
    (2, 64, 64, 96),
    (-1, 0, 128, 416),
    (-2, 0, 64, 544),
)


def dot(a, b):
    return lax.dot_general(a, b, (((1,), (0,)), ((), ())), preferred_element_type=F32)


def dot_t(a, b):
    return lax.dot_general(a, b, (((1,), (1,)), ((), ())), preferred_element_type=F32)


def kernel(
    segments,
    plan_ref,
    dict_ref,
    small_ref,
    codes_out,
    resid_out,
    rows_first,
    rows_last,
    owner_out,
    zst,
    zsend,
    sgx,
    sgown,
    rst,
    zp,
    rp,
    wb,
    wat,
    acc,
    sx,
    sx2,
    rx1,
    rx2,
    a16,
    gfull,
    gsend,
    grecv,
    zbuf,
    agbuf,
    old,
    new,
    pick,
    dt_ref,
    block_codes,
    block_low,
    by_tap,
    in_order,
    by_atom,
    strecv,
    plane_sums,
    h_send,
    h_recv,
    s_send,
    s_recv,
    c_send,
    c_recv,
    p_send,
    p_recv,
    z_send,
    z_recv,
    a_send,
    a_recv,
    t_send,
    t_recv,
    u_send,
    u_recv,
):
    unit = ENTRIES ** (-0.5)
    tm = lax.axis_index("tm")
    chan = lax.axis_index("chan")
    depth = segments // PLANE
    place = tm % PLANE
    level = tm // PLANE

    def seg(d):
        return (tm + d + segments) % segments

    def in_plane(d):
        return level * PLANE + (place + d) % PLANE

    def in_depth(d):
        return ((level + d) % depth) * PLANE + place

    partner = chan + 1 - 2 * (chan % 2)
    opposite = (chan + 2) % 4

    zsend[0] = small_ref[0:K].T
    zst[0, OWN : OWN + SEG] = zsend[0]
    low = jnp.concatenate(
        [small_ref[K : K + CHANS], jnp.zeros((SEG - CHANS, SEG), F32)], axis=0
    ).T.astype(BF16)
    sgown[...] = low
    sgx[OWN : OWN + SEG] = low


    barrier = pltpu.get_barrier_semaphore()
    peers = [{"tm": seg(d)} for d in (-3, -2, -1, 1, 2, 3)]
    peers += [{"chan": (chan + d) % 4} for d in range(1, 4)]
    peers += [{"tm": in_plane(d)} for d in range(1, PLANE)]
    peers += [{"tm": in_depth(d)} for d in range(1, depth)]
    for peer in peers:
        pl.semaphore_signal(barrier, inc=1, device_id=peer, device_id_type=MESH)
    def pick_body(o, carry):
        tall = lax.broadcasted_iota(jnp.int32, (1024, 128), 0)
        wide = lax.broadcasted_iota(jnp.int32, (1024, 128), 1)
        block = plan_ref[o]
        hit = ((tall // 128 + block) % 8 == wide // 16) & (
            tall % 128 == wide % 16 + block * BLOCK_ATOMS
        )
        pick[o] = jnp.where(hit, 1.0, 0.0).astype(BF16)
        return carry

    lax.fori_loop(0, OUTER, pick_body, 0)

    for m in range(CHANS // 4):
        tiles = [dict_ref[:, m * 384 + t * 128 : m * 384 + t * 128 + 128].T for t in range(3)]
        turned = jnp.concatenate(tiles, axis=0)
        for r in range(4):
            row = (4 * m + r) * 97
            dt_ref[row : row + L] = turned[r * L : (r + 1) * L]

    pl.semaphore_wait(barrier, len(peers))

    def remote(src, dst, send, recv, peer):
        return pltpu.make_async_remote_copy(
            src_ref=src,
            dst_ref=dst,
            send_sem=send,
            recv_sem=recv,
            device_id=peer,
            device_id_type=MESH,
        )

    def halo_copies(o):
        return [
            remote(
                zsend.at[o, pl.ds(first, rows)],
                zst.at[o, pl.ds(land, rows)],
                h_send.at[o, i],
                h_recv.at[o, i],
                {"tm": seg(d)},
            )
            for i, (d, first, rows, land) in enumerate(HALO)
        ]

    signal_copies = [
        remote(
            sgown.at[pl.ds(first, rows)],
            sgx.at[pl.ds(land, rows)],
            s_send.at[i],
            s_recv.at[i],
            {"tm": seg(d)},
        )
        for i, (d, first, rows, land) in enumerate(SIGNAL_HALO)
    ]
    halo = halo_copies(0)
    for copy in halo + signal_copies:
        copy.start()

    for q in range(3):
        for s in range(16):
            wb[q, s * 128 + CHANS : (s + 1) * 128] = jnp.zeros((128 - CHANS, 256), BF16)
        for j in range(2):
            wat[q, j * 128 + CHANS : (j + 1) * 128] = jnp.zeros((128 - CHANS, 2048), BF16)
    lane_block = lax.broadcasted_iota(jnp.int32, (CHANS, 128), 1) // BLOCK_ATOMS

    def arrange(i, carry):
        j, q = i // 3, i % 3
        here = pl.multiple_of(j * 128, 128)
        for half in range(2):
            found = [jnp.zeros((CHANS, 128), F32)] * OUTER
            for k in range(8):
                s = half * 8 + k
                value = dt_ref[pl.ds(16 * i + s, CHANS, stride=97), :]
                low = value.astype(BF16)
                wb[q, s * 128 : s * 128 + CHANS, pl.ds(here, 128)] = low
                wat[q, pl.ds(here, CHANS), s * 128 : (s + 1) * 128] = low
                turned = pltpu.roll(value, 16 * k, 1) if k else value
                found = [
                    jnp.where(lane_block == (plan_ref[o] + k) % 8, turned, found[o])
                    for o in range(OUTER)
                ]
            group = pl.ds(pl.multiple_of(i * 256 + half * 128, 128), 128)
            for o in range(OUTER):
                old[o, :, group] = found[o]
        return carry

    lax.fori_loop(0, 6, arrange, 0)

    for copy in halo + signal_copies:
        copy.wait()

    def in_window(a, b):
        when = tm * SEG - OWN + a + lax.broadcasted_iota(jnp.int32, (b - a, 1), 0)
        return when

    def clear_early(o):
        zst[o, 0:OWN] = jnp.where(in_window(0, OWN) >= 0, zst[o, 0:OWN], 0.0)

    def convolve_rows(o, a, b):
        top = a - 80
        for s in range(16):
            zp[top:b, s * 128 : (s + 1) * 128] = zst[o, pl.ds(top - s, b - top), :].astype(BF16)
        total = dot_t(zp[a - 48 : b, :], wat[0])
        total = total + dot_t(zp[a - 64 : b - 16, :], wat[1])
        acc[0 : b - a + 48] = total + dot_t(zp[a - 80 : b - 32, :], wat[2])

    def residual_rows(a, b):
        n = b - a + 48
        made = unit * (acc[48:n, 0:128] + acc[0 : n - 48, 128:256])
        value = sgx[a:b].astype(F32) - made
        rst[a:b] = jnp.where(in_window(a, b) < segments * SEG, value, 0.0)

    def update_rows(o, step, a, b):
        n, i = b - a, o * INNER + step
        half = n // 2
        end = b + 80
        for s in range(16):
            rp[a:end, s * 128 : (s + 1) * 128] = rst[pl.ds(a + s, end - a), :].astype(BF16)
        near, far = [], []
        for part, (first, last) in enumerate(((0, half + 48), (half + 48, n + 48))):
            start, stop = a + first, a + last
            total = dot(rp[start:stop, :], wb[0])
            total = total + dot(rp[start + 16 : stop + 16, :], wb[1])
            acc[first:last] = total + dot(rp[start + 32 : stop + 32, :], wb[2])
            low, high = part * half, (part + 1) * half
            scores = unit * (acc[low:high, 0:128] + acc[low + 48 : high + 48, 128:256])
            sx[low:high] = scores.astype(BF16)
            copy = remote(
                sx.at[pl.ds(low, half)],
                rx1.at[i, pl.ds(low, half)],
                c_send.at[i, 0, part],
                c_recv.at[i, 0, part],
                {"chan": partner},
            )
            copy.start()
            near.append(copy)
        for part in range(2):
            low, high = part * half, (part + 1) * half
            near[part].wait()
            sx2[low:high] = (
                sx[low:high].astype(F32) + rx1[i, pl.ds(low, half)].astype(F32)
            ).astype(BF16)
            copy = remote(
                sx2.at[pl.ds(low, half)],
                rx2.at[i, pl.ds(low, half)],
                c_send.at[i, 1, part],
                c_recv.at[i, 1, part],
                {"chan": opposite},
            )
            copy.start()
            far.append(copy)
        limit = small_ref[K + CHANS : K + CHANS + 1]
        for part in range(2):
            low, high = part * half, (part + 1) * half
            far[part].wait()
            scores = sx2[low:high].astype(F32) + rx2[i, pl.ds(low, half)].astype(F32)
            stepped = zst[o, a + low : a + high] + code_rate * scores
            value = stepped - jnp.clip(stepped, -limit, limit)
            zst[o, a + low : a + high] = jnp.where(in_window(a + low, a + high) >= 0, value, 0.0)

    def lanes_sum(row):
        total = row[:, 0:128] + row[:, 128:256] + row[:, 256:384]
        total = jnp.broadcast_to(total, (8, 128))
        for shift in (64, 32, 16):
            total = total + pltpu.roll(total, shift, 1)
        return total

    def old_piece(o, piece):
        top, left = piece // 4 * 48, piece % 4 * 384
        return old[o, top : top + 48, left : left + 384]

    def coef_of(with_old, old_old):
        return jnp.where(old_old > 0.0, with_old / jnp.maximum(old_old, 1e-30), 0.0)

    def packed(with_old, old_old, left_over):
        row = lax.broadcasted_iota(jnp.int32, (8, 128), 0)
        return jnp.where(row == 0, with_old, jnp.where(row == 1, old_old, left_over))

    def total_of(parts, row):
        total = parts[0][row : row + 1]
        for part in parts[1:]:
            total = total + part[row : row + 1]
        return total

    def pooled(parts, coef):
        total = jnp.zeros((1, 128), F32)
        for part in parts:
            gd, dd, rr = part[0:1], part[1:2], part[2:3]
            mine = coef_of(gd, dd)
            off = mine - coef
            total = total + rr + off * (off * dd + 2.0 * (gd - mine * dd))
        return total

    def three(row):
        return jnp.concatenate([row[0:1]] * 3, axis=1)

    def renew(o):
        turned = rst[OWN : OWN + SEG].T
        resid_out[...] = turned[0:CHANS]
        for half in range(2):
            lanes = slice(half * 128, half * 128 + 128)
            a16[:, lanes] = dot(
                zp[OWN - 80 : OWN + SEG, half * 1024 : half * 1024 + 1024],
                pick[o],
            ).astype(BF16)
        across_time = turned[0:CHANS].astype(BF16)
        for q in range(6):
            gfull[:, q * 256 : (q + 1) * 256] = dot(
                across_time, a16[80 - 16 * q : 208 - 16 * q, :]
            ).astype(BF16)
        for piece in range(PLANE):
            top, left = piece // 4 * 48, piece % 4 * 384
            gsend[piece] = gfull[top : top + 48, left : left + 384]
        sent = []

        def part_of(part):
            return pl.ds(part % 3 * 16, 16), pl.ds(part // 3 * 128, 128)

        def spread_rows(part, peers, source, target, send, recv):
            rows, lanes = part_of(part)
            copies = [
                remote(
                    source(d).at[rows, lanes],
                    target(d).at[rows, lanes],
                    send.at[o, d, part],
                    recv.at[o, d, part],
                    {"tm": peer},
                )
                for d, peer in peers
            ]
            for copy in copies:
                copy.start()
            sent.extend(copies)
            return copies

        plane = [(d, in_plane(d)) for d in range(1, PLANE)]
        levels = [(d, in_depth(d)) for d in range(1, depth)]
        scatter = [
            spread_rows(
                part,
                plane,
                lambda d: gsend.at[(place + d) % PLANE],
                lambda d: grecv.at[o, d],
                p_send,
                p_recv,
            )
            for part in range(PARTS)
        ]
        cover(o)
        across_levels = []
        for part in range(PARTS):
            rows, lanes = part_of(part)
            total = gsend[place, rows, lanes].astype(F32)
            for d, copy in enumerate(scatter[part], 1):
                copy.wait_recv()
                total = total + grecv[o, d, rows, lanes].astype(F32)
            zbuf[o, level, rows, lanes] = total.astype(BF16)
            slot = lambda d: zbuf.at[o, level]
            across_levels.append(spread_rows(part, levels, slot, slot, z_send, z_recv))
        gather = []
        for part in range(PARTS):
            rows, lanes = part_of(part)
            for copy in across_levels[part]:
                copy.wait_recv()
            total = zbuf[o, 0, rows, lanes].astype(F32)
            for i in range(1, depth):
                total = total + zbuf[o, i, rows, lanes].astype(F32)
            agbuf[o, place, rows, lanes] = total.astype(BF16)
            slot = lambda d: agbuf.at[o, place]
            gather.append(spread_rows(part, plane, slot, slot, a_send, a_recv))
        grad = agbuf[o, place].astype(F32)
        top = pl.multiple_of(place // 4 * 48, 16)
        left = pl.multiple_of(place % 4 * 384, 128)
        was = old[o, pl.ds(top, 48), pl.ds(left, 384)]
        with_old = lanes_sum(jnp.sum(grad * was, axis=0, keepdims=True))
        old_old = lanes_sum(jnp.sum(was * was, axis=0, keepdims=True))
        part = grad - three(coef_of(with_old, old_old)) * was
        strecv[o, chan] = packed(
            with_old, old_old, lanes_sum(jnp.sum(part * part, axis=0, keepdims=True))
        )

        def share(slot, send, recv, peers):
            copies = [
                remote(slot, slot, send.at[o, d], recv.at[o, d], peer) for d, peer in peers
            ]
            for copy in copies:
                copy.start()
            for copy in copies:
                copy.wait_recv()
            sent.extend(copies)

        share(
            strecv.at[o, chan],
            t_send,
            t_recv,
            [(d, {"chan": (chan + d) % 4}) for d in range(1, 4)],
        )
        parts = [strecv[o, i] for i in range(4)]
        with_old, old_old = total_of(parts, 0), total_of(parts, 1)
        plane_sums[o, place] = packed(
            with_old, old_old, pooled(parts, coef_of(with_old, old_old))
        )
        share(plane_sums.at[o, place], u_send, u_recv, [(d, {"tm": peer}) for d, peer in plane])
        parts = [plane_sums[o, i] for i in range(PLANE)]
        mean_sq = total_of(parts, 1)[0:1] / ENTRIES + tiny_eps
        along = total_of(parts, 0)[0:1] / ENTRIES / mean_sq
        spread = jnp.maximum(pooled(parts, along), 0.0) / ENTRIES + tiny_eps
        for copies in gather:
            for copy in copies:
                copy.wait_recv()
        along_row = three(along)
        gain = three(move_rate / jnp.sqrt(spread))
        shrink = three(1.0 / jnp.sqrt(mean_sq + 0.25))
        for piece in range(PLANE):
            was = old_piece(o, piece)
            across = agbuf[o, piece].astype(F32) - along_row * was
            top, left = piece // 4 * 48, piece % 4 * 384
            value = (was + gain * across) * shrink
            new[o, top : top + 48, left : left + 384] = value
            block_low[0, top : top + 48, left : left + 384] = value.astype(BF16)
        for copy in sent:
            copy.wait_send()

    def place_block(o):
        mine = jnp.where(lane_block == plan_ref[o], 1.0, 0.0)
        others = (1.0 - mine).astype(BF16)

        def body(i, carry):
            j, q = i // 3, i % 3
            here = pl.multiple_of(j * 128, 128)
            for half in range(2):
                value = new[o, :, pl.ds(pl.multiple_of(i * 256 + half * 128, 128), 128)]
                for k in range(8):
                    s = half * 8 + k
                    rows = slice(s * 128, s * 128 + CHANS)
                    turned = pltpu.roll(value, 128 - 16 * k, 1) if k else value
                    low = wb[q, rows, pl.ds(here, 128)] * others + (turned * mine).astype(BF16)
                    wb[q, rows, pl.ds(here, 128)] = low
                    wat[q, pl.ds(here, CHANS), s * 128 : (s + 1) * 128] = low
            return carry

        lax.fori_loop(0, 6, body, 0)

    def correct(which, sign):
        total = None
        for q in range(6):
            part = dot_t(
                block_codes[96 - 16 * q : ROWS - 16 * q, :],
                block_low[which, :, q * 256 : (q + 1) * 256],
            )
            total = part if total is None else total + part
        acc[48:560, 0:128] += sign * total

    def write_rows(o):
        rows_out = (rows_first, rows_last)[o]
        block = jnp.zeros((BLOCK_ATOMS, 128), jnp.int32) + plan_ref[o]
        bits = [block // step % 2 == 1 for step in (4, 2, 1)]
        pad = jnp.zeros((128 - CHANS, 128), F32)
        for g in range(12):
            value = new[o, :, g * 128 : (g + 1) * 128]
            by_tap[g * 128 : (g + 1) * 128] = jnp.concatenate([value, pad], axis=0).T
        for g in range(12):
            group = [by_tap[g * 128 + i * 16 : g * 128 + (i + 1) * 16] for i in range(8)]
            for step, moved in zip((4, 2, 1), bits):
                group = [jnp.where(moved, group[(i + step) % 8], group[i]) for i in range(8)]
            for i in range(8):
                in_order[g * 128 + i * 16 : g * 128 + (i + 1) * 16] = group[i]
        for atom in range(BLOCK_ATOMS):
            taps = in_order[pl.ds(atom, L, stride=BLOCK_ATOMS), :]
            turned = jnp.concatenate([taps, pad], axis=0).T
            by_atom[atom * 97 : atom * 97 + CHANS] = turned[0:CHANS]
        lane = lax.broadcasted_iota(jnp.int32, (BLOCK_ATOMS, 128), 1)

        def body(m, carry):
            one = [by_atom[pl.ds(4 * m + r, BLOCK_ATOMS, stride=97), :] for r in range(4)]
            one = [pltpu.roll(part, 96 * r % 128, 1) if r else part for r, part in enumerate(one)]
            for t in range(3):
                lanes = pl.ds(pl.multiple_of(m * 384 + t * 128, 128), 128)
                rows_out[:, lanes] = jnp.where(lane < 96 - 32 * t, one[t], one[t + 1])
            return carry

        lax.fori_loop(0, 24, body, 0)

    def cover(o):
        @pl.when(o < OUTER - 1)
        def _():
            for copy in halo_copies(1):
                copy.wait()
            clear_early(1)
            convolve_rows(1, 96, 608)
            for half in range(2):
                block_codes[16:ROWS, half * 128 : half * 128 + 128] = dot(
                    zp[16:ROWS, half * 1024 : half * 1024 + 1024], pick[0]
                ).astype(BF16)
            block_low[1, 0:CHANS] = old[0].astype(BF16)
            correct(1, -1.0)

        @pl.when(o > 0)
        def _():
            write_rows(0)

    block_low[:, CHANS:128] = jnp.zeros((2, 128 - CHANS, 1536), BF16)
    clear_early(0)
    convolve_rows(0, 96, 608)

    def outer(o, carry):
        residual_rows(96, 608)
        update_rows(o, 0, 96, 512)
        convolve_rows(o, 192, 512)
        residual_rows(192, 512)
        update_rows(o, 1, 192, 416)

        @pl.when(o < OUTER - 1)
        def _():
            zsend[1] = zst[0, OWN : OWN + SEG]
            zst[1, OWN : OWN + SEG] = zst[0, OWN : OWN + SEG]
            for copy in halo_copies(1):
                copy.start()

        convolve_rows(o, 288, 416)
        residual_rows(288, 416)
        renew(o)

        @pl.when(o < OUTER - 1)
        def _():
            correct(0, 1.0)
            place_block(0)

        return carry

    lax.fori_loop(0, OUTER, outer, 0)
    atom_block = lax.broadcasted_iota(jnp.int32, (K, 128), 0) // BLOCK_ATOMS
    owner_out[...] = jnp.where(atom_block == plan_ref[0], 1, 0) + jnp.where(
        atom_block == plan_ref[1], 2, 0
    )
    codes_out[...] = zst[OUTER - 1, OWN : OWN + SEG].T
    write_rows(OUTER - 1)


def shards(segments, signal, codes_init, dictionary_init, threshold, plan):
    limits = jnp.broadcast_to(threshold[None, :], (8, K))
    small = jnp.concatenate([codes_init, signal.astype(F32), limits], axis=0)
    depth = segments // PLANE
    vmem = pl.BlockSpec(memory_space=pltpu.VMEM)
    dma = pltpu.SemaphoreType.DMA
    codes, resid, first, last, owner = pl.pallas_call(
        functools.partial(kernel, segments),
        out_shape=(
            jax.ShapeDtypeStruct((K, SEG), F32),
            jax.ShapeDtypeStruct((CHANS, SEG), F32),
        )
        + (jax.ShapeDtypeStruct((BLOCK_ATOMS, CHANS * L), F32),) * OUTER
        + (jax.ShapeDtypeStruct((K, 128), jnp.int32),),
        in_specs=[pl.BlockSpec(memory_space=pltpu.SMEM)] + [vmem] * 2,
        out_specs=(vmem,) * 5,
        scratch_shapes=[
            pltpu.VMEM((OUTER, ROWS, 128), F32),
            pltpu.VMEM((OUTER, SEG, 128), F32),
            pltpu.VMEM((ROWS, 128), BF16),
            pltpu.VMEM((SEG, 128), BF16),
            pltpu.VMEM((ROWS, 128), F32),
            pltpu.VMEM((ROWS, 2048), BF16),
            pltpu.VMEM((ROWS, 2048), BF16),
            pltpu.VMEM((3, 2048, 256), BF16),
            pltpu.VMEM((3, 256, 2048), BF16),
            pltpu.VMEM((560, 256), F32),
            pltpu.VMEM((416, 128), BF16),
            pltpu.VMEM((416, 128), BF16),
            pltpu.VMEM((4, 416, 128), BF16),
            pltpu.VMEM((4, 416, 128), BF16),
            pltpu.VMEM((208, 256), BF16),
            pltpu.VMEM((CHANS, 1536), BF16),
            pltpu.VMEM((PLANE, 48, 384), BF16),
            pltpu.VMEM((OUTER, PLANE, 48, 384), BF16),
            pltpu.VMEM((OUTER, depth, 48, 384), BF16),
            pltpu.VMEM((OUTER, PLANE, 48, 384), BF16),
            pltpu.VMEM((OUTER, CHANS, 1536), F32),
            pltpu.VMEM((OUTER, CHANS, 1536), F32),
            pltpu.VMEM((OUTER, 1024, 128), BF16),
            pltpu.VMEM((CHANS * 97, K), F32),
            pltpu.VMEM((ROWS, 256), BF16),
            pltpu.VMEM((2, 128, 1536), BF16),
            pltpu.VMEM((1536, 128), F32),
            pltpu.VMEM((1536, 128), F32),
            pltpu.VMEM((16 * 97, 128), F32),
            pltpu.VMEM((OUTER, 4, 8, 128), F32),
            pltpu.VMEM((OUTER, PLANE, 8, 128), F32),
            dma((OUTER, 5)),
            dma((OUTER, 5)),
            dma((4,)),
            dma((4,)),
            dma((4, 2, 2)),
            dma((4, 2, 2)),
            dma((OUTER, PLANE, PARTS)),
            dma((OUTER, PLANE, PARTS)),
            dma((OUTER, depth, PARTS)),
            dma((OUTER, depth, PARTS)),
            dma((OUTER, PLANE, PARTS)),
            dma((OUTER, PLANE, PARTS)),
            dma((OUTER, 4)),
            dma((OUTER, 4)),
            dma((OUTER, PLANE)),
            dma((OUTER, PLANE)),
        ],
        compiler_params=pltpu.CompilerParams(
            collective_id=0, has_side_effects=True, vmem_limit_bytes=VMEM_LIMIT
        ),
    )(plan, dictionary_init, small)
    owner = owner[:, :1]
    first, last = (jnp.tile(rows, (K // BLOCK_ATOMS, 1)) for rows in (first, last))
    dictionary = jnp.where(owner == 1, first, jnp.where(owner == 2, last, dictionary_init))
    return codes, dictionary, resid


def solution(mesh):
    placed = (P("chan", "tm"), P(None, "tm"), P(None, "chan"), P(), P())
    return jax.shard_map(
        functools.partial(shards, mesh.shape["tm"]),
        mesh=mesh,
        in_specs=placed,
        out_specs=(P(None, "tm"), P(None, "chan"), P("chan", "tm")),
        check_vma=False,
    )
```

```python
import functools

import jax
import jax.numpy as jnp
from jax import lax
from jax.experimental import pallas as pl
from jax.experimental.pallas import tpu as pltpu
from jax.sharding import PartitionSpec as P

C = 384
K = 128
L = 96
BLOCK_ATOMS = 16
INNER = 2
OUTER = 2
CHANS = 96
SEG = 128
ENTRIES = C * L

code_rate = 0.3
move_rate = 0.5
tiny_eps = 1e-06

VMEM_LIMIT = 32 * 1024 * 1024
PARTS = 3
MESH = pl.DeviceIdType.MESH
F32 = jnp.float32
BF16 = jnp.bfloat16

OWN = 288
ROWS = 608
PLANE = 8
HALO = (
    (1, 0, 128, 160),
    (2, 0, 128, 32),
    (3, 96, 32, 0),
    (-1, 0, 128, 416),
    (-2, 0, 64, 544),
)
SIGNAL_HALO = (
    (1, 0, 128, 160),
    (2, 64, 64, 96),
    (-1, 0, 128, 416),
    (-2, 0, 64, 544),
)


def dot(a, b):
    return lax.dot_general(a, b, (((1,), (0,)), ((), ())), preferred_element_type=F32)


def dot_t(a, b):
    return lax.dot_general(a, b, (((1,), (1,)), ((), ())), preferred_element_type=F32)


def kernel(
    segments,
    plan_ref,
    dict_ref,
    small_ref,
    codes_out,
    resid_out,
    rows_first,
    rows_last,
    owner_out,
    zst,
    zsend,
    sgx,
    sgown,
    rst,
    zp,
    rp,
    wb,
    wat,
    acc,
    sx,
    sx2,
    rx1,
    rx2,
    a16,
    gfull,
    gsend,
    grecv,
    zbuf,
    agbuf,
    old,
    new,
    pick,
    dt_ref,
    block_codes,
    block_low,
    by_tap,
    in_order,
    by_atom,
    strecv,
    plane_sums,
    h_send,
    h_recv,
    s_send,
    s_recv,
    c_send,
    c_recv,
    p_send,
    p_recv,
    z_send,
    z_recv,
    a_send,
    a_recv,
    t_send,
    t_recv,
    u_send,
    u_recv,
):
    unit = ENTRIES ** (-0.5)
    tm = lax.axis_index("tm")
    chan = lax.axis_index("chan")
    depth = segments // PLANE
    place = tm % PLANE
    level = tm // PLANE

    def seg(d):
        return (tm + d + segments) % segments

    def in_plane(d):
        return level * PLANE + (place + d) % PLANE

    def in_depth(d):
        return ((level + d) % depth) * PLANE + place

    partner = chan + 1 - 2 * (chan % 2)
    opposite = (chan + 2) % 4

    zsend[0] = small_ref[0:K].T
    zst[0, OWN : OWN + SEG] = zsend[0]
    low = jnp.concatenate(
        [small_ref[K : K + CHANS], jnp.zeros((SEG - CHANS, SEG), F32)], axis=0
    ).T.astype(BF16)
    sgown[...] = low
    sgx[OWN : OWN + SEG] = low


    barrier = pltpu.get_barrier_semaphore()
    peers = [{"tm": seg(d)} for d in (-3, -2, -1, 1, 2, 3)]
    peers += [{"chan": (chan + d) % 4} for d in range(1, 4)]
    peers += [{"tm": in_plane(d)} for d in range(1, PLANE)]
    peers += [{"tm": in_depth(d)} for d in range(1, depth)]
    for peer in peers:
        pl.semaphore_signal(barrier, inc=1, device_id=peer, device_id_type=MESH)
    def pick_body(o, carry):
        tall = lax.broadcasted_iota(jnp.int32, (1024, 128), 0)
        wide = lax.broadcasted_iota(jnp.int32, (1024, 128), 1)
        block = plan_ref[o]
        hit = ((tall // 128 + block) % 8 == wide // 16) & (
            tall % 128 == wide % 16 + block * BLOCK_ATOMS
        )
        pick[o] = jnp.where(hit, 1.0, 0.0).astype(BF16)
        return carry

    lax.fori_loop(0, OUTER, pick_body, 0)

    for m in range(CHANS // 4):
        tiles = [dict_ref[:, m * 384 + t * 128 : m * 384 + t * 128 + 128].T for t in range(3)]
        turned = jnp.concatenate(tiles, axis=0)
        for r in range(4):
            row = (4 * m + r) * 97
            dt_ref[row : row + L] = turned[r * L : (r + 1) * L]

    pl.semaphore_wait(barrier, len(peers))

    def remote(src, dst, send, recv, peer):
        return pltpu.make_async_remote_copy(
            src_ref=src,
            dst_ref=dst,
            send_sem=send,
            recv_sem=recv,
            device_id=peer,
            device_id_type=MESH,
        )

    def halo_copies(o):
        return [
            remote(
                zsend.at[o, pl.ds(first, rows)],
                zst.at[o, pl.ds(land, rows)],
                h_send.at[o, i],
                h_recv.at[o, i],
                {"tm": seg(d)},
            )
            for i, (d, first, rows, land) in enumerate(HALO)
        ]

    signal_copies = [
        remote(
            sgown.at[pl.ds(first, rows)],
            sgx.at[pl.ds(land, rows)],
            s_send.at[i],
            s_recv.at[i],
            {"tm": seg(d)},
        )
        for i, (d, first, rows, land) in enumerate(SIGNAL_HALO)
    ]
    halo = halo_copies(0)
    for copy in halo + signal_copies:
        copy.start()

    for q in range(3):
        for s in range(16):
            wb[q, s * 128 + CHANS : (s + 1) * 128] = jnp.zeros((128 - CHANS, 256), BF16)
        for j in range(2):
            wat[q, j * 128 + CHANS : (j + 1) * 128] = jnp.zeros((128 - CHANS, 2048), BF16)
    lane_block = lax.broadcasted_iota(jnp.int32, (CHANS, 128), 1) // BLOCK_ATOMS

    def arrange(i, carry):
        j, q = i // 3, i % 3
        here = pl.multiple_of(j * 128, 128)
        for half in range(2):
            found = [jnp.zeros((CHANS, 128), F32)] * OUTER
            for k in range(8):
                s = half * 8 + k
                value = dt_ref[pl.ds(16 * i + s, CHANS, stride=97), :]
                low = value.astype(BF16)
                wb[q, s * 128 : s * 128 + CHANS, pl.ds(here, 128)] = low
                wat[q, pl.ds(here, CHANS), s * 128 : (s + 1) * 128] = low
                turned = pltpu.roll(value, 16 * k, 1) if k else value
                found = [
                    jnp.where(lane_block == (plan_ref[o] + k) % 8, turned, found[o])
                    for o in range(OUTER)
                ]
            group = pl.ds(pl.multiple_of(i * 256 + half * 128, 128), 128)
            for o in range(OUTER):
                old[o, :, group] = found[o]
        return carry

    lax.fori_loop(0, 6, arrange, 0)

    for copy in halo + signal_copies:
        copy.wait()

    def in_window(a, b):
        when = tm * SEG - OWN + a + lax.broadcasted_iota(jnp.int32, (b - a, 1), 0)
        return when

    def clear_early(o):
        zst[o, 0:OWN] = jnp.where(in_window(0, OWN) >= 0, zst[o, 0:OWN], 0.0)

    def convolve_rows(o, a, b):
        top = a - 80
        for s in range(16):
            zp[top:b, s * 128 : (s + 1) * 128] = zst[o, pl.ds(top - s, b - top), :].astype(BF16)
        total = dot_t(zp[a - 48 : b, :], wat[0])
        total = total + dot_t(zp[a - 64 : b - 16, :], wat[1])
        acc[0 : b - a + 48] = total + dot_t(zp[a - 80 : b - 32, :], wat[2])

    def residual_rows(a, b):
        n = b - a + 48
        made = unit * (acc[48:n, 0:128] + acc[0 : n - 48, 128:256])
        value = sgx[a:b].astype(F32) - made
        rst[a:b] = jnp.where(in_window(a, b) < segments * SEG, value, 0.0)

    def update_rows(o, step, a, b):
        n, i = b - a, o * INNER + step
        half = n // 2
        end = b + 80
        for s in range(16):
            rp[a:end, s * 128 : (s + 1) * 128] = rst[pl.ds(a + s, end - a), :].astype(BF16)
        near, far = [], []
        for part, (first, last) in enumerate(((0, half + 48), (half + 48, n + 48))):
            start, stop = a + first, a + last
            total = dot(rp[start:stop, :], wb[0])
            total = total + dot(rp[start + 16 : stop + 16, :], wb[1])
            acc[first:last] = total + dot(rp[start + 32 : stop + 32, :], wb[2])
            low, high = part * half, (part + 1) * half
            scores = unit * (acc[low:high, 0:128] + acc[low + 48 : high + 48, 128:256])
            sx[low:high] = scores.astype(BF16)
            copy = remote(
                sx.at[pl.ds(low, half)],
                rx1.at[i, pl.ds(low, half)],
                c_send.at[i, 0, part],
                c_recv.at[i, 0, part],
                {"chan": partner},
            )
            copy.start()
            near.append(copy)
        for part in range(2):
            low, high = part * half, (part + 1) * half
            near[part].wait()
            sx2[low:high] = (
                sx[low:high].astype(F32) + rx1[i, pl.ds(low, half)].astype(F32)
            ).astype(BF16)
            copy = remote(
                sx2.at[pl.ds(low, half)],
                rx2.at[i, pl.ds(low, half)],
                c_send.at[i, 1, part],
                c_recv.at[i, 1, part],
                {"chan": opposite},
            )
            copy.start()
            far.append(copy)
        limit = small_ref[K + CHANS : K + CHANS + 1]
        for part in range(2):
            low, high = part * half, (part + 1) * half
            far[part].wait()
            scores = sx2[low:high].astype(F32) + rx2[i, pl.ds(low, half)].astype(F32)
            stepped = zst[o, a + low : a + high] + code_rate * scores
            value = stepped - jnp.clip(stepped, -limit, limit)
            zst[o, a + low : a + high] = jnp.where(in_window(a + low, a + high) >= 0, value, 0.0)

    def lanes_sum(row):
        total = row[:, 0:128] + row[:, 128:256] + row[:, 256:384]
        total = jnp.broadcast_to(total, (8, 128))
        for shift in (64, 32, 16):
            total = total + pltpu.roll(total, shift, 1)
        return total

    def old_piece(o, piece):
        top, left = piece // 4 * 48, piece % 4 * 384
        return old[o, top : top + 48, left : left + 384]

    def coef_of(with_old, old_old):
        return jnp.where(old_old > 0.0, with_old / jnp.maximum(old_old, 1e-30), 0.0)

    def packed(with_old, old_old, left_over):
        row = lax.broadcasted_iota(jnp.int32, (8, 128), 0)
        return jnp.where(row == 0, with_old, jnp.where(row == 1, old_old, left_over))

    def total_of(parts, row):
        total = parts[0][row : row + 1]
        for part in parts[1:]:
            total = total + part[row : row + 1]
        return total

    def pooled(parts, coef):
        total = jnp.zeros((1, 128), F32)
        for part in parts:
            gd, dd, rr = part[0:1], part[1:2], part[2:3]
            mine = coef_of(gd, dd)
            off = mine - coef
            total = total + rr + off * (off * dd + 2.0 * (gd - mine * dd))
        return total

    def three(row):
        return jnp.concatenate([row[0:1]] * 3, axis=1)

    def renew(o):
        turned = rst[OWN : OWN + SEG].T
        resid_out[...] = turned[0:CHANS]
        for half in range(2):
            lanes = slice(half * 128, half * 128 + 128)
            a16[:, lanes] = dot(
                zp[OWN - 80 : OWN + SEG, half * 1024 : half * 1024 + 1024],
                pick[o],
            ).astype(BF16)
        across_time = turned[0:CHANS].astype(BF16)
        for q in range(6):
            gfull[:, q * 256 : (q + 1) * 256] = dot(
                across_time, a16[80 - 16 * q : 208 - 16 * q, :]
            ).astype(BF16)
        for piece in range(PLANE):
            top, left = piece // 4 * 48, piece % 4 * 384
            gsend[piece] = gfull[top : top + 48, left : left + 384]
        sent = []

        def part_of(part):
            return pl.ds(part * 16, 16), pl.ds(0, 384)

        def spread_rows(part, peers, source, target, send, recv):
            rows, lanes = part_of(part)
            copies = [
                remote(
                    source(d).at[rows, lanes],
                    target(d).at[rows, lanes],
                    send.at[o, d, part],
                    recv.at[o, d, part],
                    {"tm": peer},
                )
                for d, peer in peers
            ]
            for copy in copies:
                copy.start()
            sent.extend(copies)
            return copies

        plane = [(d, in_plane(d)) for d in range(1, PLANE)]
        levels = [(d, in_depth(d)) for d in range(1, depth)]
        scatter = [
            spread_rows(
                part,
                plane,
                lambda d: gsend.at[(place + d) % PLANE],
                lambda d: grecv.at[o, d],
                p_send,
                p_recv,
            )
            for part in range(PARTS)
        ]
        cover(o)
        across_levels = []
        for part in range(PARTS):
            rows, lanes = part_of(part)
            total = gsend[place, rows, lanes].astype(F32)
            for d, copy in enumerate(scatter[part], 1):
                copy.wait_recv()
                total = total + grecv[o, d, rows, lanes].astype(F32)
            zbuf[o, level, rows, lanes] = total.astype(BF16)
            slot = lambda d: zbuf.at[o, level]
            across_levels.append(spread_rows(part, levels, slot, slot, z_send, z_recv))

        def share(slot, send, recv, peers):
            copies = [
                remote(slot, slot, send.at[o, d], recv.at[o, d], peer) for d, peer in peers
            ]
            for copy in copies:
                copy.start()
            sent.extend(copies)
            return copies

        def sums_over_chan():
            grad = agbuf[o, place].astype(F32)
            top = pl.multiple_of(place // 4 * 48, 16)
            left = pl.multiple_of(place % 4 * 384, 128)
            was = old[o, pl.ds(top, 48), pl.ds(left, 384)]
            with_old = lanes_sum(jnp.sum(grad * was, axis=0, keepdims=True))
            old_old = lanes_sum(jnp.sum(was * was, axis=0, keepdims=True))
            rest = grad - three(coef_of(with_old, old_old)) * was
            strecv[o, chan] = packed(
                with_old, old_old, lanes_sum(jnp.sum(rest * rest, axis=0, keepdims=True))
            )
            return share(
                strecv.at[o, chan],
                t_send,
                t_recv,
                [(d, {"chan": (chan + d) % 4}) for d in range(1, 4)],
            )

        gather = []
        for part in range(PARTS):
            rows, lanes = part_of(part)
            for copy in across_levels[part]:
                copy.wait_recv()
            total = zbuf[o, 0, rows, lanes].astype(F32)
            for i in range(1, depth):
                total = total + zbuf[o, i, rows, lanes].astype(F32)
            agbuf[o, place, rows, lanes] = total.astype(BF16)
            if part == PARTS - 1:
                over_chan = sums_over_chan()
            slot = lambda d: agbuf.at[o, place]
            gather.append(spread_rows(part, plane, slot, slot, a_send, a_recv))
        for copy in over_chan:
            copy.wait_recv()
        parts = [strecv[o, i] for i in range(4)]
        with_old, old_old = total_of(parts, 0), total_of(parts, 1)
        plane_sums[o, place] = packed(
            with_old, old_old, pooled(parts, coef_of(with_old, old_old))
        )
        over_plane = share(
            plane_sums.at[o, place], u_send, u_recv, [(d, {"tm": peer}) for d, peer in plane]
        )
        for copy in over_plane:
            copy.wait_recv()
        parts = [plane_sums[o, i] for i in range(PLANE)]
        mean_sq = total_of(parts, 1)[0:1] / ENTRIES + tiny_eps
        along = total_of(parts, 0)[0:1] / ENTRIES / mean_sq
        spread = jnp.maximum(pooled(parts, along), 0.0) / ENTRIES + tiny_eps
        for copies in gather:
            for copy in copies:
                copy.wait_recv()
        along_row = three(along)
        gain = three(move_rate / jnp.sqrt(spread))
        shrink = three(1.0 / jnp.sqrt(mean_sq + 0.25))
        for piece in range(PLANE):
            was = old_piece(o, piece)
            across = agbuf[o, piece].astype(F32) - along_row * was
            top, left = piece // 4 * 48, piece % 4 * 384
            value = (was + gain * across) * shrink
            new[o, top : top + 48, left : left + 384] = value
            block_low[0, top : top + 48, left : left + 384] = value.astype(BF16)
        for copy in sent:
            copy.wait_send()

    def place_block(o):
        mine = jnp.where(lane_block == plan_ref[o], 1.0, 0.0)
        others = (1.0 - mine).astype(BF16)

        def body(i, carry):
            j, q = i // 3, i % 3
            here = pl.multiple_of(j * 128, 128)
            for half in range(2):
                value = new[o, :, pl.ds(pl.multiple_of(i * 256 + half * 128, 128), 128)]
                for k in range(8):
                    s = half * 8 + k
                    rows = slice(s * 128, s * 128 + CHANS)
                    turned = pltpu.roll(value, 128 - 16 * k, 1) if k else value
                    low = wb[q, rows, pl.ds(here, 128)] * others + (turned * mine).astype(BF16)
                    wb[q, rows, pl.ds(here, 128)] = low
                    wat[q, pl.ds(here, CHANS), s * 128 : (s + 1) * 128] = low
            return carry

        lax.fori_loop(0, 6, body, 0)

    def correct(which, sign):
        total = None
        for q in range(6):
            part = dot_t(
                block_codes[96 - 16 * q : ROWS - 16 * q, :],
                block_low[which, :, q * 256 : (q + 1) * 256],
            )
            total = part if total is None else total + part
        acc[48:560, 0:128] += sign * total

    def write_rows(o):
        rows_out = (rows_first, rows_last)[o]
        block = jnp.zeros((BLOCK_ATOMS, 128), jnp.int32) + plan_ref[o]
        bits = [block // step % 2 == 1 for step in (4, 2, 1)]
        pad = jnp.zeros((128 - CHANS, 128), F32)
        for g in range(12):
            value = new[o, :, g * 128 : (g + 1) * 128]
            by_tap[g * 128 : (g + 1) * 128] = jnp.concatenate([value, pad], axis=0).T
        for g in range(12):
            group = [by_tap[g * 128 + i * 16 : g * 128 + (i + 1) * 16] for i in range(8)]
            for step, moved in zip((4, 2, 1), bits):
                group = [jnp.where(moved, group[(i + step) % 8], group[i]) for i in range(8)]
            for i in range(8):
                in_order[g * 128 + i * 16 : g * 128 + (i + 1) * 16] = group[i]
        for atom in range(BLOCK_ATOMS):
            taps = in_order[pl.ds(atom, L, stride=BLOCK_ATOMS), :]
            turned = jnp.concatenate([taps, pad], axis=0).T
            by_atom[atom * 97 : atom * 97 + CHANS] = turned[0:CHANS]
        lane = lax.broadcasted_iota(jnp.int32, (BLOCK_ATOMS, 128), 1)

        def body(m, carry):
            one = [by_atom[pl.ds(4 * m + r, BLOCK_ATOMS, stride=97), :] for r in range(4)]
            one = [pltpu.roll(part, 96 * r % 128, 1) if r else part for r, part in enumerate(one)]
            for t in range(3):
                lanes = pl.ds(pl.multiple_of(m * 384 + t * 128, 128), 128)
                rows_out[:, lanes] = jnp.where(lane < 96 - 32 * t, one[t], one[t + 1])
            return carry

        lax.fori_loop(0, 24, body, 0)

    def cover(o):
        @pl.when(o < OUTER - 1)
        def _():
            for copy in halo_copies(1):
                copy.wait()
            clear_early(1)
            convolve_rows(1, 96, 608)
            for half in range(2):
                block_codes[16:ROWS, half * 128 : half * 128 + 128] = dot(
                    zp[16:ROWS, half * 1024 : half * 1024 + 1024], pick[0]
                ).astype(BF16)
            block_low[1, 0:CHANS] = old[0].astype(BF16)
            correct(1, -1.0)

        @pl.when(o > 0)
        def _():
            write_rows(0)

    block_low[:, CHANS:128] = jnp.zeros((2, 128 - CHANS, 1536), BF16)
    clear_early(0)
    convolve_rows(0, 96, 608)

    def outer(o, carry):
        residual_rows(96, 608)
        update_rows(o, 0, 96, 512)
        convolve_rows(o, 192, 512)
        residual_rows(192, 512)
        update_rows(o, 1, 192, 416)

        @pl.when(o < OUTER - 1)
        def _():
            zsend[1] = zst[0, OWN : OWN + SEG]
            zst[1, OWN : OWN + SEG] = zst[0, OWN : OWN + SEG]
            for copy in halo_copies(1):
                copy.start()

        convolve_rows(o, 288, 416)
        residual_rows(288, 416)
        renew(o)

        @pl.when(o < OUTER - 1)
        def _():
            correct(0, 1.0)
            place_block(0)

        return carry

    lax.fori_loop(0, OUTER, outer, 0)
    atom_block = lax.broadcasted_iota(jnp.int32, (K, 128), 0) // BLOCK_ATOMS
    owner_out[...] = jnp.where(atom_block == plan_ref[0], 1, 0) + jnp.where(
        atom_block == plan_ref[1], 2, 0
    )
    codes_out[...] = zst[OUTER - 1, OWN : OWN + SEG].T
    write_rows(OUTER - 1)


def shards(segments, signal, codes_init, dictionary_init, threshold, plan):
    limits = jnp.broadcast_to(threshold[None, :], (8, K))
    small = jnp.concatenate([codes_init, signal.astype(F32), limits], axis=0)
    depth = segments // PLANE
    vmem = pl.BlockSpec(memory_space=pltpu.VMEM)
    dma = pltpu.SemaphoreType.DMA
    codes, resid, first, last, owner = pl.pallas_call(
        functools.partial(kernel, segments),
        out_shape=(
            jax.ShapeDtypeStruct((K, SEG), F32),
            jax.ShapeDtypeStruct((CHANS, SEG), F32),
        )
        + (jax.ShapeDtypeStruct((BLOCK_ATOMS, CHANS * L), F32),) * OUTER
        + (jax.ShapeDtypeStruct((K, 128), jnp.int32),),
        in_specs=[pl.BlockSpec(memory_space=pltpu.SMEM)] + [vmem] * 2,
        out_specs=(vmem,) * 5,
        scratch_shapes=[
            pltpu.VMEM((OUTER, ROWS, 128), F32),
            pltpu.VMEM((OUTER, SEG, 128), F32),
            pltpu.VMEM((ROWS, 128), BF16),
            pltpu.VMEM((SEG, 128), BF16),
            pltpu.VMEM((ROWS, 128), F32),
            pltpu.VMEM((ROWS, 2048), BF16),
            pltpu.VMEM((ROWS, 2048), BF16),
            pltpu.VMEM((3, 2048, 256), BF16),
            pltpu.VMEM((3, 256, 2048), BF16),
            pltpu.VMEM((560, 256), F32),
            pltpu.VMEM((416, 128), BF16),
            pltpu.VMEM((416, 128), BF16),
            pltpu.VMEM((4, 416, 128), BF16),
            pltpu.VMEM((4, 416, 128), BF16),
            pltpu.VMEM((208, 256), BF16),
            pltpu.VMEM((CHANS, 1536), BF16),
            pltpu.VMEM((PLANE, 48, 384), BF16),
            pltpu.VMEM((OUTER, PLANE, 48, 384), BF16),
            pltpu.VMEM((OUTER, depth, 48, 384), BF16),
            pltpu.VMEM((OUTER, PLANE, 48, 384), BF16),
            pltpu.VMEM((OUTER, CHANS, 1536), F32),
            pltpu.VMEM((OUTER, CHANS, 1536), F32),
            pltpu.VMEM((OUTER, 1024, 128), BF16),
            pltpu.VMEM((CHANS * 97, K), F32),
            pltpu.VMEM((ROWS, 256), BF16),
            pltpu.VMEM((2, 128, 1536), BF16),
            pltpu.VMEM((1536, 128), F32),
            pltpu.VMEM((1536, 128), F32),
            pltpu.VMEM((16 * 97, 128), F32),
            pltpu.VMEM((OUTER, 4, 8, 128), F32),
            pltpu.VMEM((OUTER, PLANE, 8, 128), F32),
            dma((OUTER, 5)),
            dma((OUTER, 5)),
            dma((4,)),
            dma((4,)),
            dma((4, 2, 2)),
            dma((4, 2, 2)),
            dma((OUTER, PLANE, PARTS)),
            dma((OUTER, PLANE, PARTS)),
            dma((OUTER, depth, PARTS)),
            dma((OUTER, depth, PARTS)),
            dma((OUTER, PLANE, PARTS)),
            dma((OUTER, PLANE, PARTS)),
            dma((OUTER, 4)),
            dma((OUTER, 4)),
            dma((OUTER, PLANE)),
            dma((OUTER, PLANE)),
        ],
        compiler_params=pltpu.CompilerParams(
            collective_id=0, has_side_effects=True, vmem_limit_bytes=VMEM_LIMIT
        ),
    )(plan, dictionary_init, small)
    owner = owner[:, :1]
    first, last = (jnp.tile(rows, (K // BLOCK_ATOMS, 1)) for rows in (first, last))
    dictionary = jnp.where(owner == 1, first, jnp.where(owner == 2, last, dictionary_init))
    return codes, dictionary, resid


def solution(mesh):
    placed = (P("chan", "tm"), P(None, "tm"), P(None, "chan"), P(), P())
    return jax.shard_map(
        functools.partial(shards, mesh.shape["tm"]),
        mesh=mesh,
        in_specs=placed,
        out_specs=(P(None, "tm"), P(None, "chan"), P("chan", "tm")),
        check_vma=False,
    )
```
